32 devices in a mesh: dp: 8 (over z, y), tensor: 4 (over x, core).
Axes of the slice: x: 2, y: 2, z: 4, core: 2. Of those that a mesh axis runs over, the one named last changes fastest.
Arguments:
- query_tokens: float32 [2048, 768], P('dp'), may hold values from -6 to 6
- passage_tokens: float32 [6144, 768], P('dp'), may hold values from -6 to 6
- query_mask: int32 [64, 32], P('dp'), may hold values from 0 to 1, as said below
- passage_lengths: int32 [24], replicated, may hold values from 64 to 256, as said below
- positives: int32 [64], replicated, may hold values from 0 to 23
- qkv_weight: float32 [2, 3, 768, 768], P(None, None, 'dp', 'tensor'), may hold values from -0.21875 to 0.21875
- qkv_moment: float32 [2, 3, 768, 768], P(None, None, 'dp', 'tensor'), may hold values from -0.18 to 0.18
- qkv_second: float32 [2, 3, 768, 768], P(None, None, 'dp', 'tensor'), may hold values from 5e-05 to 0.0005
- out_weight: float32 [2, 768, 768], P(None, 'tensor', 'dp'), may hold values from -0.875 to 0.875
- out_moment: float32 [2, 768, 768], P(None, 'tensor', 'dp'), may hold values from -0.09 to 0.09
- out_second: float32 [2, 768, 768], P(None, 'tensor', 'dp'), may hold values from 7e-06 to 7e-05
- up_weight: float32 [2, 768, 3072], P(None, 'dp', 'tensor'), may hold values from -0.21875 to 0.21875
- up_moment: float32 [2, 768, 3072], P(None, 'dp', 'tensor'), may hold values from -0.12 to 0.12
- up_second: float32 [2, 768, 3072], P(None, 'dp', 'tensor'), may hold values from 1.5e-05 to 0.00015
- down_weight: float32 [2, 3072, 768], P(None, 'tensor', 'dp'), may hold values from -0.15625 to 0.15625
- down_moment: float32 [2, 3072, 768], P(None, 'tensor', 'dp'), may hold values from -0.15 to 0.15
- down_second: float32 [2, 3072, 768], P(None, 'tensor', 'dp'), may hold values from 3e-05 to 0.0003
- projection: float32 [768, 128], P('dp'), may hold values from -0.21875 to 0.21875
- projection_moment: float32 [768, 128], P('dp'), may hold values from -0.6 to 0.6
- projection_second: float32 [768, 128], P('dp'), may hold values from 0.0004 to 0.004
- bias_pair: float32 [2, 2, 768], P(None, None, 'tensor'), may hold values from -3 to 3
- bias_pair_moment: float32 [2, 2, 768], P(None, None, 'tensor'), may hold values from -0.36 to 0.36
- bias_pair_second: float32 [2, 2, 768], P(None, None, 'tensor'), may hold values from 0.0002 to 0.002
- bias_up: float32 [2, 3072], P(None, 'tensor'), may hold values from -3 to 3
- bias_up_moment: float32 [2, 3072], P(None, 'tensor'), may hold values from -0.072 to 0.072
- bias_up_second: float32 [2, 3072], P(None, 'tensor'), may hold values from 5e-06 to 5e-05
- norm_terms: float32 [2, 6, 768], replicated, may hold values from -2 to 2, as said below
- norm_terms_moment: float32 [2, 6, 768], replicated, may hold values from -0.18 to 0.18
- norm_terms_second: float32 [2, 6, 768], replicated, may hold values from 5e-05 to 0.0005
Outputs:
- loss_mean: float32 [], replicated
- query_grad: float32 [2048, 768], P(('dp', 'tensor'))
- passage_grad: float32 [6144, 768], P(('dp', 'tensor'))
- qkv_grad: float32 [2, 3, 768, 768], P(None, None, 'dp', 'tensor')
- qkv_moment_new: float32 [2, 3, 768, 768], P(None, None, 'dp', 'tensor')
- qkv_second_new: float32 [2, 3, 768, 768], P(None, None, 'dp', 'tensor')
- qkv_update: float32 [2, 3, 768, 768], P(None, None, 'dp', 'tensor')
- out_grad: float32 [2, 768, 768], P(None, 'tensor', 'dp')
- out_moment_new: float32 [2, 768, 768], P(None, 'tensor', 'dp')
- out_second_new: float32 [2, 768, 768], P(None, 'tensor', 'dp')
- out_update: float32 [2, 768, 768], P(None, 'tensor', 'dp')
- up_grad: float32 [2, 768, 3072], P(None, 'dp', 'tensor')
- up_moment_new: float32 [2, 768, 3072], P(None, 'dp', 'tensor')
- up_second_new: float32 [2, 768, 3072], P(None, 'dp', 'tensor')
- up_update: float32 [2, 768, 3072], P(None, 'dp', 'tensor')
- down_grad: float32 [2, 3072, 768], P(None, 'tensor', 'dp')
- down_moment_new: float32 [2, 3072, 768], P(None, 'tensor', 'dp')
- down_second_new: float32 [2, 3072, 768], P(None, 'tensor', 'dp')
- down_update: float32 [2, 3072, 768], P(None, 'tensor', 'dp')
- projection_grad: float32 [768, 128], P('dp')
- projection_moment_new: float32 [768, 128], P('dp')
- projection_second_new: float32 [768, 128], P('dp')
- projection_update: float32 [768, 128], P('dp')
- bias_pair_grad: float32 [2, 2, 768], P(None, None, 'tensor')
- bias_pair_moment_new: float32 [2, 2, 768], P(None, None, 'tensor')
- bias_pair_second_new: float32 [2, 2, 768], P(None, None, 'tensor')
- bias_pair_update: float32 [2, 2, 768], P(None, None, 'tensor')
- bias_up_grad: float32 [2, 3072], P(None, 'tensor')
- bias_up_moment_new: float32 [2, 3072], P(None, 'tensor')
- bias_up_second_new: float32 [2, 3072], P(None, 'tensor')
- bias_up_update: float32 [2, 3072], P(None, 'tensor')
- norm_terms_grad: float32 [2, 6, 768], replicated
- norm_terms_moment_new: float32 [2, 6, 768], replicated
- norm_terms_second_new: float32 [2, 6, 768], replicated
- norm_terms_update: float32 [2, 6, 768], replicated
The draws below stay inside these ranges and needn't reach their ends.
Inputs may be any that keep to these rules, and one draw needn't show every extreme that they name: `query_mask`: each row holds ones at its first 4 to 32 positions and zeros after them; some row is all ones. `passage_lengths`: some passage has all 256 tokens. `norm_terms`: rows 1 and 4 of each layer are gains between 0.4 and 1.6; the other rows lie between -2 and 2.
All inputs are finite; a program needn't handle non-finite values.
Results may differ from the reference program's by a relative error of at most 0.034.
Values may be sent and summed in bfloat16 or wider, within the bound.
No kernel may reach another device: no remote copies, remote signals or barrier semaphores. Data moves between devices by JAX's collectives and lax.ppermute only.
A program may use at most 192 MiB of HBM per device.

```python
import math
import jax
import jax.numpy as jnp
from jax import lax

D = 768
HEAD = 64
FF = 3072
DIM = 128
QLEN = 32
PLEN = 256
LAYERS = 2
STEP = 10
QDEV = 8
QUERIES = 64
PASSAGES = 24


def draw_query_mask(key, part):
    counts = jax.random.randint(jax.random.fold_in(key, 11), (QUERIES,), 4, QLEN + 1)
    longest = jax.random.randint(jax.random.fold_in(key, 12), (), 0, QUERIES)
    counts = jnp.where(jnp.arange(QUERIES) == longest, QLEN, counts)
    return (jnp.arange(QLEN)[None, :] < counts[:, None]).astype(jnp.int32)


def draw_passage_lengths(key, part):
    counts = jax.random.randint(jax.random.fold_in(key, 21), (PASSAGES,), PLEN // 4, PLEN + 1)
    longest = jax.random.randint(jax.random.fold_in(key, 22), (), 0, PASSAGES)
    return jnp.where(jnp.arange(PASSAGES) == longest, PLEN, counts).astype(jnp.int32)


def draw_norm_terms(key, part):
    base = jnp.clip(jax.random.normal(key, (LAYERS, 6, D), jnp.float32), -4.0, 4.0)
    row_index = lax.broadcasted_iota(jnp.int32, (LAYERS, 6, D), 1)
    gain_rows = (row_index == 1) | (row_index == 4)
    return jnp.where(gain_rows, 1.0 + 0.15 * base, 0.5 * base).astype(jnp.float32)


def set_ends(drawn, key, least, top_value):
    longest = drawn.shape.index(max(drawn.shape))
    spots = []
    for shift in (0, 1):
        where = [jax.random.randint(jax.random.fold_in(key, axis), (), 0, length) for axis, length in enumerate(drawn.shape)]
        where[longest] = (where[longest] + shift) % drawn.shape[longest]
        spots.append(tuple(where))
    return drawn.at[spots[0]].set(least).at[spots[1]].set(top_value)


def block_scale(rng, shape, pieces, low, high):
    gain, own = 1.0, jax.random.fold_in(rng, 6)
    for position, shards_of in pieces:
        heights = jnp.exp(jax.random.uniform(jax.random.fold_in(own, position), (shards_of,), jnp.float32, low / len(pieces), high / len(pieces)))
        gain = gain * jnp.repeat(heights, shape[position] // shards_of).reshape([-1 if axis == position else 1 for axis in range(len(shape))])
    return gain


def bell_draw(key, extent, deviation, bound, cuts=(), kind=jnp.bfloat16):
    drawn = jax.random.normal(key, extent, jnp.float32) * deviation
    if len(cuts) > 0:
        drawn = block_scale(key, extent, cuts, -0.22, 0.18) * drawn
    return jnp.clip(drawn, min=-bound, max=bound).astype(kind)


def setup_inputs(seed: int = 0) -> dict:
    key_list = jax.random.split(jax.random.key(seed), 30)
    query_tokens = bell_draw(key_list[0], (QUERIES * QLEN, D), 1.0, 6.0, ((0, 8),), jnp.float32)
    passage_tokens = bell_draw(key_list[1], (PASSAGES * PLEN, D), 1.0, 6.0, ((0, 8),), jnp.float32)
    query_mask = draw_query_mask(jax.random.fold_in(key_list[29], 71), 0)
    passage_lengths = draw_passage_lengths(jax.random.fold_in(key_list[29], 71), 0)
    positives = set_ends(jax.random.randint(key_list[4], (QUERIES,), 0, PASSAGES), jax.random.fold_in(key_list[4], 1), 0, PASSAGES - 1).astype(jnp.int32)
    qkv_weight = bell_draw(key_list[5], (LAYERS, 3, D, D), D ** -0.5, 0.21875, ((2, 8), (3, 4)), jnp.float32)
    qkv_moment = bell_draw(key_list[6], (LAYERS, 3, D, D), 0.03, 0.18, ((2, 8), (3, 4)), jnp.float32)
    qkv_second = jnp.clip(jnp.exp(math.log(0.0005) - 2.3025852 * jax.random.uniform(key_list[7], (LAYERS, 3, D, D), jnp.float32) ** block_scale(key_list[7], (LAYERS, 3, D, D), ((2, 8), (3, 4)), -0.2, 0.2)), 4.999999873689376e-05, 0.0005)
    out_weight = bell_draw(key_list[8], (LAYERS, D, D), (D // 16) ** -0.5, 0.875, ((1, 4), (2, 8)), jnp.float32)
    out_moment = bell_draw(key_list[9], (LAYERS, D, D), 0.015, 0.09, ((1, 4), (2, 8)), jnp.float32)
    out_second = jnp.clip(jnp.exp(math.log(7.000000186963007e-05) - 2.3025851 * jax.random.uniform(key_list[10], (LAYERS, D, D), jnp.float32) ** block_scale(key_list[10], (LAYERS, D, D), ((1, 4), (2, 8)), -0.2, 0.2)), 7.000000096013537e-06, 7.000000186963007e-05)
    up_weight = bell_draw(key_list[11], (LAYERS, D, FF), D ** -0.5, 0.21875, ((1, 8), (2, 4)), jnp.float32)
    up_moment = bell_draw(key_list[12], (LAYERS, D, FF), 0.02, 0.12, ((1, 8), (2, 4)), jnp.float32)
    up_second = jnp.clip(jnp.exp(math.log(0.00015) - 2.3025852 * jax.random.uniform(key_list[13], (LAYERS, D, FF), jnp.float32) ** block_scale(key_list[13], (LAYERS, D, FF), ((1, 8), (2, 4)), -0.2, 0.2)), 1.4999999621068127e-05, 0.00015)
    down_weight = bell_draw(key_list[14], (LAYERS, FF, D), (FF // 2) ** -0.5, 0.15625, ((1, 4), (2, 8)), jnp.float32)
    down_moment = bell_draw(key_list[15], (LAYERS, FF, D), 0.025, 0.15, ((1, 4), (2, 8)), jnp.float32)
    down_second = jnp.clip(jnp.exp(math.log(0.0003) - 2.3025852 * jax.random.uniform(key_list[16], (LAYERS, FF, D), jnp.float32) ** block_scale(key_list[16], (LAYERS, FF, D), ((1, 4), (2, 8)), -0.2, 0.2)), 2.9999999242136255e-05, 0.0003)
    projection = bell_draw(key_list[17], (D, DIM), D ** -0.5, 0.21875, ((0, 8),), jnp.float32)
    projection_moment = bell_draw(key_list[18], (D, DIM), 0.1, 0.6, ((0, 8),), jnp.float32)
    projection_second = jnp.clip(jnp.exp(math.log(0.004) - 2.3025852 * jax.random.uniform(key_list[19], (D, DIM), jnp.float32) ** block_scale(key_list[19], (D, DIM), ((0, 8),), -0.2, 0.2)), 0.0004, 0.004)
    bias_pair = bell_draw(key_list[20], (LAYERS, 2, D), 0.5, 3.0, ((2, 4),), jnp.float32)
    bias_pair_moment = bell_draw(key_list[21], (LAYERS, 2, D), 0.06, 0.36, ((2, 4),), jnp.float32)
    bias_pair_second = jnp.clip(jnp.exp(math.log(0.002) - 2.3025852 * jax.random.uniform(key_list[22], (LAYERS, 2, D), jnp.float32) ** block_scale(key_list[22], (LAYERS, 2, D), ((2, 4),), -0.2, 0.2)), 0.0002, 0.002)
    bias_up = bell_draw(key_list[23], (LAYERS, FF), 0.5, 3.0, ((1, 4),), jnp.float32)
    bias_up_moment = bell_draw(key_list[24], (LAYERS, FF), 0.012, 0.072, ((1, 4),), jnp.float32)
    bias_up_second = jnp.clip(jnp.exp(math.log(4.999999873689376e-05) - 2.3025851 * jax.random.uniform(key_list[25], (LAYERS, FF), jnp.float32) ** block_scale(key_list[25], (LAYERS, FF), ((1, 4),), -0.2, 0.2)), 4.999999873689376e-06, 4.999999873689376e-05)
    norm_terms = draw_norm_terms(jax.random.fold_in(key_list[29], 71), 0)
    norm_terms_moment = bell_draw(key_list[27], (LAYERS, 6, D), 0.03, 0.18, (), jnp.float32)
    norm_terms_second = jnp.clip(jnp.exp(jax.random.uniform(key_list[28], (LAYERS, 6, D), jnp.float32, math.log(4.999999873689376e-05), math.log(0.0005))), 4.999999873689376e-05, 0.0005)
    return {"query_tokens": query_tokens, "passage_tokens": passage_tokens, "query_mask": query_mask, "passage_lengths": passage_lengths, "positives": positives, "qkv_weight": qkv_weight, "qkv_moment": qkv_moment, "qkv_second": qkv_second, "out_weight": out_weight, "out_moment": out_moment, "out_second": out_second, "up_weight": up_weight, "up_moment": up_moment, "up_second": up_second, "down_weight": down_weight, "down_moment": down_moment, "down_second": down_second, "projection": projection, "projection_moment": projection_moment, "projection_second": projection_second, "bias_pair": bias_pair, "bias_pair_moment": bias_pair_moment, "bias_pair_second": bias_pair_second, "bias_up": bias_up, "bias_up_moment": bias_up_moment, "bias_up_second": bias_up_second, "norm_terms": norm_terms, "norm_terms_moment": norm_terms_moment, "norm_terms_second": norm_terms_second}


@jax.custom_vjp
def low(v):
    return lax.optimization_barrier(v.astype(jnp.bfloat16)).astype(jnp.float32)

@jax.custom_vjp
def low_back(v):
    return v

def low_keep(v):
    return (low(v), None)

def low_pass(kept, grad):
    return (grad,)

def back_keep(v):
    return (v, None)

def back_low(kept, grad):
    return (low(grad),)
low.defvjp(low_keep, low_pass)
low_back.defvjp(back_keep, back_low)
MASKED = -1e+30
SHARPNESS = 24.0
SCORE_SCALE = 4.0
LN_EPS = 1e-12
NORM_EPS = 1e-12
BETA_ONE = 0.9
BETA_TWO = 0.999
ADAM_EPS = 1e-08
LEARN_RATE = 0.02
WEIGHT_DECAY = 0.01
HIGHEST = lax.Precision.HIGHEST

def rounded_both(values):
    return low_back(low(values))

def matmul(left, right):
    return jnp.dot(left, right, precision=HIGHEST, preferred_element_type=jnp.float32)

def layer_norm(values, gains, shifts):
    average = lax.optimization_barrier(jnp.mean(values, -1, keepdims=True))
    centred = values - average
    factor = lax.rsqrt(lax.optimization_barrier(jnp.mean(centred * centred, -1, keepdims=True)) + LN_EPS)
    return centred * factor * gains + shifts

def encoder_layer(hidden, key_valid, qkv_low, out_low, up_low, down_low, bias_pair, bias_up, norm_terms):
    seq_count, length, width = hidden.shape
    row_data = hidden.reshape(seq_count * length, width)
    inputs = low(row_data)
    queries = rounded_both(matmul(inputs, qkv_low[0]) + bias_pair[0]).reshape(seq_count, length, -1, HEAD)
    keys_all = rounded_both(matmul(inputs, qkv_low[1])).reshape(seq_count, length, -1, HEAD)
    values = rounded_both(matmul(inputs, qkv_low[2]) + bias_pair[1]).reshape(seq_count, length, -1, HEAD)
    scores = low_back(jnp.einsum('sqhd,skhd->shqk', queries, keys_all, precision=HIGHEST) * 0.125)
    scores = jnp.where(key_valid[:, None, None, :], scores, MASKED)
    highest = lax.optimization_barrier(jnp.max(scores, -1, keepdims=True))
    powers = jnp.exp(scores - highest)
    chances = low(powers / lax.optimization_barrier(jnp.sum(powers, -1, keepdims=True)))
    mixture = jnp.einsum('shqk,skhd->sqhd', chances, values, precision=HIGHEST)
    mixture = rounded_both(mixture.reshape(seq_count * length, width))
    attended = low_back(matmul(mixture, out_low))
    first = layer_norm(row_data + attended + norm_terms[0], norm_terms[1], norm_terms[2])
    pre_act = low_back(matmul(low(first), up_low) + bias_up)
    spread = low_back(matmul(low(jax.nn.gelu(pre_act, approximate=False)), down_low))
    second = layer_norm(first + spread + norm_terms[3], norm_terms[4], norm_terms[5])
    return second.reshape(seq_count, length, width)

def embed(hidden, proj_low):
    seq_count, length, width = hidden.shape
    projected = low_back(matmul(low(hidden.reshape(seq_count * length, width)), proj_low))
    normed = projected * lax.rsqrt(lax.optimization_barrier(jnp.sum(projected * projected, -1, keepdims=True)) + NORM_EPS)
    return low(normed).reshape(seq_count, length, DIM)

def late_scores(query_block, passages, passage_valid, log_counts):
    similar = low_back(jnp.einsum('qid,pjd->qipj', query_block, passages, precision=HIGHEST))
    sharp = jnp.where(passage_valid[None, None], SHARPNESS * similar, MASKED)
    highest = lax.optimization_barrier(jnp.max(sharp, -1, keepdims=True))
    summed = lax.optimization_barrier(jnp.sum(jnp.exp(sharp - highest), -1))
    smooth = (highest[..., 0] + jnp.log(summed) - log_counts[None, None, :]) / SHARPNESS
    return SCORE_SCALE * lax.optimization_barrier(jnp.sum(smooth, 1))

def objective(qkv_weight, out_weight, up_weight, down_weight, projection, bias_pair, bias_up, norm_terms, query_tokens, passage_tokens, query_valid, passage_valid, log_counts, positives):
    qkv_low = low(qkv_weight)
    out_low = low(out_weight)
    up_low = low(up_weight)
    down_low = low(down_weight)
    queries = query_tokens.reshape(QUERIES, QLEN, D)
    passages = passage_tokens.reshape(PASSAGES, PLEN, D)
    for layer_at in range(LAYERS):
        queries = encoder_layer(queries, query_valid, qkv_low[layer_at], out_low[layer_at], up_low[layer_at], down_low[layer_at], bias_pair[layer_at], bias_up[layer_at], norm_terms[layer_at])
        passages = encoder_layer(passages, passage_valid, qkv_low[layer_at], out_low[layer_at], up_low[layer_at], down_low[layer_at], bias_pair[layer_at], bias_up[layer_at], norm_terms[layer_at])
    proj_low = low(projection)
    query_emb = embed(queries, proj_low)
    passage_emb = embed(passages, proj_low)
    blocks = query_emb.reshape(QUERIES // QDEV, QDEV, QLEN, DIM)
    scorer = jax.checkpoint(lambda block_in: late_scores(block_in, passage_emb, passage_valid, log_counts))
    logits = lax.map(scorer, blocks).reshape(QUERIES, PASSAGES)
    highest = lax.optimization_barrier(jnp.max(logits, -1, keepdims=True))
    log_total = highest[:, 0] + jnp.log(lax.optimization_barrier(jnp.sum(jnp.exp(logits - highest), -1)))
    chosen = jnp.arange(PASSAGES, dtype=jnp.int32)[None, :] == positives[:, None]
    picked = lax.optimization_barrier(jnp.sum(jnp.where(chosen, logits, 0.0), -1))
    return jnp.sum(log_total - picked)

def adam_step(master, moment, second, gradient, decay):
    moment_new = BETA_ONE * moment + (1.0 - BETA_ONE) * gradient
    second_new = BETA_TWO * second + (1.0 - BETA_TWO) * gradient * gradient
    rising = moment_new / (1.0 - BETA_ONE ** STEP)
    spread = jnp.sqrt(second_new / (1.0 - BETA_TWO ** STEP))
    return (moment_new, second_new, -LEARN_RATE * (rising / (spread + ADAM_EPS) + decay * master))

def reference(query_tokens, passage_tokens, query_mask, passage_lengths, positives, qkv_weight, qkv_moment, qkv_second, out_weight, out_moment, out_second, up_weight, up_moment, up_second, down_weight, down_moment, down_second, projection, projection_moment, projection_second, bias_pair, bias_pair_moment, bias_pair_second, bias_up, bias_up_moment, bias_up_second, norm_terms, norm_terms_moment, norm_terms_second):
    query_valid = query_mask == 1
    passage_valid = jnp.arange(PLEN, dtype=jnp.int32)[None, :] < passage_lengths[:, None]
    log_counts = jnp.log(passage_lengths.astype(jnp.float32))

    def closed(qkv_in, out_in, up_in, down_in, proj_in, pair_in, bias_in, norms_in, query_in, passage_in):
        return objective(qkv_in, out_in, up_in, down_in, proj_in, pair_in, bias_in, norms_in, query_in, passage_in, query_valid, passage_valid, log_counts, positives)
    total, pullback = jax.vjp(closed, qkv_weight, out_weight, up_weight, down_weight, projection, bias_pair, bias_up, norm_terms, query_tokens, passage_tokens)
    grads = pullback(jnp.ones_like(total))
    loss_mean = total / QUERIES
    qkv_m, qkv_v, qkv_u = adam_step(qkv_weight, qkv_moment, qkv_second, grads[0], WEIGHT_DECAY)
    out_m, out_v, out_u = adam_step(out_weight, out_moment, out_second, grads[1], WEIGHT_DECAY)
    up_m, up_v, up_u = adam_step(up_weight, up_moment, up_second, grads[2], WEIGHT_DECAY)
    down_m, down_v, down_u = adam_step(down_weight, down_moment, down_second, grads[3], WEIGHT_DECAY)
    proj_m, proj_v, proj_u = adam_step(projection, projection_moment, projection_second, grads[4], WEIGHT_DECAY)
    pair_m, pair_v, pair_u = adam_step(bias_pair, bias_pair_moment, bias_pair_second, grads[5], 0.0)
    bias_m, bias_v, bias_u = adam_step(bias_up, bias_up_moment, bias_up_second, grads[6], 0.0)
    norm_m, norm_v, norm_u = adam_step(norm_terms, norm_terms_moment, norm_terms_second, grads[7], 0.0)
    return (loss_mean, grads[8], grads[9], grads[0], qkv_m, qkv_v, qkv_u, grads[1], out_m, out_v, out_u, grads[2], up_m, up_v, up_u, grads[3], down_m, down_v, down_u, grads[4], proj_m, proj_v, proj_u, grads[5], pair_m, pair_v, pair_u, grads[6], bias_m, bias_v, bias_u, grads[7], norm_m, norm_v, norm_u)
```

```python
import functools

import jax
import jax.numpy as jnp
from jax import lax
from jax.experimental import pallas as pl
from jax.experimental.pallas import tpu as pltpu
from jax.sharding import PartitionSpec as P

WIDTH = 768
HEAD = 64
DIM = 128
QLEN = 32
PLEN = 256
LAYERS = 2
STEP = 10
QDEV = 8
PDEV = 3
ROWS = 256
PARTS = 4
HEADS_EACH = 3
OWN = HEADS_EACH * HEAD
SLAB = 768
HELD = 640
PACK = 3 * SLAB

MASKED = -1e30
SHARPNESS = 24.0
SCORE_SCALE = 4.0
LN_EPS = 1e-12
NORM_EPS = 1e-12
BETA_ONE = 0.9
BETA_TWO = 0.999
ADAM_EPS = 1e-08
LEARN_RATE = 0.02
WEIGHT_DECAY = 0.01
VMEM_BYTES = 60 * 1024 * 1024

BF = jnp.bfloat16
F32 = jnp.float32
BOTH = ("dp", "tensor")


def nn(left, right):
    return jnp.dot(left, right, preferred_element_type=F32)


def nt(left, right):
    return lax.dot_general(left, right, (((1,), (1,)), ((), ())), preferred_element_type=F32)


def norm_forward(values):
    average = jnp.mean(values, -1, keepdims=True)
    centred = values - average
    factor = lax.rsqrt(jnp.mean(centred * centred, -1, keepdims=True) + LN_EPS)
    return centred * factor, factor


def norm_backward(upstream, normal, factor, gains):
    scaled = upstream * gains
    average = jnp.mean(scaled, -1, keepdims=True)
    cross = jnp.mean(scaled * normal, -1, keepdims=True)
    return factor * (scaled - average - normal * cross)


def column_sum(values):
    return jnp.sum(values.astype(F32), 0, keepdims=True)


def part_order(place, split):
    if not split:
        return list(range(PARTS))
    x_at, c_at = place[0], place[1]
    return [
        (x_at ^ x_rel) * 2 + (c_at ^ c_rel) for c_rel in range(2) for x_rel in range(2)
    ]


def weight_copies(w_ref, held, sems, parts, base):
    return [
        pltpu.make_async_copy(
            w_ref.at[:, part, :, pl.ds(base, SLAB)], held.at[slot], sems.at[slot]
        )
        for slot, part in enumerate(parts)
    ]


def projection_copy(w_ref, proj, sem):
    return pltpu.make_async_copy(w_ref.at[:, 0, :, pl.ds(LAYERS * PACK, DIM)], proj, sem)


def stored(refs, slot, value):
    refs[slot // 2 if len(refs) > 1 else 0][slot % 2 if len(refs) > 1 else slot] = value


def attention_kernel(base, split, place, *refs):
    x_ref, mask_ref, pair_ref, norm_ref, w_ref = refs[:5]
    first_ref, low_t_ref, packed_ref, chances_ref, normal_ref, factor_ref, first_t_ref = refs[5:12]
    mixture_refs = refs[12:-2]
    held, sems = refs[-2:]
    parts = part_order(place, split)
    copies = weight_copies(w_ref, held, sems, parts, base)
    for copy in copies:
        copy.start()
    hidden = x_ref[...]
    low = hidden.astype(BF)
    low_t_ref[...] = low.T
    mask = mask_ref[...]
    attended = jnp.zeros((ROWS, WIDTH), F32)
    for slot in range(PARTS):
        copies[slot].wait()
        weight = held[slot, :, :, :HELD].reshape(WIDTH, HELD)
        packed = (nn(low, weight) + pair_ref[parts[slot]]).astype(BF)
        packed_ref[slot] = packed
        values_t = packed[:, 2 * OWN : 3 * OWN].T
        mixed = [jnp.zeros((HEAD, ROWS), F32)]
        for head in range(HEADS_EACH):
            queries = packed[:, head * HEAD : (head + 1) * HEAD]
            keys = packed[:, OWN + head * HEAD : OWN + (head + 1) * HEAD]
            scores = nt(keys, queries) * 0.125 + mask
            powers = jnp.exp(scores - jnp.max(scores, 0, keepdims=True))
            chances = (powers * (1.0 / jnp.sum(powers, 0, keepdims=True))).astype(BF)
            chances_ref[slot * HEADS_EACH + head] = chances
            mixed.append(nn(values_t[head * HEAD : (head + 1) * HEAD], chances))
        mixture = jnp.concatenate(mixed, 0).astype(BF).T
        stored(mixture_refs, slot, mixture)
        attended = attended + nt(
            mixture, held[slot, :, :, SLAB - ROWS :].reshape(WIDTH, ROWS)
        )
    normal, factor = norm_forward(hidden + attended + norm_ref[0:1])
    normal_ref[...] = normal
    factor_ref[...] = jnp.broadcast_to(factor, factor_ref.shape)
    first = normal * norm_ref[1:2] + norm_ref[2:3]
    first_ref[...] = first
    first_t_ref[...] = first.astype(BF).T


def mlp_kernel(base, top, split, place, *refs):
    first_ref, up_bias_ref, norm_ref, w_ref = refs[:4]
    out_ref, slope_ref, normal_ref, factor_ref = refs[4:8]
    act_refs = refs[8 : 10 if split else 9]
    refs = refs[8 + len(act_refs) :]
    if top:
        emb_ref, unit_ref, scale_ref, top_t_ref = refs[:4]
        refs = refs[4:]
    up_held, down_held, up_sems, down_sems = refs[:4]
    parts = part_order(place, split)
    ups = weight_copies(w_ref, up_held, up_sems, parts, base + SLAB)
    downs = weight_copies(w_ref, down_held, down_sems, parts, base + 2 * SLAB)
    for slot in range(PARTS):
        ups[slot].start()
        downs[slot].start()
    if top:
        proj, proj_sem = refs[4:]
        proj_load = projection_copy(w_ref, proj, proj_sem)
        proj_load.start()
    first = first_ref[...]
    first_low = first.astype(BF)
    spread = jnp.zeros((ROWS, WIDTH), F32)
    for slot in range(PARTS):
        ups[slot].wait()
        pre_act = nn(first_low, up_held[slot].reshape(WIDTH, SLAB)) + up_bias_ref[parts[slot]]
        chance = 0.5 * (1.0 + lax.erf(pre_act * 0.7071067811865476))
        act = (pre_act * chance).astype(BF)
        stored(act_refs, slot, act)
        slope_ref[slot] = (
            chance + pre_act * jnp.exp(-0.5 * pre_act * pre_act) * 0.3989422804014327
        ).astype(BF)
        downs[slot].wait()
        spread = spread + nt(act, down_held[slot].reshape(WIDTH, SLAB))
    normal, factor = norm_forward(first + spread + norm_ref[3:4])
    normal_ref[...] = normal
    factor_ref[...] = jnp.broadcast_to(factor, factor_ref.shape)
    second = normal * norm_ref[4:5] + norm_ref[5:6]
    out_ref[...] = second
    if top:
        second_low = second.astype(BF)
        top_t_ref[...] = second_low.T
        proj_load.wait()
        embedded = nn(second_low, proj[...].reshape(WIDTH, DIM))
        scale = lax.rsqrt(jnp.sum(embedded * embedded, -1, keepdims=True) + NORM_EPS)
        unit = embedded * scale
        unit_ref[...] = unit
        emb_ref[...] = unit.astype(BF)
        scale_ref[...] = jnp.broadcast_to(scale, scale_ref.shape)


def mlp_pull_kernel(base, top, split, place, *refs):
    if top:
        grad_emb_ref, unit_ref, scale_ref, top_t_ref = refs[:4]
        refs = refs[4:]
    else:
        dy_ref = refs[0]
        refs = refs[1:]
    slope_ref, normal_ref, factor_ref, norm_ref, w_ref = refs[:5]
    grad_ref, sum_ref, low_t_ref = refs[5:8]
    pre_refs = refs[8 : 10 if split else 9]
    refs = refs[8 + len(pre_refs) :]
    if top:
        proj_grad_ref = refs[0]
        refs = refs[1:]
    up_held, down_held, up_sems, down_sems = refs[:4]
    parts = part_order(place, split)
    ups = weight_copies(w_ref, up_held, up_sems, parts, base + SLAB)
    downs = weight_copies(w_ref, down_held, down_sems, parts, base + 2 * SLAB)
    if top:
        proj, proj_sem = refs[4:]
        proj_load = projection_copy(w_ref, proj, proj_sem)
        proj_load.start()
    order = (2, 3, 0, 1) if split else (0, 1, 2, 3)
    for slot in order:
        downs[slot].start()
        ups[slot].start()
    if top:
        grad_emb = grad_emb_ref[...]
        unit = unit_ref[...]
        low_emb = (
            scale_ref[:, :1] * (grad_emb - unit * jnp.sum(grad_emb * unit, -1, keepdims=True))
        ).astype(BF)
        proj_grad_ref[...] = nn(top_t_ref[...], low_emb)
        proj_load.wait()
        dy = nt(low_emb, proj[...].reshape(WIDTH, DIM))
    else:
        dy = dy_ref[...]
    normal = normal_ref[...]
    grad_two = norm_backward(dy, normal, factor_ref[:, :1], norm_ref[4:5])
    sum_ref[0:1] = column_sum(grad_two)
    sum_ref[1:2] = column_sum(dy * normal)
    sum_ref[2:3] = column_sum(dy)
    sum_ref[7:8] = jnp.zeros((1, WIDTH), F32)
    low = grad_two.astype(BF)
    low_t_ref[...] = low.T
    grad_first = grad_two
    for slot in order:
        downs[slot].wait()
        grad_act = nn(low, down_held[slot].reshape(WIDTH, SLAB))
        pre_low = (grad_act * slope_ref[slot].astype(F32)).astype(BF)
        sum_ref[pl.ds(3 + parts[slot], 1), :] = column_sum(pre_low)
        stored(pre_refs, slot, pre_low)
        ups[slot].wait()
        grad_first = grad_first + nt(pre_low, up_held[slot].reshape(WIDTH, SLAB))
    grad_ref[...] = grad_first


def attention_pull_kernel(base, split, place, *refs):
    grad_first_ref, packed_ref, chances_ref, normal_ref, factor_ref, norm_ref, w_ref = refs[:7]
    dx_ref, sum_ref, low_t_ref = refs[7:10]
    packed_grad_refs = refs[10:-2]
    held, sems = refs[-2:]
    parts = part_order(place, split)
    copies = weight_copies(w_ref, held, sems, parts, base)
    order = (2, 3, 0, 1) if split else (0, 1, 2, 3)
    for slot in order:
        copies[slot].start()
    normal = normal_ref[...]
    grad_first = grad_first_ref[...]
    grad_one = norm_backward(grad_first, normal, factor_ref[:, :1], norm_ref[1:2])
    sum_ref[0:1] = column_sum(grad_one)
    sum_ref[1:2] = column_sum(grad_first * normal)
    sum_ref[2:3] = column_sum(grad_first)
    sum_ref[7:8] = jnp.zeros((1, WIDTH), F32)
    low = grad_one.astype(BF)
    low_t_ref[...] = low.T
    grad_input = grad_one
    for slot in order:
        copies[slot].wait()
        grad_mix = nn(low, held[slot, :, :, SLAB - ROWS :].reshape(WIDTH, ROWS)).astype(BF)
        packed = packed_ref[slot]
        keys_t = packed[:, OWN : 2 * OWN].T
        grad_queries, grad_keys, grad_values = [], [], []
        for head in range(HEADS_EACH):
            queries = packed[:, head * HEAD : (head + 1) * HEAD]
            values = packed[:, 2 * OWN + head * HEAD : 2 * OWN + (head + 1) * HEAD]
            upstream = grad_mix[:, (head + 1) * HEAD : (head + 2) * HEAD]
            chances = chances_ref[slot * HEADS_EACH + head]
            grad_values.append(nn(chances, upstream).astype(BF))
            wide = chances.astype(F32)
            product = wide * nt(values, upstream)
            grad_scores = (product - wide * jnp.sum(product, 0, keepdims=True)).astype(BF)
            grad_keys.append((nn(grad_scores, queries) * 0.125).astype(BF))
            grad_queries.append(nn(keys_t[head * HEAD : (head + 1) * HEAD], grad_scores) * 0.125)
        grad_packed = jnp.concatenate(
            [jnp.concatenate(grad_queries, 0).astype(BF).T]
            + grad_keys
            + grad_values
            + [jnp.zeros((ROWS, SLAB - 3 * OWN), BF)],
            1,
        )
        sum_ref[pl.ds(3 + parts[slot], 1), :] = column_sum(grad_packed)
        stored(packed_grad_refs, slot, grad_packed)
        grad_input = grad_input + nt(grad_packed, held[slot].reshape(WIDTH, SLAB))
    dx_ref[...] = grad_input


def rows_of(refs):
    return jnp.concatenate([ref[...] for ref in refs], 1)


def rows_at(refs, slot):
    return jnp.concatenate([ref[slot] for ref in refs], 0)


def block_sends(stage, slot, targets, sems, place, y_first, base):
    width = stage.shape[-1]
    lanes = pl.ds(base, width)
    if len(targets) == 1:
        copies = [
            pltpu.make_async_copy(
                stage.at[0, 0], targets[0].at[slot, :, lanes], sems.at[0, 0]
            )
        ]
    else:
        copies = []
        for y_rel in range(2):
            first, second = (y_rel, slot) if y_first else (slot, y_rel)
            for z_rel in range(4):
                copies.append(
                    pltpu.make_async_copy(
                        stage.at[(place[3] + z_rel) & 3, place[2] ^ y_rel],
                        targets[first].at[second, z_rel, :, lanes],
                        sems.at[y_rel, z_rel],
                    )
                )
    for copy in copies:
        copy.start()
    return copies


def mlp_grad_kernel(top, split, place, *refs):
    sides = 2 if split else 1
    groups = []
    for _ in range(4):
        groups.append(refs[:sides])
        refs = refs[sides:]
    first_t_refs, pre_refs, low_t_refs, act_refs = groups
    if top:
        proj_refs, refs = refs[:sides], refs[sides:]
    up_targets, refs = refs[:sides], refs[sides:]
    down_targets, refs = refs[:sides], refs[sides:]
    stage, sems = refs[:2]
    fold = stage.shape[2:]
    slots = PARTS // sides
    sends = []
    if top:
        proj_stage, proj_sems = refs[2:]
        total = proj_refs[0][...]
        for ref in proj_refs[1:]:
            total = total + ref[...]
        proj_stage[...] = total.astype(BF).reshape(proj_stage.shape)
        for slot in range(slots):
            sends += block_sends(
                proj_stage, slot, down_targets, proj_sems.at[slot], place, True, SLAB
            )
    first_t = rows_of(first_t_refs)
    low_t = rows_of(low_t_refs)
    for slot in reversed(range(slots)):
        stage[0, slot] = nn(first_t, rows_at(pre_refs, slot)).astype(BF).reshape(*fold)
        sends += block_sends(stage.at[0, slot], slot, up_targets, sems.at[0, slot], place, False, 0)
        stage[1, slot] = nn(low_t, rows_at(act_refs, slot)).astype(BF).reshape(*fold)
        sends += block_sends(stage.at[1, slot], slot, down_targets, sems.at[1, slot], place, True, 0)
    for copy in sends:
        copy.wait()


def attention_grad_kernel(y_first, split, place, *refs):
    sides = 2 if split else 1
    groups = []
    for _ in range(4):
        groups.append(refs[:sides])
        refs = refs[sides:]
    x_t_refs, packed_refs, low_t_refs, mixture_refs = groups
    targets, refs = refs[:sides], refs[sides:]
    stage, sems = refs
    fold = stage.shape[1:]
    sends = []
    x_t = rows_of(x_t_refs)
    low_t = rows_of(low_t_refs)
    for slot in reversed(range(PARTS // sides)):
        grad_weight = nn(x_t, rows_at(packed_refs, slot))
        grad_out = nn(low_t, rows_at(mixture_refs, slot))
        stage[slot] = (
            jnp.concatenate(
                [grad_weight[:, : SLAB - ROWS], grad_weight[:, SLAB - ROWS :] + grad_out], 1
            )
            .astype(BF)
            .reshape(*fold)
        )
        sends += block_sends(stage.at[slot], slot, targets, sems.at[slot], place, y_first, 0)
    for copy in sends:
        copy.wait()


def any_spec():
    return pl.BlockSpec(memory_space=pl.ANY)


def vmem_spec():
    return pl.BlockSpec(memory_space=pltpu.VMEM)


def shaped(shape, kind):
    return jax.ShapeDtypeStruct(shape, kind)


def price(micros):
    return pl.CostEstimate(
        flops=int(micros * 1e6), bytes_accessed=int(micros * 3e3), transcendentals=0
    )


def params():
    return pltpu.CompilerParams(vmem_limit_bytes=VMEM_BYTES)


def smem_spec():
    return pl.BlockSpec(memory_space=pltpu.SMEM)


def sided(split, shape, kind):
    if split:
        return [shaped((2, *shape), kind)] * 2
    return [shaped((PARTS, *shape), kind)]


def held_scratch(gathered, count):
    depth = (gathered.shape[0], gathered.shape[2])
    return [pltpu.VMEM((PARTS, *depth, SLAB), BF)] * count + [
        pltpu.SemaphoreType.DMA((PARTS,))
    ] * count


def projection_scratch(gathered):
    depth = (gathered.shape[0], gathered.shape[2])
    return [pltpu.VMEM((*depth, DIM), BF), pltpu.SemaphoreType.DMA]


def call(kernel, name, micros, place, args, outs, scratch, in_hbm=(), out_hbm=()):
    return pl.pallas_call(
        kernel,
        out_shape=outs,
        in_specs=[smem_spec()]
        + [any_spec() if at in in_hbm else vmem_spec() for at in range(len(args))],
        out_specs=[any_spec() if at in out_hbm else vmem_spec() for at in range(len(outs))],
        scratch_shapes=scratch,
        compiler_params=params(),
        cost_estimate=price(micros),
        name=name,
    )(place, *args)


def run_attention(layer_at, place, hidden, mask, pair_rows, norms, gathered, split):
    outs = [
        shaped((ROWS, WIDTH), F32),
        shaped((WIDTH, ROWS), BF),
        shaped((PARTS, ROWS, HELD), BF),
        shaped((PARTS * HEADS_EACH, ROWS, ROWS), BF),
        shaped((ROWS, WIDTH), F32),
        shaped((ROWS, DIM), F32),
        shaped((WIDTH, ROWS), BF),
    ] + sided(split, (ROWS, ROWS), BF)
    return call(
        functools.partial(attention_kernel, layer_at * PACK, split),
        f"attention_{layer_at}",
        9,
        place,
        [hidden, mask, pair_rows, norms, gathered],
        outs,
        held_scratch(gathered, 1),
        in_hbm=(4,),
    )


def run_mlp(layer_at, place, first, up_rows, norms, gathered, split):
    top = layer_at == LAYERS - 1
    outs = [
        shaped((ROWS, WIDTH), F32),
        shaped((PARTS, ROWS, SLAB), BF),
        shaped((ROWS, WIDTH), F32),
        shaped((ROWS, DIM), F32),
    ] + sided(split, (ROWS, SLAB), BF)
    scratch = held_scratch(gathered, 2)
    if top:
        outs += [
            shaped((ROWS, DIM), BF),
            shaped((ROWS, DIM), F32),
            shaped((ROWS, DIM), F32),
            shaped((WIDTH, ROWS), BF),
        ]
        scratch += projection_scratch(gathered)
    return call(
        functools.partial(mlp_kernel, layer_at * PACK, top, split),
        f"mlp_{layer_at}",
        9,
        place,
        [first, up_rows, norms, gathered],
        outs,
        scratch,
        in_hbm=(3,),
    )


def run_mlp_pull(layer_at, place, upstream, saved, norms, gathered, split):
    top = layer_at == LAYERS - 1
    outs = [
        shaped((ROWS, WIDTH), F32),
        shaped((8, WIDTH), F32),
        shaped((WIDTH, ROWS), BF),
    ] + sided(split, (ROWS, SLAB), BF)
    scratch = held_scratch(gathered, 2)
    if top:
        outs += [shaped((WIDTH, DIM), F32)]
        scratch += projection_scratch(gathered)
    args = [*upstream, *saved, norms, gathered]
    return call(
        functools.partial(mlp_pull_kernel, layer_at * PACK, top, split),
        f"pull_mlp_{layer_at}",
        8,
        place,
        args,
        outs,
        scratch,
        in_hbm=(len(args) - 1,),
    )


def run_attention_pull(layer_at, place, grad_first, saved, norms, gathered, split):
    outs = [
        shaped((ROWS, WIDTH), F32),
        shaped((8, WIDTH), F32),
        shaped((WIDTH, ROWS), BF),
    ] + sided(split, (ROWS, SLAB), BF)
    args = [grad_first, *saved, norms, gathered]
    return call(
        functools.partial(attention_pull_kernel, layer_at * PACK, split),
        f"pull_attention_{layer_at}",
        10,
        place,
        args,
        outs,
        held_scratch(gathered, 1),
        in_hbm=(len(args) - 1,),
    )


def grad_shapes(split, rows_each, width):
    if split:
        return [shaped((2, 4, rows_each, width), BF)] * 2
    return [shaped((PARTS, WIDTH, width), BF)]


def run_mlp_grad(layer_at, place, groups, split, rows_each):
    top = layer_at == LAYERS - 1
    args = [value for group in groups for value in group]
    sides = 2 if split else 1
    outs = grad_shapes(split, rows_each, SLAB)
    outs += grad_shapes(split, rows_each, SLAB + (DIM if top else 0))
    fold = (4, 2, rows_each) if split else (1, 1, WIDTH)
    slots = PARTS // sides
    scratch = [
        pltpu.VMEM((2, slots, *fold, SLAB), BF),
        pltpu.SemaphoreType.DMA((2, slots, 2, 4)),
    ]
    if top:
        scratch += [pltpu.VMEM((*fold, DIM), BF), pltpu.SemaphoreType.DMA((slots, 2, 4))]
    results = call(
        functools.partial(mlp_grad_kernel, top, split),
        f"grad_mlp_{layer_at}",
        8,
        place,
        args,
        outs,
        scratch,
        out_hbm=range(len(outs)),
    )
    return results[:sides], results[sides:]


def run_attention_grad(layer_at, y_first, place, groups, split, rows_each):
    args = [value for group in groups for value in group]
    outs = grad_shapes(split, rows_each, SLAB)
    fold = (4, 2, rows_each) if split else (1, 1, WIDTH)
    slots = PARTS // (2 if split else 1)
    return call(
        functools.partial(attention_grad_kernel, y_first, split),
        f"grad_attention_{layer_at}",
        5,
        place,
        args,
        outs,
        [pltpu.VMEM((slots, *fold, SLAB), BF), pltpu.SemaphoreType.DMA((slots, 2, 4))],
        out_hbm=range(len(outs)),
    )


CORE_SWAP = [(at, at ^ 1) for at in range(PARTS)]
X_SWAP = [(at, at ^ 2) for at in range(PARTS)]
Y_SWAP = [(at, at ^ 1) for at in range(8)]
Z_GROUPS = [[0, 2, 4, 6], [1, 3, 5, 7]]


def added(*terms):
    total = terms[0].astype(F32)
    for term in terms[1:]:
        total = total + term.astype(F32)
    return total


def over_x(value, name):
    with jax.named_scope(f"x_{name}"):
        return lax.ppermute(value, "tensor", X_SWAP)


def over_y(value, name):
    with jax.named_scope(f"y_{name}"):
        return lax.ppermute(value, "dp", Y_SWAP)


def over_core(value, name="pair"):
    with jax.named_scope(f"core_{name}"):
        return lax.ppermute(value, "tensor", CORE_SWAP)


def along_z(value, step, name):
    pairs = [(at, ((at // 2 + step) % 4) * 2 + at % 2) for at in range(8)]
    with jax.named_scope(f"z_{name}_{step}"):
        return lax.ppermute(value, "dp", pairs)


def tied(*values):
    return lax.optimization_barrier(values)


class Reduction:
    def __init__(self, name, pieces, y_first):
        self.name = name
        self.keep, self.send = pieces
        self.first, self.second = (over_y, over_x) if y_first else (over_x, over_y)

    def start(self):
        self.one = self.first(self.send, self.name + "_first")

    def add_second(self):
        with jax.named_scope(f"add_{self.name}_second"):
            self.terms = added(self.keep[1], self.one[1]).astype(BF)

    def start_second(self):
        self.two = self.second(self.terms, self.name + "_second")

    def add_third(self):
        with jax.named_scope(f"add_{self.name}_third"):
            self.blocks = [
                added(self.keep[0, step], self.one[0, step], self.two[step]).astype(BF)
                for step in range(1, 4)
            ]

    def start_third(self):
        self.arrived = [
            along_z(block, step + 1, self.name) for step, block in enumerate(self.blocks)
        ]

    def total(self):
        with jax.named_scope(f"add_{self.name}_last"):
            return added(self.keep[0, 0], self.one[0, 0], self.two[0], *self.arrived)


def reduce_whole(grads, devices):
    grads = grads.reshape(PARTS, devices, WIDTH // devices, -1)
    grads = jnp.transpose(grads, (1, 0, 2, 3)).reshape(devices * PARTS, WIDTH // devices, -1)
    return lax.psum_scatter(grads, BOTH, scatter_dimension=0, tiled=True)[0].astype(F32)


def total_over_all(value, split):
    if not split:
        return lax.psum(value, BOTH)
    value = value + over_core(value)
    value = value + over_x(value, "sums")
    value = value + over_y(value, "sums")
    value = value + lax.ppermute(value, "dp", [(at, at ^ 2) for at in range(8)])
    return value + lax.ppermute(value, "dp", [(at, at ^ 4) for at in range(8)])


def score_kernel(count, lengths_ref, log_ref, queries_ref, passages_ref, powers_ref, sums_ref, logit_ref):
    queries = queries_ref[...]

    def single(at, carry):
        similar = nt(passages_ref[at], queries)
        spot = lax.broadcasted_iota(jnp.int32, (PLEN, ROWS), 0)
        powers = jnp.where(spot < lengths_ref[at], jnp.exp(SHARPNESS * similar), 0.0)
        powers_ref[at] = powers.astype(BF)
        sums_ref[pl.ds(at, 1), :] = jnp.sum(powers, 0, keepdims=True)
        return carry

    lax.fori_loop(0, count, single, 0)
    smooth = (jnp.log(sums_ref[...]) - log_ref[...]) / SHARPNESS
    token = lax.broadcasted_iota(jnp.int32, (ROWS, DIM), 0) // QLEN
    query = lax.broadcasted_iota(jnp.int32, (ROWS, DIM), 1)
    pick = (token == query).astype(F32)
    logit_ref[...] = SCORE_SCALE * jnp.dot(
        smooth, pick, precision=lax.Precision.HIGHEST, preferred_element_type=F32
    )


def pull_kernel(count, powers_ref, steer_ref, queries_ref, passages_ref, passage_out, query_out, total):
    queries = queries_ref[...]
    total[...] = jnp.zeros_like(total)

    def single(at, carry):
        shares = (powers_ref[at].astype(F32) * steer_ref[pl.ds(at, 1), :]).astype(BF)
        passage_out[at] = nn(shares, queries).astype(BF)
        total[...] += nn(passages_ref[at].T, shares)
        return carry

    lax.fori_loop(0, count, single, 0)
    query_out[...] = total[...].T


def scores_of(queries, passages, lengths):
    count = passages.shape[0]
    return pl.pallas_call(
        functools.partial(score_kernel, count),
        out_shape=[
            shaped((count, PLEN, ROWS), BF),
            shaped((count, ROWS), F32),
            shaped((count, DIM), F32),
        ],
        in_specs=[pl.BlockSpec(memory_space=pltpu.SMEM)] + [vmem_spec()] * 3,
        out_specs=[vmem_spec()] * 3,
        compiler_params=params(),
        cost_estimate=price(4),
        name="scores",
    )(lengths, jnp.log(lengths.astype(F32))[:, None], queries, passages)


def pulls_of(powers, steer, queries, passages):
    count = passages.shape[0]
    return pl.pallas_call(
        functools.partial(pull_kernel, count),
        out_shape=[shaped((count, PLEN, DIM), BF), shaped((ROWS, DIM), F32)],
        in_specs=[vmem_spec()] * 4,
        out_specs=[vmem_spec()] * 2,
        scratch_shapes=[pltpu.VMEM((DIM, ROWS), F32)],
        compiler_params=params(),
        cost_estimate=price(4),
        name="score_pulls",
    )(powers, steer, queries, passages)


def adam_step(master, moment, second, gradient, decay):
    moment_new = BETA_ONE * moment + (1.0 - BETA_ONE) * gradient
    second_new = BETA_TWO * second + (1.0 - BETA_TWO) * gradient * gradient
    rising = moment_new / (1.0 - BETA_ONE**STEP)
    spread = jnp.sqrt(second_new / (1.0 - BETA_TWO**STEP))
    return (moment_new, second_new, -LEARN_RATE * (rising / (spread + ADAM_EPS) + decay * master))


def pack_weights(qkv, out, up, down, proj):
    pieces = []
    for layer_at in range(LAYERS):
        pieces += [qkv[layer_at, 0], qkv[layer_at, 1], qkv[layer_at, 2]]
        pieces += [out[layer_at].T, up[layer_at], down[layer_at].T]
    pieces.append(proj)
    return jnp.concatenate([piece.astype(BF) for piece in pieces], 1)


def unpack_grads(att_list, up_list, down_list):
    qkv = jnp.stack(
        [
            jnp.stack([att[:, kind * OWN : (kind + 1) * OWN] for kind in range(3)])
            for att in att_list
        ]
    )
    out = jnp.stack([att[:, 3 * OWN :].T for att in att_list])
    return qkv, out, jnp.stack(up_list), jnp.stack([down[:, :SLAB].T for down in down_list])


def to_output_rows(grad, tensor_at):
    rows = PDEV * PLEN // PARTS
    query_rows = QDEV * QLEN // PARTS
    start = jnp.where(tensor_at == PARTS - 1, 0, ROWS - rows)
    step = lax.ppermute(
        lax.dynamic_slice_in_dim(grad, start, rows, 0),
        "tensor",
        [(at, (at + 1) % PARTS) for at in range(PARTS)],
    )
    last = PARTS - 1
    one = lax.ppermute(grad[query_rows : 2 * query_rows], "tensor", [(last, 1)])
    two = lax.ppermute(grad[2 * query_rows : 3 * query_rows], "tensor", [(last, 2)])
    own = grad[last * query_rows :]
    query = jnp.where(
        tensor_at == 0,
        step[:query_rows],
        jnp.where(tensor_at == 1, one, jnp.where(tensor_at == 2, two, own)),
    )
    unit = query_rows
    passage = jnp.where(
        tensor_at == 0,
        grad[:rows],
        jnp.where(
            tensor_at == 1,
            jnp.concatenate([step[2 * unit :], grad[: 2 * unit]]),
            jnp.where(tensor_at == 2, jnp.concatenate([step[unit:], grad[:unit]]), step),
        ),
    )
    return query, passage


def body(
    query_tokens,
    passage_tokens,
    query_mask,
    passage_lengths,
    positives,
    qkv_weight,
    qkv_moment,
    qkv_second,
    out_weight,
    out_moment,
    out_second,
    up_weight,
    up_moment,
    up_second,
    down_weight,
    down_moment,
    down_second,
    projection,
    projection_moment,
    projection_second,
    bias_pair,
    bias_pair_moment,
    bias_pair_second,
    bias_up,
    bias_up_moment,
    bias_up_second,
    norm_terms,
    norm_terms_moment,
    norm_terms_second,
):
    devices = lax.axis_size("dp")
    dev_index = lax.axis_index("dp")
    tensor_at = lax.axis_index("tensor")
    last = PARTS - 1
    is_query = tensor_at == last
    rows_each = WIDTH // devices
    pack = pack_weights(qkv_weight, out_weight, up_weight, down_weight, projection)
    gathered = lax.all_gather(pack, BOTH, axis=0, tiled=False)
    gathered = gathered.reshape(devices, PARTS, rows_each, -1)
    split = devices == 8
    if not split:
        gathered = jnp.transpose(gathered, (1, 0, 2, 3)).reshape(1, PARTS, WIDTH, -1)
    small = jnp.concatenate([bias_pair.reshape(-1), bias_up.reshape(-1)])
    small_all = lax.all_gather(small, "tensor", axis=0, tiled=False)
    pair_all = small_all[:, : LAYERS * 2 * OWN].reshape(PARTS, LAYERS, 2, OWN)
    up_all = small_all[:, LAYERS * 2 * OWN :].reshape(PARTS, LAYERS, 1, SLAB)
    pair_rows = jnp.concatenate(
        [
            pair_all[:, :, 0],
            jnp.zeros((PARTS, LAYERS, OWN), F32),
            pair_all[:, :, 1],
            jnp.zeros((PARTS, LAYERS, HELD - 3 * OWN), F32),
        ],
        -1,
    )[:, :, None, :]

    passage_at = jnp.minimum(tensor_at, last - 1)
    own_passage = lax.dynamic_slice_in_dim(passage_tokens, passage_at * PLEN, PLEN, 0)
    hidden = jnp.where(is_query, query_tokens, own_passage)
    own_length = lax.dynamic_slice_in_dim(passage_lengths, dev_index * PDEV + passage_at, 1, 0)
    spot = jnp.arange(ROWS, dtype=jnp.int32)
    key_valid = jnp.where(is_query, query_mask.reshape(ROWS) == 1, spot < own_length)
    together = jnp.logical_or(
        jnp.logical_not(is_query), spot[:, None] // QLEN == spot[None, :] // QLEN
    )
    mask = jnp.where(jnp.logical_and(key_valid[:, None], together), 0.0, MASKED).astype(F32)

    place = jnp.stack([tensor_at // 2, tensor_at % 2, dev_index % 2, dev_index // 2]).astype(jnp.int32)

    def sides_of(keep, send):
        return [keep, over_core(send)] if split else [keep]

    def shared(value):
        return [value, over_core(value)] if split else [value]

    saved_list = []
    for layer_at in range(LAYERS):
        outs = run_attention(
            layer_at,
            place,
            hidden,
            mask,
            pair_rows[:, layer_at],
            norm_terms[layer_at],
            gathered,
            split,
        )
        first, x_t, packed, chances, normal_one, factor_one, first_t = outs[:7]
        mixtures = sides_of(outs[7], outs[-1])
        outs = run_mlp(
            layer_at, place, first, up_all[:, layer_at], norm_terms[layer_at], gathered, split
        )
        hidden, slope, normal_two, factor_two = outs[:4]
        acts = sides_of(outs[4], outs[5 if split else 4])
        saved_list.append(
            dict(
                mlp=(slope, normal_two, factor_two),
                attention=(packed, chances, normal_one, factor_one),
                x_t=shared(x_t),
                first_t=shared(first_t),
                mixtures=mixtures,
                acts=acts,
            )
        )
    embedding, unit, scale, top_t = outs[-4:]

    passages = lax.all_to_all(
        jnp.broadcast_to(embedding[None], (devices, ROWS, DIM)), "dp", 0, 0, tiled=True
    )
    queries = embedding
    arrived = [lax.ppermute(embedding, "tensor", [(last, at)]) for at in range(last)]
    for at in range(last):
        queries = jnp.where(tensor_at == at, arrived[at], queries)
    length_table = passage_lengths.reshape(devices, PDEV)
    own_lengths = lax.dynamic_slice_in_dim(length_table, passage_at, 1, 1)[:, 0]
    powers, sums, logit_part = scores_of(queries, passages, own_lengths)
    logits = lax.all_gather(logit_part[:, :QDEV], "tensor", axis=0, tiled=False)[:last]
    own_positives = lax.dynamic_slice_in_dim(positives, dev_index * QDEV, QDEV, 0)
    ids = (
        lax.broadcasted_iota(jnp.int32, logits.shape, 1) * PDEV
        + lax.broadcasted_iota(jnp.int32, logits.shape, 0)
    )
    chosen = ids == own_positives[None, None, :]
    highest = jnp.max(logits, (0, 1), keepdims=True)
    raised = jnp.exp(logits - highest)
    summed = jnp.sum(raised, (0, 1), keepdims=True)
    losses = highest + jnp.log(summed) - jnp.sum(jnp.where(chosen, logits, 0.0), (0, 1), keepdims=True)
    deltas = raised / summed - chosen.astype(F32)
    own_deltas = lax.dynamic_slice_in_dim(deltas, passage_at, 1, 0)[0]
    steer = jnp.where(is_query, 0.0, SCORE_SCALE) * jnp.repeat(own_deltas, QLEN, axis=1) / sums
    passage_terms, query_terms = pulls_of(powers, steer, queries, passages)
    passage_back = lax.all_to_all(passage_terms, "dp", 0, 0, tiled=True)
    grad_passage = jnp.sum(passage_back.astype(F32), 0)
    returned = [lax.ppermute(query_terms, "tensor", [(at, last)]) for at in range(last)]
    grad_query = returned[0] + returned[1] + returned[2]
    grad_emb = jnp.where(is_query, grad_query, grad_passage)

    upstream = (grad_emb, unit, scale, top_t)
    mlp_sums, attention_sums = [None] * LAYERS, [None] * LAYERS

    def mlp_pull(layer_at, upstream):
        saved = saved_list[layer_at]
        outs = run_mlp_pull(
            layer_at, place, upstream, saved["mlp"], norm_terms[layer_at], gathered, split
        )
        grad_first, mlp_sums[layer_at], low_t = outs[:3]
        groups = [
            saved["first_t"],
            sides_of(outs[3], outs[4 if split else 3]),
            shared(low_t),
            saved["acts"],
        ]
        if layer_at == LAYERS - 1:
            groups.append(shared(outs[-1]))
        return grad_first, groups

    def attention_pull(layer_at, grad_first):
        saved = saved_list[layer_at]
        outs = run_attention_pull(
            layer_at,
            place,
            grad_first,
            saved["attention"],
            norm_terms[layer_at],
            gathered,
            split,
        )
        dx, attention_sums[layer_at], low_t = outs[:3]
        return dx, [
            saved["x_t"],
            sides_of(outs[3], outs[-1]),
            shared(low_t),
            saved["mixtures"],
        ]

    def mlp_grad(layer_at, groups):
        return run_mlp_grad(layer_at, place, groups, split, rows_each)

    def attention_grad(layer_at, y_first, groups):
        return run_attention_grad(layer_at, y_first, place, groups, split, rows_each)

    if split:
        grad_first, mlp_groups = mlp_pull(1, upstream)
        up_grads, down_grads = mlp_grad(1, mlp_groups)
        up_one, down_one = Reduction("up_1", up_grads, False), Reduction("down_1", down_grads, True)
        grad_first, up_one.send, down_one.send = tied(grad_first, up_one.send, down_one.send)
        up_one.start()
        down_one.start()
        dx, att_groups = attention_pull(1, grad_first)
        att_one = Reduction("att_1", attention_grad(1, False, att_groups), False)
        dx, att_one.send = tied(dx, att_one.send)
        att_one.start()
        grad_first, mlp_groups = mlp_pull(0, (dx,))
        up_one.add_second()
        down_one.add_second()
        mlp_groups[0][0], up_one.terms, down_one.terms = tied(
            mlp_groups[0][0], up_one.terms, down_one.terms
        )
        up_one.start_second()
        down_one.start_second()
        up_grads, down_grads = mlp_grad(0, mlp_groups)
        up_zero = Reduction("up_0", up_grads, False)
        down_zero = Reduction("down_0", down_grads, True)
        grad_first, up_zero.send, down_zero.send = tied(grad_first, up_zero.send, down_zero.send)
        up_zero.start()
        down_zero.start()
        dx, att_groups = attention_pull(0, grad_first)
        att_one.add_second()
        att_groups[0][0], att_one.terms = tied(att_groups[0][0], att_one.terms)
        att_one.start_second()
        up_one.add_third()
        down_one.add_third()
        up_zero.add_second()
        down_zero.add_second()
        att_groups[0][0], up_zero.terms, down_zero.terms = tied(
            att_groups[0][0], up_zero.terms, down_zero.terms
        )
        att_zero = Reduction("att_0", attention_grad(0, True, att_groups), True)
        att_zero.start()
        att_one.add_third()
        att_zero.add_second()
        for item in (up_one, down_one, att_one):
            item.start_third()
        for item in (up_zero, down_zero, att_zero):
            item.start_second()
        for item in (up_zero, down_zero, att_zero):
            item.add_third()
            item.start_third()
        attention_sums[0] = tied(attention_sums[0], att_zero.terms)[0]
        att_list = [att_zero.total(), att_one.total()]
        up_list = [up_zero.total(), up_one.total()]
        down_list = [down_zero.total(), down_one.total()]
    else:
        att_list, up_list, down_list = [], [], []
        dx = None
        for layer_at in range(LAYERS - 1, -1, -1):
            grad_first, groups = mlp_pull(layer_at, (dx,) if upstream is None else upstream)
            upstream = None
            up_grads, down_grads = mlp_grad(layer_at, groups)
            dx, groups = attention_pull(layer_at, grad_first)
            att_grads = attention_grad(layer_at, False, groups)
            up_list.insert(0, reduce_whole(up_grads[0], devices))
            down_list.insert(0, reduce_whole(down_grads[0], devices))
            att_list.insert(0, reduce_whole(att_grads[0], devices))
    loss_part = jnp.where(tensor_at == 0, jnp.sum(losses), 0.0)
    sums = jnp.stack([attention_sums[0], mlp_sums[0], attention_sums[1], mlp_sums[1]])
    row_ids = lax.broadcasted_iota(jnp.int32, sums.shape, 1)
    sums = sums + jnp.where(row_ids == 7, loss_part, 0.0)
    sums = total_over_all(sums, split).reshape(LAYERS, 2, 8, WIDTH)
    norms_grad = sums[:, :, :3].reshape(LAYERS, 6, WIDTH)
    own_sums = lax.dynamic_slice_in_dim(sums, 3 + tensor_at, 1, 2)[:, :, 0]
    pair_grad = jnp.stack([own_sums[:, 0, :OWN], own_sums[:, 0, 2 * OWN : 3 * OWN]], 1)
    bias_grad = own_sums[:, 1]
    loss_mean = sums[0, 0, 7, 0] / (QDEV * devices)
    projection_grad = down_list[LAYERS - 1][:, SLAB:]
    qkv_grad, out_grad, up_grad, down_grad = unpack_grads(att_list, up_list, down_list)
    qkv_m, qkv_v, qkv_u = adam_step(qkv_weight, qkv_moment, qkv_second, qkv_grad, WEIGHT_DECAY)
    out_m, out_v, out_u = adam_step(out_weight, out_moment, out_second, out_grad, WEIGHT_DECAY)
    up_m, up_v, up_u = adam_step(up_weight, up_moment, up_second, up_grad, WEIGHT_DECAY)
    down_m, down_v, down_u = adam_step(
        down_weight, down_moment, down_second, down_grad, WEIGHT_DECAY
    )
    proj_m, proj_v, proj_u = adam_step(
        projection, projection_moment, projection_second, projection_grad, WEIGHT_DECAY
    )
    pair_m, pair_v, pair_u = adam_step(
        bias_pair, bias_pair_moment, bias_pair_second, pair_grad, 0.0
    )
    bias_m, bias_v, bias_u = adam_step(bias_up, bias_up_moment, bias_up_second, bias_grad, 0.0)
    norm_m, norm_v, norm_u = adam_step(
        norm_terms, norm_terms_moment, norm_terms_second, norms_grad, 0.0
    )
    query_grad, passage_grad = to_output_rows(dx, tensor_at)
    return (
        loss_mean,
        query_grad,
        passage_grad,
        qkv_grad,
        qkv_m,
        qkv_v,
        qkv_u,
        out_grad,
        out_m,
        out_v,
        out_u,
        up_grad,
        up_m,
        up_v,
        up_u,
        down_grad,
        down_m,
        down_v,
        down_u,
        projection_grad,
        proj_m,
        proj_v,
        proj_u,
        pair_grad,
        pair_m,
        pair_v,
        pair_u,
        bias_grad,
        bias_m,
        bias_v,
        bias_u,
        norms_grad,
        norm_m,
        norm_v,
        norm_u,
    )


def solution(mesh):
    placed = (
        P("dp", None),
        P("dp", None),
        P("dp", None),
        P(),
        P(),
        P(None, None, "dp", "tensor"),
        P(None, None, "dp", "tensor"),
        P(None, None, "dp", "tensor"),
        P(None, "tensor", "dp"),
        P(None, "tensor", "dp"),
        P(None, "tensor", "dp"),
        P(None, "dp", "tensor"),
        P(None, "dp", "tensor"),
        P(None, "dp", "tensor"),
        P(None, "tensor", "dp"),
        P(None, "tensor", "dp"),
        P(None, "tensor", "dp"),
        P("dp", None),
        P("dp", None),
        P("dp", None),
        P(None, None, "tensor"),
        P(None, None, "tensor"),
        P(None, None, "tensor"),
        P(None, "tensor"),
        P(None, "tensor"),
        P(None, "tensor"),
        P(),
        P(),
        P(),
    )
    return jax.shard_map(
        body,
        mesh=mesh,
        in_specs=placed,
        out_specs=(
            P(),
            P(("dp", "tensor"), None),
            P(("dp", "tensor"), None),
            P(None, None, "dp", "tensor"),
            P(None, None, "dp", "tensor"),
            P(None, None, "dp", "tensor"),
            P(None, None, "dp", "tensor"),
            P(None, "tensor", "dp"),
            P(None, "tensor", "dp"),
            P(None, "tensor", "dp"),
            P(None, "tensor", "dp"),
            P(None, "dp", "tensor"),
            P(None, "dp", "tensor"),
            P(None, "dp", "tensor"),
            P(None, "dp", "tensor"),
            P(None, "tensor", "dp"),
            P(None, "tensor", "dp"),
            P(None, "tensor", "dp"),
            P(None, "tensor", "dp"),
            P("dp", None),
            P("dp", None),
            P("dp", None),
            P("dp", None),
            P(None, None, "tensor"),
            P(None, None, "tensor"),
            P(None, None, "tensor"),
            P(None, None, "tensor"),
            P(None, "tensor"),
            P(None, "tensor"),
            P(None, "tensor"),
            P(None, "tensor"),
            P(),
            P(),
            P(),
            P(),
        ),
        check_vma=False,
    )
```

```python
import functools

import jax
import jax.numpy as jnp
from jax import lax
from jax.experimental import pallas as pl
from jax.experimental.pallas import tpu as pltpu
from jax.sharding import PartitionSpec as P

WIDTH = 768
HEAD = 64
DIM = 128
QLEN = 32
PLEN = 256
LAYERS = 2
STEP = 10
QDEV = 8
PDEV = 3
ROWS = 256
PARTS = 4
HEADS_EACH = 3
OWN = HEADS_EACH * HEAD
SLAB = 768
HELD = 640
PACK = 3 * SLAB

MASKED = -1e30
SHARPNESS = 24.0
SCORE_SCALE = 4.0
LN_EPS = 1e-12
NORM_EPS = 1e-12
BETA_ONE = 0.9
BETA_TWO = 0.999
ADAM_EPS = 1e-08
LEARN_RATE = 0.02
WEIGHT_DECAY = 0.01
VMEM_BYTES = 60 * 1024 * 1024

BF = jnp.bfloat16
F32 = jnp.float32
BOTH = ("dp", "tensor")


def nn(left, right):
    return jnp.dot(left, right, preferred_element_type=F32)


def nt(left, right):
    return lax.dot_general(left, right, (((1,), (1,)), ((), ())), preferred_element_type=F32)


def norm_forward(values):
    average = jnp.mean(values, -1, keepdims=True)
    centred = values - average
    factor = lax.rsqrt(jnp.mean(centred * centred, -1, keepdims=True) + LN_EPS)
    return centred * factor, factor


def norm_backward(upstream, normal, factor, gains):
    scaled = upstream * gains
    average = jnp.mean(scaled, -1, keepdims=True)
    cross = jnp.mean(scaled * normal, -1, keepdims=True)
    return factor * (scaled - average - normal * cross)


def column_sum(values):
    return jnp.sum(values.astype(F32), 0, keepdims=True)


def part_order(place, split):
    if not split:
        return list(range(PARTS))
    x_at, c_at = place[0], place[1]
    return [
        (x_at ^ x_rel) * 2 + (c_at ^ c_rel) for c_rel in range(2) for x_rel in range(2)
    ]


class Copies:
    def __init__(self, copies):
        self.copies = copies

    def start(self):
        for copy in self.copies:
            copy.start()

    def wait(self):
        for copy in self.copies:
            copy.wait()


def weight_copies(refs, plan, held, sems, parts, place):
    kind, base = plan
    groups = []
    for slot, part in enumerate(parts):
        copies = []
        if kind == "whole":
            source = refs[0].at[:, :, part, :, pl.ds(base, SLAB)]
            copies.append(pltpu.make_async_copy(source, held.at[slot], sems.at[slot, 0]))
        else:
            c_rel, x_rel = divmod(slot, 2)
            for y_rel in range(2):
                outer, inner = (x_rel, y_rel) if kind == "x_last" else (y_rel, x_rel)
                for back in range(4):
                    copies.append(
                        pltpu.make_async_copy(
                            refs[2 * c_rel + outer].at[inner, back],
                            held.at[slot, (place[3] - back) & 3, place[2] ^ y_rel],
                            sems.at[slot, 4 * y_rel + back],
                        )
                    )
        groups.append(Copies(copies))
    return groups


def projection_copy(w_ref, proj, sem, base):
    return pltpu.make_async_copy(w_ref.at[:, :, 0, :, pl.ds(base, DIM)], proj, sem)


def stored(refs, slot, value):
    refs[slot // 2 if len(refs) > 1 else 0][slot % 2 if len(refs) > 1 else slot] = value


def attention_kernel(plan, count, split, place, *refs):
    x_ref, mask_ref, pair_ref, norm_ref = refs[:4]
    w_refs, refs = refs[4 : 4 + count], refs[4 + count :]
    first_ref, low_t_ref, packed_ref, chances_ref, normal_ref, factor_ref, first_t_ref = refs[:7]
    mixture_refs = refs[7:-2]
    held, sems = refs[-2:]
    parts = part_order(place, split)
    copies = weight_copies(w_refs, plan, held, sems, parts, place)
    for copy in copies:
        copy.start()
    hidden = x_ref[...]
    low = hidden.astype(BF)
    low_t_ref[...] = low.T
    mask = mask_ref[...]
    attended = jnp.zeros((ROWS, WIDTH), F32)
    for slot in range(PARTS):
        copies[slot].wait()
        weight = held[slot, :, :, :, :HELD].reshape(WIDTH, HELD)
        packed = (nn(low, weight) + pair_ref[slot]).astype(BF)
        packed_ref[slot] = packed
        values_t = packed[:, 2 * OWN : 3 * OWN].T
        mixed = [jnp.zeros((HEAD, ROWS), F32)]
        for head in range(HEADS_EACH):
            queries = packed[:, head * HEAD : (head + 1) * HEAD]
            keys = packed[:, OWN + head * HEAD : OWN + (head + 1) * HEAD]
            scores = nt(keys, queries) * 0.125 + mask
            powers = jnp.exp(scores - jnp.max(scores, 0, keepdims=True))
            chances = (powers * (1.0 / jnp.sum(powers, 0, keepdims=True))).astype(BF)
            chances_ref[slot * HEADS_EACH + head] = chances
            mixed.append(nn(values_t[head * HEAD : (head + 1) * HEAD], chances))
        mixture = jnp.concatenate(mixed, 0).astype(BF).T
        stored(mixture_refs, slot, mixture)
        attended = attended + nt(
            mixture, held[slot, :, :, :, SLAB - ROWS :].reshape(WIDTH, ROWS)
        )
    normal, factor = norm_forward(hidden + attended + norm_ref[0:1])
    normal_ref[...] = normal
    factor_ref[...] = jnp.broadcast_to(factor, factor_ref.shape)
    first = normal * norm_ref[1:2] + norm_ref[2:3]
    first_ref[...] = first
    first_t_ref[...] = first.astype(BF).T


def mlp_kernel(up_plan, down_plan, proj_base, count, top, split, place, *refs):
    first_ref, up_bias_ref, norm_ref = refs[:3]
    up_refs, down_refs = refs[3 : 3 + count], refs[3 + count : 3 + 2 * count]
    refs = refs[3 + 2 * count :]
    out_ref, slope_ref, normal_ref, factor_ref = refs[:4]
    act_refs = refs[4 : 6 if split else 5]
    refs = refs[4 + len(act_refs) :]
    if top:
        emb_ref, unit_ref, scale_ref, top_t_ref = refs[:4]
        refs = refs[4:]
    up_held, down_held, up_sems, down_sems = refs[:4]
    parts = part_order(place, split)
    ups = weight_copies(up_refs, up_plan, up_held, up_sems, parts, place)
    downs = weight_copies(down_refs, down_plan, down_held, down_sems, parts, place)
    for slot in range(PARTS):
        ups[slot].start()
        downs[slot].start()
    if top:
        proj, proj_sem = refs[4:]
        proj_load = projection_copy(up_refs[0], proj, proj_sem, proj_base)
        proj_load.start()
    first = first_ref[...]
    first_low = first.astype(BF)
    spread = jnp.zeros((ROWS, WIDTH), F32)
    for slot in range(PARTS):
        ups[slot].wait()
        pre_act = nn(first_low, up_held[slot].reshape(WIDTH, SLAB)) + up_bias_ref[slot]
        chance = 0.5 * (1.0 + lax.erf(pre_act * 0.7071067811865476))
        act = (pre_act * chance).astype(BF)
        stored(act_refs, slot, act)
        slope_ref[slot] = (
            chance + pre_act * jnp.exp(-0.5 * pre_act * pre_act) * 0.3989422804014327
        ).astype(BF)
        downs[slot].wait()
        spread = spread + nt(act, down_held[slot].reshape(WIDTH, SLAB))
    normal, factor = norm_forward(first + spread + norm_ref[3:4])
    normal_ref[...] = normal
    factor_ref[...] = jnp.broadcast_to(factor, factor_ref.shape)
    second = normal * norm_ref[4:5] + norm_ref[5:6]
    out_ref[...] = second
    if top:
        second_low = second.astype(BF)
        top_t_ref[...] = second_low.T
        proj_load.wait()
        embedded = nn(second_low, proj[...].reshape(WIDTH, DIM))
        scale = lax.rsqrt(jnp.sum(embedded * embedded, -1, keepdims=True) + NORM_EPS)
        unit = embedded * scale
        unit_ref[...] = unit
        emb_ref[...] = unit.astype(BF)
        scale_ref[...] = jnp.broadcast_to(scale, scale_ref.shape)


def mlp_pull_kernel(up_plan, down_plan, proj_base, count, top, split, place, *refs):
    if top:
        grad_emb_ref, unit_ref, scale_ref, top_t_ref = refs[:4]
        refs = refs[4:]
    else:
        dy_ref = refs[0]
        refs = refs[1:]
    slope_ref, normal_ref, factor_ref, norm_ref = refs[:4]
    up_refs, down_refs = refs[4 : 4 + count], refs[4 + count : 4 + 2 * count]
    refs = refs[4 + 2 * count :]
    grad_ref, sum_ref, low_t_ref = refs[:3]
    pre_refs = refs[3 : 5 if split else 4]
    refs = refs[3 + len(pre_refs) :]
    if top:
        proj_grad_ref = refs[0]
        refs = refs[1:]
    up_held, down_held, up_sems, down_sems = refs[:4]
    parts = part_order(place, split)
    ups = weight_copies(up_refs, up_plan, up_held, up_sems, parts, place)
    downs = weight_copies(down_refs, down_plan, down_held, down_sems, parts, place)
    if top:
        proj, proj_sem = refs[4:]
        proj_load = projection_copy(up_refs[0], proj, proj_sem, proj_base)
        proj_load.start()
    order = (2, 3, 0, 1) if split else (0, 1, 2, 3)
    for slot in order:
        downs[slot].start()
        ups[slot].start()
    if top:
        grad_emb = grad_emb_ref[...]
        unit = unit_ref[...]
        low_emb = (
            scale_ref[:, :1] * (grad_emb - unit * jnp.sum(grad_emb * unit, -1, keepdims=True))
        ).astype(BF)
        proj_grad_ref[...] = nn(top_t_ref[...], low_emb)
        proj_load.wait()
        dy = nt(low_emb, proj[...].reshape(WIDTH, DIM))
    else:
        dy = dy_ref[...]
    normal = normal_ref[...]
    grad_two = norm_backward(dy, normal, factor_ref[:, :1], norm_ref[4:5])
    sum_ref[0:1] = column_sum(grad_two)
    sum_ref[1:2] = column_sum(dy * normal)
    sum_ref[2:3] = column_sum(dy)
    sum_ref[7:8] = jnp.zeros((1, WIDTH), F32)
    low = grad_two.astype(BF)
    low_t_ref[...] = low.T
    grad_first = grad_two
    for slot in order:
        downs[slot].wait()
        grad_act = nn(low, down_held[slot].reshape(WIDTH, SLAB))
        pre_low = (grad_act * slope_ref[slot].astype(F32)).astype(BF)
        sum_ref[pl.ds(3 + parts[slot], 1), :] = column_sum(pre_low)
        stored(pre_refs, slot, pre_low)
        ups[slot].wait()
        grad_first = grad_first + nt(pre_low, up_held[slot].reshape(WIDTH, SLAB))
    grad_ref[...] = grad_first


def attention_pull_kernel(plan, count, split, place, *refs):
    grad_first_ref, packed_ref, chances_ref, normal_ref, factor_ref, norm_ref = refs[:6]
    w_refs, refs = refs[6 : 6 + count], refs[6 + count :]
    dx_ref, sum_ref, low_t_ref = refs[:3]
    packed_grad_refs = refs[3:-2]
    held, sems = refs[-2:]
    parts = part_order(place, split)
    copies = weight_copies(w_refs, plan, held, sems, parts, place)
    order = (2, 3, 0, 1) if split else (0, 1, 2, 3)
    for slot in order:
        copies[slot].start()
    normal = normal_ref[...]
    grad_first = grad_first_ref[...]
    grad_one = norm_backward(grad_first, normal, factor_ref[:, :1], norm_ref[1:2])
    sum_ref[0:1] = column_sum(grad_one)
    sum_ref[1:2] = column_sum(grad_first * normal)
    sum_ref[2:3] = column_sum(grad_first)
    sum_ref[7:8] = jnp.zeros((1, WIDTH), F32)
    low = grad_one.astype(BF)
    low_t_ref[...] = low.T
    grad_input = grad_one
    for slot in order:
        copies[slot].wait()
        grad_mix = nn(low, held[slot, :, :, :, SLAB - ROWS :].reshape(WIDTH, ROWS)).astype(BF)
        packed = packed_ref[slot]
        keys_t = packed[:, OWN : 2 * OWN].T
        grad_queries, grad_keys, grad_values = [], [], []
        for head in range(HEADS_EACH):
            queries = packed[:, head * HEAD : (head + 1) * HEAD]
            values = packed[:, 2 * OWN + head * HEAD : 2 * OWN + (head + 1) * HEAD]
            upstream = grad_mix[:, (head + 1) * HEAD : (head + 2) * HEAD]
            chances = chances_ref[slot * HEADS_EACH + head]
            grad_values.append(nn(chances, upstream).astype(BF))
            wide = chances.astype(F32)
            product = wide * nt(values, upstream)
            grad_scores = (product - wide * jnp.sum(product, 0, keepdims=True)).astype(BF)
            grad_keys.append((nn(grad_scores, queries) * 0.125).astype(BF))
            grad_queries.append(nn(keys_t[head * HEAD : (head + 1) * HEAD], grad_scores) * 0.125)
        grad_packed = jnp.concatenate(
            [jnp.concatenate(grad_queries, 0).astype(BF).T]
            + grad_keys
            + grad_values
            + [jnp.zeros((ROWS, SLAB - 3 * OWN), BF)],
            1,
        )
        sum_ref[pl.ds(3 + parts[slot], 1), :] = column_sum(grad_packed)
        stored(packed_grad_refs, slot, grad_packed)
        grad_input = grad_input + nt(grad_packed, held[slot].reshape(WIDTH, SLAB))
    dx_ref[...] = grad_input


def rows_of(refs):
    return jnp.concatenate([ref[...] for ref in refs], 1)


def rows_at(refs, slot):
    return jnp.concatenate([ref[slot] for ref in refs], 0)


def block_sends(stage, slot, targets, sems, place, y_first, base):
    width = stage.shape[-1]
    lanes = pl.ds(base, width)
    if len(targets) == 1:
        copies = [
            pltpu.make_async_copy(
                stage.at[0, 0], targets[0].at[slot, :, lanes], sems.at[0, 0]
            )
        ]
    else:
        copies = []
        for y_rel in range(2):
            first, second = (y_rel, slot) if y_first else (slot, y_rel)
            for z_rel in range(4):
                copies.append(
                    pltpu.make_async_copy(
                        stage.at[(place[3] + z_rel) & 3, place[2] ^ y_rel],
                        targets[first].at[second, z_rel, :, lanes],
                        sems.at[y_rel, z_rel],
                    )
                )
    for copy in copies:
        copy.start()
    return copies


def mlp_grad_kernel(top, split, place, *refs):
    sides = 2 if split else 1
    groups = []
    for _ in range(4):
        groups.append(refs[:sides])
        refs = refs[sides:]
    first_t_refs, pre_refs, low_t_refs, act_refs = groups
    if top:
        proj_refs, refs = refs[:sides], refs[sides:]
    up_targets, refs = refs[:sides], refs[sides:]
    down_targets, refs = refs[:sides], refs[sides:]
    stage, sems = refs[:2]
    fold = stage.shape[2:]
    slots = PARTS // sides
    sends = []
    if top:
        proj_stage, proj_sems = refs[2:]
        total = proj_refs[0][...]
        for ref in proj_refs[1:]:
            total = total + ref[...]
        proj_stage[...] = total.astype(BF).reshape(proj_stage.shape)
        for slot in range(slots):
            sends += block_sends(
                proj_stage, slot, down_targets, proj_sems.at[slot], place, True, SLAB
            )
    first_t = rows_of(first_t_refs)
    low_t = rows_of(low_t_refs)
    for slot in reversed(range(slots)):
        stage[0, slot] = nn(first_t, rows_at(pre_refs, slot)).astype(BF).reshape(*fold)
        sends += block_sends(stage.at[0, slot], slot, up_targets, sems.at[0, slot], place, False, 0)
        stage[1, slot] = nn(low_t, rows_at(act_refs, slot)).astype(BF).reshape(*fold)
        sends += block_sends(stage.at[1, slot], slot, down_targets, sems.at[1, slot], place, True, 0)
    for copy in sends:
        copy.wait()


def attention_grad_kernel(y_first, split, place, *refs):
    sides = 2 if split else 1
    groups = []
    for _ in range(4):
        groups.append(refs[:sides])
        refs = refs[sides:]
    x_t_refs, packed_refs, low_t_refs, mixture_refs = groups
    targets, refs = refs[:sides], refs[sides:]
    stage, sems = refs
    fold = stage.shape[1:]
    sends = []
    x_t = rows_of(x_t_refs)
    low_t = rows_of(low_t_refs)
    for slot in reversed(range(PARTS // sides)):
        grad_weight = nn(x_t, rows_at(packed_refs, slot))
        grad_out = nn(low_t, rows_at(mixture_refs, slot))
        stage[slot] = (
            jnp.concatenate(
                [grad_weight[:, : SLAB - ROWS], grad_weight[:, SLAB - ROWS :] + grad_out], 1
            )
            .astype(BF)
            .reshape(*fold)
        )
        sends += block_sends(stage.at[slot], slot, targets, sems.at[slot], place, y_first, 0)
    for copy in sends:
        copy.wait()


def any_spec():
    return pl.BlockSpec(memory_space=pl.ANY)


def vmem_spec():
    return pl.BlockSpec(memory_space=pltpu.VMEM)


def shaped(shape, kind):
    return jax.ShapeDtypeStruct(shape, kind)


def price(micros):
    return pl.CostEstimate(
        flops=int(micros * 1e6), bytes_accessed=int(micros * 3e3), transcendentals=0
    )


def params():
    return pltpu.CompilerParams(vmem_limit_bytes=VMEM_BYTES)


def smem_spec():
    return pl.BlockSpec(memory_space=pltpu.SMEM)


def sided(split, shape, kind):
    if split:
        return [shaped((2, *shape), kind)] * 2
    return [shaped((PARTS, *shape), kind)]


def held_scratch(fold, count):
    return [pltpu.VMEM((PARTS, *fold, SLAB), BF)] * count + [
        pltpu.SemaphoreType.DMA((PARTS, 8))
    ] * count


def projection_scratch(fold):
    return [pltpu.VMEM((*fold, DIM), BF), pltpu.SemaphoreType.DMA]


def call(kernel, name, micros, place, args, outs, scratch, in_hbm=(), out_hbm=()):
    return pl.pallas_call(
        kernel,
        out_shape=outs,
        in_specs=[smem_spec()]
        + [any_spec() if at in in_hbm else vmem_spec() for at in range(len(args))],
        out_specs=[any_spec() if at in out_hbm else vmem_spec() for at in range(len(outs))],
        scratch_shapes=scratch,
        compiler_params=params(),
        cost_estimate=price(micros),
        name=name,
    )(place, *args)


def run_attention(layer_at, place, hidden, mask, pair_rows, norms, weights, split):
    arrays, plan = weights["att"]
    outs = [
        shaped((ROWS, WIDTH), F32),
        shaped((WIDTH, ROWS), BF),
        shaped((PARTS, ROWS, HELD), BF),
        shaped((PARTS * HEADS_EACH, ROWS, ROWS), BF),
        shaped((ROWS, WIDTH), F32),
        shaped((ROWS, DIM), F32),
        shaped((WIDTH, ROWS), BF),
    ] + sided(split, (ROWS, ROWS), BF)
    args = [hidden, mask, pair_rows, norms, *arrays]
    return call(
        functools.partial(attention_kernel, plan, len(arrays), split),
        f"attention_{layer_at}",
        9,
        place,
        args,
        outs,
        held_scratch(weights["fold"], 1),
        in_hbm=range(4, len(args)),
    )


def run_mlp(layer_at, place, first, up_rows, norms, weights, split):
    top = layer_at == LAYERS - 1
    ups, up_plan = weights["up"]
    downs, down_plan = weights["down"]
    outs = [
        shaped((ROWS, WIDTH), F32),
        shaped((PARTS, ROWS, SLAB), BF),
        shaped((ROWS, WIDTH), F32),
        shaped((ROWS, DIM), F32),
    ] + sided(split, (ROWS, SLAB), BF)
    scratch = held_scratch(weights["fold"], 2)
    if top:
        outs += [
            shaped((ROWS, DIM), BF),
            shaped((ROWS, DIM), F32),
            shaped((ROWS, DIM), F32),
            shaped((WIDTH, ROWS), BF),
        ]
        scratch += projection_scratch(weights["fold"])
    args = [first, up_rows, norms, *ups, *downs]
    return call(
        functools.partial(
            mlp_kernel, up_plan, down_plan, weights.get("proj"), len(ups), top, split
        ),
        f"mlp_{layer_at}",
        9,
        place,
        args,
        outs,
        scratch,
        in_hbm=range(3, len(args)),
    )


def run_mlp_pull(layer_at, place, upstream, saved, norms, weights, split):
    top = layer_at == LAYERS - 1
    ups, up_plan = weights["up"]
    downs, down_plan = weights["down"]
    outs = [
        shaped((ROWS, WIDTH), F32),
        shaped((8, WIDTH), F32),
        shaped((WIDTH, ROWS), BF),
    ] + sided(split, (ROWS, SLAB), BF)
    scratch = held_scratch(weights["fold"], 2)
    if top:
        outs += [shaped((WIDTH, DIM), F32)]
        scratch += projection_scratch(weights["fold"])
    inputs = [*upstream, *saved, norms]
    args = [*inputs, *ups, *downs]
    return call(
        functools.partial(
            mlp_pull_kernel, up_plan, down_plan, weights.get("proj"), len(ups), top, split
        ),
        f"pull_mlp_{layer_at}",
        8,
        place,
        args,
        outs,
        scratch,
        in_hbm=range(len(inputs), len(args)),
    )


def run_attention_pull(layer_at, place, grad_first, saved, norms, weights, split):
    arrays, plan = weights["att"]
    outs = [
        shaped((ROWS, WIDTH), F32),
        shaped((8, WIDTH), F32),
        shaped((WIDTH, ROWS), BF),
    ] + sided(split, (ROWS, SLAB), BF)
    inputs = [grad_first, *saved, norms]
    args = [*inputs, *arrays]
    return call(
        functools.partial(attention_pull_kernel, plan, len(arrays), split),
        f"pull_attention_{layer_at}",
        10,
        place,
        args,
        outs,
        held_scratch(weights["fold"], 1),
        in_hbm=range(len(inputs), len(args)),
    )


def grad_shapes(split, rows_each, width):
    if split:
        return [shaped((2, 4, rows_each, width), BF)] * 2
    return [shaped((PARTS, WIDTH, width), BF)]


def run_mlp_grad(layer_at, place, groups, split, rows_each):
    top = layer_at == LAYERS - 1
    args = [value for group in groups for value in group]
    sides = 2 if split else 1
    outs = grad_shapes(split, rows_each, SLAB)
    outs += grad_shapes(split, rows_each, SLAB + (DIM if top else 0))
    fold = (4, 2, rows_each) if split else (1, 1, WIDTH)
    slots = PARTS // sides
    scratch = [
        pltpu.VMEM((2, slots, *fold, SLAB), BF),
        pltpu.SemaphoreType.DMA((2, slots, 2, 4)),
    ]
    if top:
        scratch += [pltpu.VMEM((*fold, DIM), BF), pltpu.SemaphoreType.DMA((slots, 2, 4))]
    results = call(
        functools.partial(mlp_grad_kernel, top, split),
        f"grad_mlp_{layer_at}",
        8,
        place,
        args,
        outs,
        scratch,
        out_hbm=range(len(outs)),
    )
    return results[:sides], results[sides:]


def run_attention_grad(layer_at, y_first, place, groups, split, rows_each):
    args = [value for group in groups for value in group]
    outs = grad_shapes(split, rows_each, SLAB)
    fold = (4, 2, rows_each) if split else (1, 1, WIDTH)
    slots = PARTS // (2 if split else 1)
    return call(
        functools.partial(attention_grad_kernel, y_first, split),
        f"grad_attention_{layer_at}",
        5,
        place,
        args,
        outs,
        [pltpu.VMEM((slots, *fold, SLAB), BF), pltpu.SemaphoreType.DMA((slots, 2, 4))],
        out_hbm=range(len(outs)),
    )


CORE_SWAP = [(at, at ^ 1) for at in range(PARTS)]
X_SWAP = [(at, at ^ 2) for at in range(PARTS)]
Y_SWAP = [(at, at ^ 1) for at in range(8)]
Z_GROUPS = [[0, 2, 4, 6], [1, 3, 5, 7]]


def added(*terms):
    total = terms[0].astype(F32)
    for term in terms[1:]:
        total = total + term.astype(F32)
    return total


def over_x(value, name):
    with jax.named_scope(f"x_{name}"):
        return lax.ppermute(value, "tensor", X_SWAP)


def over_y(value, name):
    with jax.named_scope(f"y_{name}"):
        return lax.ppermute(value, "dp", Y_SWAP)


def over_core(value, name="pair"):
    with jax.named_scope(f"core_{name}"):
        return lax.ppermute(value, "tensor", CORE_SWAP)


def along_z(value, step, name):
    pairs = [(at, ((at // 2 + step) % 4) * 2 + at % 2) for at in range(8)]
    with jax.named_scope(f"z_{name}_{step}"):
        return lax.ppermute(value, "dp", pairs)


def tied(*values):
    return lax.optimization_barrier(values)


class Reduction:
    def __init__(self, name, pieces, y_first):
        self.name = name
        self.keep, self.send = pieces
        self.first, self.second = (over_y, over_x) if y_first else (over_x, over_y)

    def start(self):
        self.one = self.first(self.send, self.name + "_first")

    def add_second(self):
        with jax.named_scope(f"add_{self.name}_second"):
            self.terms = added(self.keep[1], self.one[1]).astype(BF)

    def start_second(self):
        self.two = self.second(self.terms, self.name + "_second")

    def add_third(self):
        with jax.named_scope(f"add_{self.name}_third"):
            self.blocks = [
                added(self.keep[0, step], self.one[0, step], self.two[step]).astype(BF)
                for step in range(1, 4)
            ]

    def start_third(self):
        self.arrived = [
            along_z(block, step + 1, self.name) for step, block in enumerate(self.blocks)
        ]

    def total(self):
        with jax.named_scope(f"add_{self.name}_last"):
            return added(self.keep[0, 0], self.one[0, 0], self.two[0], *self.arrived)


def reduce_whole(grads, devices):
    grads = grads.reshape(PARTS, devices, WIDTH // devices, -1)
    grads = jnp.transpose(grads, (1, 0, 2, 3)).reshape(devices * PARTS, WIDTH // devices, -1)
    return lax.psum_scatter(grads, BOTH, scatter_dimension=0, tiled=True)[0].astype(F32)


def total_over_all(value, split):
    if not split:
        return lax.psum(value, BOTH)
    value = value + over_core(value)
    value = value + over_x(value, "sums")
    value = value + over_y(value, "sums")
    value = value + lax.ppermute(value, "dp", [(at, at ^ 2) for at in range(8)])
    return value + lax.ppermute(value, "dp", [(at, at ^ 4) for at in range(8)])


def score_kernel(count, lengths_ref, log_ref, queries_ref, passages_ref, powers_ref, sums_ref, logit_ref):
    queries = queries_ref[...]

    def single(at, carry):
        similar = nt(passages_ref[at], queries)
        spot = lax.broadcasted_iota(jnp.int32, (PLEN, ROWS), 0)
        powers = jnp.where(spot < lengths_ref[at], jnp.exp(SHARPNESS * similar), 0.0)
        powers_ref[at] = powers.astype(BF)
        sums_ref[pl.ds(at, 1), :] = jnp.sum(powers, 0, keepdims=True)
        return carry

    lax.fori_loop(0, count, single, 0)
    smooth = (jnp.log(sums_ref[...]) - log_ref[...]) / SHARPNESS
    token = lax.broadcasted_iota(jnp.int32, (ROWS, DIM), 0) // QLEN
    query = lax.broadcasted_iota(jnp.int32, (ROWS, DIM), 1)
    pick = (token == query).astype(F32)
    logit_ref[...] = SCORE_SCALE * jnp.dot(
        smooth, pick, precision=lax.Precision.HIGHEST, preferred_element_type=F32
    )


def pull_kernel(count, powers_ref, steer_ref, queries_ref, passages_ref, passage_out, query_out, total):
    queries = queries_ref[...]
    total[...] = jnp.zeros_like(total)

    def single(at, carry):
        shares = (powers_ref[at].astype(F32) * steer_ref[pl.ds(at, 1), :]).astype(BF)
        passage_out[at] = nn(shares, queries).astype(BF)
        total[...] += nn(passages_ref[at].T, shares)
        return carry

    lax.fori_loop(0, count, single, 0)
    query_out[...] = total[...].T


def scores_of(queries, passages, lengths):
    count = passages.shape[0]
    return pl.pallas_call(
        functools.partial(score_kernel, count),
        out_shape=[
            shaped((count, PLEN, ROWS), BF),
            shaped((count, ROWS), F32),
            shaped((count, DIM), F32),
        ],
        in_specs=[pl.BlockSpec(memory_space=pltpu.SMEM)] + [vmem_spec()] * 3,
        out_specs=[vmem_spec()] * 3,
        compiler_params=params(),
        cost_estimate=price(4),
        name="scores",
    )(lengths, jnp.log(lengths.astype(F32))[:, None], queries, passages)


def pulls_of(powers, steer, queries, passages):
    count = passages.shape[0]
    return pl.pallas_call(
        functools.partial(pull_kernel, count),
        out_shape=[shaped((count, PLEN, DIM), BF), shaped((ROWS, DIM), F32)],
        in_specs=[vmem_spec()] * 4,
        out_specs=[vmem_spec()] * 2,
        scratch_shapes=[pltpu.VMEM((DIM, ROWS), F32)],
        compiler_params=params(),
        cost_estimate=price(4),
        name="score_pulls",
    )(powers, steer, queries, passages)


def adam_step(master, moment, second, gradient, decay):
    moment_new = BETA_ONE * moment + (1.0 - BETA_ONE) * gradient
    second_new = BETA_TWO * second + (1.0 - BETA_TWO) * gradient * gradient
    rising = moment_new / (1.0 - BETA_ONE**STEP)
    spread = jnp.sqrt(second_new / (1.0 - BETA_TWO**STEP))
    return (moment_new, second_new, -LEARN_RATE * (rising / (spread + ADAM_EPS) + decay * master))


def joined(*pieces):
    return jnp.concatenate([piece.astype(BF) for piece in pieces], 1)


def attention_shard(qkv, out):
    return joined(qkv[0], qkv[1], qkv[2], out.T)


class Gathering:
    def __init__(self, name, shard, x_last):
        self.name = name
        self.shard = shard
        self.plan = ("x_last" if x_last else "y_last", 0)
        self.first, self.second = (over_y, over_x) if x_last else (over_x, over_y)

    def column(self):
        arrived = [along_z(self.shard, step, self.name) for step in range(1, 4)]
        self.held = jnp.stack([self.shard, *arrived])

    def plane(self):
        self.held = jnp.stack([self.held, self.first(self.held, self.name + "_first")])

    def cross(self):
        self.other = self.second(self.held, self.name + "_second")

    def all(self):
        pairs = [over_core(self.held, self.name), over_core(self.other, self.name)]
        return [self.held, self.other, *pairs], self.plan


def gather_whole(shard, devices):
    rows_each = shard.shape[0]
    value = lax.all_gather(shard, BOTH, axis=0, tiled=False)
    if devices == 8:
        return value.reshape(4, 2, PARTS, rows_each, -1)
    value = value.reshape(devices, PARTS, rows_each, -1)
    return jnp.transpose(value, (1, 0, 2, 3)).reshape(1, 1, PARTS, WIDTH, -1)


def whole_weights(value):
    return {
        "att": ([value], ("whole", 0)),
        "up": ([value], ("whole", SLAB)),
        "down": ([value], ("whole", 2 * SLAB)),
        "proj": PACK,
    }


def unpack_grads(att_list, up_list, down_list):
    qkv = jnp.stack(
        [
            jnp.stack([att[:, kind * OWN : (kind + 1) * OWN] for kind in range(3)])
            for att in att_list
        ]
    )
    out = jnp.stack([att[:, 3 * OWN :].T for att in att_list])
    return qkv, out, jnp.stack(up_list), jnp.stack([down[:, :SLAB].T for down in down_list])


def to_output_rows(grad, tensor_at):
    rows = PDEV * PLEN // PARTS
    query_rows = QDEV * QLEN // PARTS
    start = jnp.where(tensor_at == PARTS - 1, 0, ROWS - rows)
    step = lax.ppermute(
        lax.dynamic_slice_in_dim(grad, start, rows, 0),
        "tensor",
        [(at, (at + 1) % PARTS) for at in range(PARTS)],
    )
    last = PARTS - 1
    one = lax.ppermute(grad[query_rows : 2 * query_rows], "tensor", [(last, 1)])
    two = lax.ppermute(grad[2 * query_rows : 3 * query_rows], "tensor", [(last, 2)])
    own = grad[last * query_rows :]
    query = jnp.where(
        tensor_at == 0,
        step[:query_rows],
        jnp.where(tensor_at == 1, one, jnp.where(tensor_at == 2, two, own)),
    )
    unit = query_rows
    passage = jnp.where(
        tensor_at == 0,
        grad[:rows],
        jnp.where(
            tensor_at == 1,
            jnp.concatenate([step[2 * unit :], grad[: 2 * unit]]),
            jnp.where(tensor_at == 2, jnp.concatenate([step[unit:], grad[:unit]]), step),
        ),
    )
    return query, passage


def body(
    query_tokens,
    passage_tokens,
    query_mask,
    passage_lengths,
    positives,
    qkv_weight,
    qkv_moment,
    qkv_second,
    out_weight,
    out_moment,
    out_second,
    up_weight,
    up_moment,
    up_second,
    down_weight,
    down_moment,
    down_second,
    projection,
    projection_moment,
    projection_second,
    bias_pair,
    bias_pair_moment,
    bias_pair_second,
    bias_up,
    bias_up_moment,
    bias_up_second,
    norm_terms,
    norm_terms_moment,
    norm_terms_second,
):
    devices = lax.axis_size("dp")
    dev_index = lax.axis_index("dp")
    tensor_at = lax.axis_index("tensor")
    last = PARTS - 1
    is_query = tensor_at == last
    rows_each = WIDTH // devices
    split = devices == 8
    pair_own = jnp.concatenate(
        [
            bias_pair[:, 0],
            jnp.zeros((LAYERS, OWN), F32),
            bias_pair[:, 1],
            jnp.zeros((LAYERS, HELD - 3 * OWN), F32),
        ],
        -1,
    )
    small = jnp.concatenate([pair_own, bias_up], -1)
    if split:
        crossed = over_x(small, "biases")
        small_all = [small, crossed, over_core(small, "biases"), over_core(crossed, "biases")]
        small_all = jnp.stack(small_all)
    else:
        small_all = lax.all_gather(small, "tensor", axis=0, tiled=False)

    shards = [
        (
            attention_shard(qkv_weight[at], out_weight[at]),
            up_weight[at].astype(BF),
            down_weight[at].T.astype(BF),
        )
        for at in range(LAYERS)
    ]
    if split:
        last_layer = whole_weights(gather_whole(joined(*shards[1], projection), devices))
        att = Gathering("att_0", shards[0][0], True)
        up = Gathering("up_0", shards[0][1], False)
        down = Gathering("down_0", shards[0][2], True)
        att.column()
        att.held, up.shard, down.shard, small_all = tied(
            att.held, up.shard, down.shard, small_all
        )
        att.plane()
        up.column()
        down.column()
        up.plane()
        down.plane()
        att.cross()
        up.cross()
        down.cross()
        first_layer = {"att": att.all()}
    else:
        first_layer = whole_weights(gather_whole(joined(*shards[0]), devices))
        last_layer = whole_weights(gather_whole(joined(*shards[1], projection), devices))
    weights = [first_layer, last_layer]
    for layer in weights:
        layer["fold"] = (4, 2, rows_each) if split else (1, 1, WIDTH)
    pair_rows = small_all[:, :, None, :HELD]
    up_all = small_all[:, :, None, HELD:]
    passage_at = jnp.minimum(tensor_at, last - 1)
    own_passage = lax.dynamic_slice_in_dim(passage_tokens, passage_at * PLEN, PLEN, 0)
    hidden = jnp.where(is_query, query_tokens, own_passage)
    own_length = lax.dynamic_slice_in_dim(passage_lengths, dev_index * PDEV + passage_at, 1, 0)
    spot = jnp.arange(ROWS, dtype=jnp.int32)
    key_valid = jnp.where(is_query, query_mask.reshape(ROWS) == 1, spot < own_length)
    together = jnp.logical_or(
        jnp.logical_not(is_query), spot[:, None] // QLEN == spot[None, :] // QLEN
    )
    mask = jnp.where(jnp.logical_and(key_valid[:, None], together), 0.0, MASKED).astype(F32)

    place = jnp.stack([tensor_at // 2, tensor_at % 2, dev_index % 2, dev_index // 2]).astype(jnp.int32)

    def sides_of(keep, send):
        return [keep, over_core(send)] if split else [keep]

    def shared(value):
        return [value, over_core(value)] if split else [value]

    saved_list = []
    for layer_at in range(LAYERS):
        outs = run_attention(
            layer_at,
            place,
            hidden,
            mask,
            pair_rows[:, layer_at],
            norm_terms[layer_at],
            weights[layer_at],
            split,
        )
        first, x_t, packed, chances, normal_one, factor_one, first_t = outs[:7]
        if split and layer_at == 0:
            first, up.held, up.other, down.held, down.other = tied(
                first, up.held, up.other, down.held, down.other
            )
            weights[0].update(up=up.all(), down=down.all())
        mixtures = sides_of(outs[7], outs[-1])
        outs = run_mlp(
            layer_at, place, first, up_all[:, layer_at], norm_terms[layer_at], weights[layer_at], split
        )
        hidden, slope, normal_two, factor_two = outs[:4]
        acts = sides_of(outs[4], outs[5 if split else 4])
        saved_list.append(
            dict(
                mlp=(slope, normal_two, factor_two),
                attention=(packed, chances, normal_one, factor_one),
                x_t=shared(x_t),
                first_t=shared(first_t),
                mixtures=mixtures,
                acts=acts,
            )
        )
    embedding, unit, scale, top_t = outs[-4:]

    passages = lax.all_to_all(
        jnp.broadcast_to(embedding[None], (devices, ROWS, DIM)), "dp", 0, 0, tiled=True
    )
    queries = embedding
    arrived = [lax.ppermute(embedding, "tensor", [(last, at)]) for at in range(last)]
    for at in range(last):
        queries = jnp.where(tensor_at == at, arrived[at], queries)
    length_table = passage_lengths.reshape(devices, PDEV)
    own_lengths = lax.dynamic_slice_in_dim(length_table, passage_at, 1, 1)[:, 0]
    powers, sums, logit_part = scores_of(queries, passages, own_lengths)
    logits = lax.all_gather(logit_part[:, :QDEV], "tensor", axis=0, tiled=False)[:last]
    own_positives = lax.dynamic_slice_in_dim(positives, dev_index * QDEV, QDEV, 0)
    ids = (
        lax.broadcasted_iota(jnp.int32, logits.shape, 1) * PDEV
        + lax.broadcasted_iota(jnp.int32, logits.shape, 0)
    )
    chosen = ids == own_positives[None, None, :]
    highest = jnp.max(logits, (0, 1), keepdims=True)
    raised = jnp.exp(logits - highest)
    summed = jnp.sum(raised, (0, 1), keepdims=True)
    losses = highest + jnp.log(summed) - jnp.sum(jnp.where(chosen, logits, 0.0), (0, 1), keepdims=True)
    deltas = raised / summed - chosen.astype(F32)
    own_deltas = lax.dynamic_slice_in_dim(deltas, passage_at, 1, 0)[0]
    steer = jnp.where(is_query, 0.0, SCORE_SCALE) * jnp.repeat(own_deltas, QLEN, axis=1) / sums
    passage_terms, query_terms = pulls_of(powers, steer, queries, passages)
    passage_back = lax.all_to_all(passage_terms, "dp", 0, 0, tiled=True)
    grad_passage = jnp.sum(passage_back.astype(F32), 0)
    returned = [lax.ppermute(query_terms, "tensor", [(at, last)]) for at in range(last)]
    grad_query = returned[0] + returned[1] + returned[2]
    grad_emb = jnp.where(is_query, grad_query, grad_passage)

    upstream = (grad_emb, unit, scale, top_t)
    mlp_sums, attention_sums = [None] * LAYERS, [None] * LAYERS

    def mlp_pull(layer_at, upstream):
        saved = saved_list[layer_at]
        outs = run_mlp_pull(
            layer_at, place, upstream, saved["mlp"], norm_terms[layer_at], weights[layer_at], split
        )
        grad_first, mlp_sums[layer_at], low_t = outs[:3]
        groups = [
            saved["first_t"],
            sides_of(outs[3], outs[4 if split else 3]),
            shared(low_t),
            saved["acts"],
        ]
        if layer_at == LAYERS - 1:
            groups.append(shared(outs[-1]))
        return grad_first, groups

    def attention_pull(layer_at, grad_first):
        saved = saved_list[layer_at]
        outs = run_attention_pull(
            layer_at,
            place,
            grad_first,
            saved["attention"],
            norm_terms[layer_at],
            weights[layer_at],
            split,
        )
        dx, attention_sums[layer_at], low_t = outs[:3]
        return dx, [
            saved["x_t"],
            sides_of(outs[3], outs[-1]),
            shared(low_t),
            saved["mixtures"],
        ]

    def mlp_grad(layer_at, groups):
        return run_mlp_grad(layer_at, place, groups, split, rows_each)

    def attention_grad(layer_at, y_first, groups):
        return run_attention_grad(layer_at, y_first, place, groups, split, rows_each)

    if split:
        grad_first, mlp_groups = mlp_pull(1, upstream)
        up_grads, down_grads = mlp_grad(1, mlp_groups)
        up_one, down_one = Reduction("up_1", up_grads, False), Reduction("down_1", down_grads, True)
        grad_first, up_one.send, down_one.send = tied(grad_first, up_one.send, down_one.send)
        up_one.start()
        down_one.start()
        dx, att_groups = attention_pull(1, grad_first)
        att_one = Reduction("att_1", attention_grad(1, False, att_groups), False)
        dx, att_one.send = tied(dx, att_one.send)
        att_one.start()
        grad_first, mlp_groups = mlp_pull(0, (dx,))
        up_one.add_second()
        down_one.add_second()
        mlp_groups[0][0], up_one.terms, down_one.terms = tied(
            mlp_groups[0][0], up_one.terms, down_one.terms
        )
        up_one.start_second()
        down_one.start_second()
        up_grads, down_grads = mlp_grad(0, mlp_groups)
        up_zero = Reduction("up_0", up_grads, False)
        down_zero = Reduction("down_0", down_grads, True)
        grad_first, up_zero.send, down_zero.send = tied(grad_first, up_zero.send, down_zero.send)
        up_zero.start()
        down_zero.start()
        dx, att_groups = attention_pull(0, grad_first)
        att_one.add_second()
        att_groups[0][0], att_one.terms = tied(att_groups[0][0], att_one.terms)
        att_one.start_second()
        up_one.add_third()
        down_one.add_third()
        up_zero.add_second()
        down_zero.add_second()
        att_groups[0][0], up_zero.terms, down_zero.terms = tied(
            att_groups[0][0], up_zero.terms, down_zero.terms
        )
        att_zero = Reduction("att_0", attention_grad(0, True, att_groups), True)
        att_zero.start()
        att_one.add_third()
        att_zero.add_second()
        for item in (up_one, down_one, att_one):
            item.start_third()
        for item in (up_zero, down_zero, att_zero):
            item.start_second()
        for item in (up_zero, down_zero, att_zero):
            item.add_third()
            item.start_third()
        attention_sums[0] = tied(attention_sums[0], att_zero.terms)[0]
        att_list = [att_zero.total(), att_one.total()]
        up_list = [up_zero.total(), up_one.total()]
        down_list = [down_zero.total(), down_one.total()]
    else:
        att_list, up_list, down_list = [], [], []
        dx = None
        for layer_at in range(LAYERS - 1, -1, -1):
            grad_first, groups = mlp_pull(layer_at, (dx,) if upstream is None else upstream)
            upstream = None
            up_grads, down_grads = mlp_grad(layer_at, groups)
            dx, groups = attention_pull(layer_at, grad_first)
            att_grads = attention_grad(layer_at, False, groups)
            up_list.insert(0, reduce_whole(up_grads[0], devices))
            down_list.insert(0, reduce_whole(down_grads[0], devices))
            att_list.insert(0, reduce_whole(att_grads[0], devices))
    loss_part = jnp.where(tensor_at == 0, jnp.sum(losses), 0.0)
    sums = jnp.stack([attention_sums[0], mlp_sums[0], attention_sums[1], mlp_sums[1]])
    row_ids = lax.broadcasted_iota(jnp.int32, sums.shape, 1)
    sums = sums + jnp.where(row_ids == 7, loss_part, 0.0)
    sums = total_over_all(sums, split).reshape(LAYERS, 2, 8, WIDTH)
    norms_grad = sums[:, :, :3].reshape(LAYERS, 6, WIDTH)
    own_sums = lax.dynamic_slice_in_dim(sums, 3 + tensor_at, 1, 2)[:, :, 0]
    pair_grad = jnp.stack([own_sums[:, 0, :OWN], own_sums[:, 0, 2 * OWN : 3 * OWN]], 1)
    bias_grad = own_sums[:, 1]
    loss_mean = sums[0, 0, 7, 0] / (QDEV * devices)
    projection_grad = down_list[LAYERS - 1][:, SLAB:]
    qkv_grad, out_grad, up_grad, down_grad = unpack_grads(att_list, up_list, down_list)
    qkv_m, qkv_v, qkv_u = adam_step(qkv_weight, qkv_moment, qkv_second, qkv_grad, WEIGHT_DECAY)
    out_m, out_v, out_u = adam_step(out_weight, out_moment, out_second, out_grad, WEIGHT_DECAY)
    up_m, up_v, up_u = adam_step(up_weight, up_moment, up_second, up_grad, WEIGHT_DECAY)
    down_m, down_v, down_u = adam_step(
        down_weight, down_moment, down_second, down_grad, WEIGHT_DECAY
    )
    proj_m, proj_v, proj_u = adam_step(
        projection, projection_moment, projection_second, projection_grad, WEIGHT_DECAY
    )
    pair_m, pair_v, pair_u = adam_step(
        bias_pair, bias_pair_moment, bias_pair_second, pair_grad, 0.0
    )
    bias_m, bias_v, bias_u = adam_step(bias_up, bias_up_moment, bias_up_second, bias_grad, 0.0)
    norm_m, norm_v, norm_u = adam_step(
        norm_terms, norm_terms_moment, norm_terms_second, norms_grad, 0.0
    )
    query_grad, passage_grad = to_output_rows(dx, tensor_at)
    return (
        loss_mean,
        query_grad,
        passage_grad,
        qkv_grad,
        qkv_m,
        qkv_v,
        qkv_u,
        out_grad,
        out_m,
        out_v,
        out_u,
        up_grad,
        up_m,
        up_v,
        up_u,
        down_grad,
        down_m,
        down_v,
        down_u,
        projection_grad,
        proj_m,
        proj_v,
        proj_u,
        pair_grad,
        pair_m,
        pair_v,
        pair_u,
        bias_grad,
        bias_m,
        bias_v,
        bias_u,
        norms_grad,
        norm_m,
        norm_v,
        norm_u,
    )


def solution(mesh):
    placed = (
        P("dp", None),
        P("dp", None),
        P("dp", None),
        P(),
        P(),
        P(None, None, "dp", "tensor"),
        P(None, None, "dp", "tensor"),
        P(None, None, "dp", "tensor"),
        P(None, "tensor", "dp"),
        P(None, "tensor", "dp"),
        P(None, "tensor", "dp"),
        P(None, "dp", "tensor"),
        P(None, "dp", "tensor"),
        P(None, "dp", "tensor"),
        P(None, "tensor", "dp"),
        P(None, "tensor", "dp"),
        P(None, "tensor", "dp"),
        P("dp", None),
        P("dp", None),
        P("dp", None),
        P(None, None, "tensor"),
        P(None, None, "tensor"),
        P(None, None, "tensor"),
        P(None, "tensor"),
        P(None, "tensor"),
        P(None, "tensor"),
        P(),
        P(),
        P(),
    )
    return jax.shard_map(
        body,
        mesh=mesh,
        in_specs=placed,
        out_specs=(
            P(),
            P(("dp", "tensor"), None),
            P(("dp", "tensor"), None),
            P(None, None, "dp", "tensor"),
            P(None, None, "dp", "tensor"),
            P(None, None, "dp", "tensor"),
            P(None, None, "dp", "tensor"),
            P(None, "tensor", "dp"),
            P(None, "tensor", "dp"),
            P(None, "tensor", "dp"),
            P(None, "tensor", "dp"),
            P(None, "dp", "tensor"),
            P(None, "dp", "tensor"),
            P(None, "dp", "tensor"),
            P(None, "dp", "tensor"),
            P(None, "tensor", "dp"),
            P(None, "tensor", "dp"),
            P(None, "tensor", "dp"),
            P(None, "tensor", "dp"),
            P("dp", None),
            P("dp", None),
            P("dp", None),
            P("dp", None),
            P(None, None, "tensor"),
            P(None, None, "tensor"),
            P(None, None, "tensor"),
            P(None, None, "tensor"),
            P(None, "tensor"),
            P(None, "tensor"),
            P(None, "tensor"),
            P(None, "tensor"),
            P(),
            P(),
            P(),
            P(),
        ),
        check_vma=False,
    )
```

```python
import functools

import jax
import jax.numpy as jnp
from jax import lax
from jax.experimental import pallas as pl
from jax.experimental.pallas import tpu as pltpu
from jax.sharding import PartitionSpec as P

WIDTH = 768
HEAD = 64
DIM = 128
QLEN = 32
PLEN = 256
LAYERS = 2
STEP = 10
QDEV = 8
PDEV = 3
ROWS = 256
PARTS = 4
HEADS_EACH = 3
OWN = HEADS_EACH * HEAD
SLAB = 768
HELD = 640
PACK = 3 * SLAB

MASKED = -1e30
SHARPNESS = 24.0
SCORE_SCALE = 4.0
LN_EPS = 1e-12
NORM_EPS = 1e-12
BETA_ONE = 0.9
BETA_TWO = 0.999
ADAM_EPS = 1e-08
LEARN_RATE = 0.02
WEIGHT_DECAY = 0.01
VMEM_BYTES = 60 * 1024 * 1024

BF = jnp.bfloat16
F32 = jnp.float32
BOTH = ("dp", "tensor")


def nn(left, right):
    return jnp.dot(left, right, preferred_element_type=F32)


def nt(left, right):
    return lax.dot_general(left, right, (((1,), (1,)), ((), ())), preferred_element_type=F32)


def norm_forward(values):
    average = jnp.mean(values, -1, keepdims=True)
    centred = values - average
    factor = lax.rsqrt(jnp.mean(centred * centred, -1, keepdims=True) + LN_EPS)
    return centred * factor, factor


def norm_backward(upstream, normal, factor, gains):
    scaled = upstream * gains
    average = jnp.mean(scaled, -1, keepdims=True)
    cross = jnp.mean(scaled * normal, -1, keepdims=True)
    return factor * (scaled - average - normal * cross)


def column_sum(values):
    return jnp.sum(values.astype(F32), 0, keepdims=True)


def part_order(place, split):
    if not split:
        return list(range(PARTS))
    x_at, c_at = place[0], place[1]
    return [
        (x_at ^ x_rel) * 2 + (c_at ^ c_rel) for c_rel in range(2) for x_rel in range(2)
    ]


class Copies:
    def __init__(self, copies):
        self.copies = copies

    def start(self):
        for copy in self.copies:
            copy.start()

    def wait(self):
        for copy in self.copies:
            copy.wait()


def weight_copies(refs, plan, held, sems, parts, place):
    kind, base = plan
    groups = []
    for slot, part in enumerate(parts):
        copies = []
        if kind == "whole":
            source = refs[0].at[:, :, part, :, pl.ds(base, SLAB)]
            copies.append(pltpu.make_async_copy(source, held.at[slot], sems.at[slot, 0]))
        else:
            c_rel, x_rel = divmod(slot, 2)
            for y_rel in range(2):
                outer, inner = (x_rel, y_rel) if kind == "x_last" else (y_rel, x_rel)
                for back in range(4):
                    copies.append(
                        pltpu.make_async_copy(
                            refs[2 * c_rel + outer].at[inner, back],
                            held.at[slot, (place[3] - back) & 3, place[2] ^ y_rel],
                            sems.at[slot, 4 * y_rel + back],
                        )
                    )
        groups.append(Copies(copies))
    return groups


def projection_copy(w_ref, proj, sem, base):
    return pltpu.make_async_copy(w_ref.at[:, :, 0, :, pl.ds(base, DIM)], proj, sem)


def stored(refs, slot, value):
    refs[slot // 2 if len(refs) > 1 else 0][slot % 2 if len(refs) > 1 else slot] = value


def attention_kernel(plan, count, split, place, *refs):
    x_ref, mask_ref, pair_ref, norm_ref = refs[:4]
    w_refs, refs = refs[4 : 4 + count], refs[4 + count :]
    first_ref, low_t_ref, packed_ref, chances_ref, normal_ref, factor_ref, first_t_ref = refs[:7]
    mixture_refs = refs[7:-2]
    held, sems = refs[-2:]
    parts = part_order(place, split)
    copies = weight_copies(w_refs, plan, held, sems, parts, place)
    for copy in copies:
        copy.start()
    hidden = x_ref[...]
    low = hidden.astype(BF)
    low_t_ref[...] = low.T
    mask = mask_ref[...]
    attended = jnp.zeros((ROWS, WIDTH), F32)
    for slot in range(PARTS):
        copies[slot].wait()
        weight = held[slot, :, :, :, :HELD].reshape(WIDTH, HELD)
        packed = (nn(low, weight) + pair_ref[slot]).astype(BF)
        packed_ref[slot] = packed
        values_t = packed[:, 2 * OWN : 3 * OWN].T
        mixed = [jnp.zeros((HEAD, ROWS), F32)]
        for head in range(HEADS_EACH):
            queries = packed[:, head * HEAD : (head + 1) * HEAD]
            keys = packed[:, OWN + head * HEAD : OWN + (head + 1) * HEAD]
            scores = nt(keys, queries) * 0.125 + mask
            powers = jnp.exp(scores - jnp.max(scores, 0, keepdims=True))
            chances = (powers * (1.0 / jnp.sum(powers, 0, keepdims=True))).astype(BF)
            chances_ref[slot * HEADS_EACH + head] = chances
            mixed.append(nn(values_t[head * HEAD : (head + 1) * HEAD], chances))
        mixture = jnp.concatenate(mixed, 0).astype(BF).T
        stored(mixture_refs, slot, mixture)
        attended = attended + nt(
            mixture, held[slot, :, :, :, SLAB - ROWS :].reshape(WIDTH, ROWS)
        )
    normal, factor = norm_forward(hidden + attended + norm_ref[0:1])
    normal_ref[...] = normal
    factor_ref[...] = jnp.broadcast_to(factor, factor_ref.shape)
    first = normal * norm_ref[1:2] + norm_ref[2:3]
    first_ref[...] = first
    first_t_ref[...] = first.astype(BF).T


def mlp_kernel(up_plan, down_plan, proj_base, count, top, split, place, *refs):
    first_ref, up_bias_ref, norm_ref = refs[:3]
    up_refs, down_refs = refs[3 : 3 + count], refs[3 + count : 3 + 2 * count]
    refs = refs[3 + 2 * count :]
    out_ref, slope_ref, normal_ref, factor_ref = refs[:4]
    act_refs = refs[4 : 6 if split else 5]
    refs = refs[4 + len(act_refs) :]
    if top:
        emb_ref, unit_ref, scale_ref, top_t_ref = refs[:4]
        refs = refs[4:]
    up_held, down_held, up_sems, down_sems = refs[:4]
    parts = part_order(place, split)
    ups = weight_copies(up_refs, up_plan, up_held, up_sems, parts, place)
    downs = weight_copies(down_refs, down_plan, down_held, down_sems, parts, place)
    for slot in range(PARTS):
        ups[slot].start()
        downs[slot].start()
    if top:
        proj, proj_sem = refs[4:]
        proj_load = projection_copy(up_refs[0], proj, proj_sem, proj_base)
        proj_load.start()
    first = first_ref[...]
    first_low = first.astype(BF)
    spread = jnp.zeros((ROWS, WIDTH), F32)
    for slot in range(PARTS):
        ups[slot].wait()
        pre_act = nn(first_low, up_held[slot].reshape(WIDTH, SLAB)) + up_bias_ref[slot]
        chance = 0.5 * (1.0 + lax.erf(pre_act * 0.7071067811865476))
        act = (pre_act * chance).astype(BF)
        stored(act_refs, slot, act)
        slope_ref[slot] = (
            chance + pre_act * jnp.exp(-0.5 * pre_act * pre_act) * 0.3989422804014327
        ).astype(BF)
        downs[slot].wait()
        spread = spread + nt(act, down_held[slot].reshape(WIDTH, SLAB))
    normal, factor = norm_forward(first + spread + norm_ref[3:4])
    normal_ref[...] = normal
    factor_ref[...] = jnp.broadcast_to(factor, factor_ref.shape)
    second = normal * norm_ref[4:5] + norm_ref[5:6]
    out_ref[...] = second
    if top:
        second_low = second.astype(BF)
        top_t_ref[...] = second_low.T
        proj_load.wait()
        embedded = nn(second_low, proj[...].reshape(WIDTH, DIM))
        scale = lax.rsqrt(jnp.sum(embedded * embedded, -1, keepdims=True) + NORM_EPS)
        unit = embedded * scale
        unit_ref[...] = unit
        emb_ref[...] = unit.astype(BF)
        scale_ref[...] = jnp.broadcast_to(scale, scale_ref.shape)


def mlp_pull_kernel(up_plan, down_plan, proj_base, count, top, split, place, *refs):
    if top:
        grad_emb_ref, unit_ref, scale_ref, top_t_ref = refs[:4]
        refs = refs[4:]
    else:
        dy_ref = refs[0]
        refs = refs[1:]
    slope_ref, normal_ref, factor_ref, norm_ref = refs[:4]
    up_refs, down_refs = refs[4 : 4 + count], refs[4 + count : 4 + 2 * count]
    refs = refs[4 + 2 * count :]
    grad_ref, sum_ref, low_t_ref = refs[:3]
    pre_refs = refs[3 : 5 if split else 4]
    refs = refs[3 + len(pre_refs) :]
    if top:
        proj_grad_ref = refs[0]
        refs = refs[1:]
    up_held, down_held, up_sems, down_sems = refs[:4]
    parts = part_order(place, split)
    ups = weight_copies(up_refs, up_plan, up_held, up_sems, parts, place)
    downs = weight_copies(down_refs, down_plan, down_held, down_sems, parts, place)
    if top:
        proj, proj_sem = refs[4:]
        proj_load = projection_copy(up_refs[0], proj, proj_sem, proj_base)
        proj_load.start()
    order = (2, 3, 0, 1) if split else (0, 1, 2, 3)
    for slot in order:
        downs[slot].start()
        ups[slot].start()
    if top:
        grad_emb = grad_emb_ref[...]
        unit = unit_ref[...]
        low_emb = (
            scale_ref[:, :1] * (grad_emb - unit * jnp.sum(grad_emb * unit, -1, keepdims=True))
        ).astype(BF)
        proj_grad_ref[...] = nn(top_t_ref[...], low_emb)
        proj_load.wait()
        dy = nt(low_emb, proj[...].reshape(WIDTH, DIM))
    else:
        dy = dy_ref[...]
    normal = normal_ref[...]
    grad_two = norm_backward(dy, normal, factor_ref[:, :1], norm_ref[4:5])
    sum_ref[0:1] = column_sum(grad_two)
    sum_ref[1:2] = column_sum(dy * normal)
    sum_ref[2:3] = column_sum(dy)
    sum_ref[7:8] = jnp.zeros((1, WIDTH), F32)
    low = grad_two.astype(BF)
    low_t_ref[...] = low.T
    grad_first = grad_two
    for slot in order:
        downs[slot].wait()
        grad_act = nn(low, down_held[slot].reshape(WIDTH, SLAB))
        pre_low = (grad_act * slope_ref[slot].astype(F32)).astype(BF)
        sum_ref[pl.ds(3 + parts[slot], 1), :] = column_sum(pre_low)
        stored(pre_refs, slot, pre_low)
        ups[slot].wait()
        grad_first = grad_first + nt(pre_low, up_held[slot].reshape(WIDTH, SLAB))
    grad_ref[...] = grad_first


def attention_pull_kernel(plan, count, split, place, *refs):
    grad_first_ref, packed_ref, chances_ref, normal_ref, factor_ref, norm_ref = refs[:6]
    w_refs, refs = refs[6 : 6 + count], refs[6 + count :]
    dx_ref, sum_ref, low_t_ref = refs[:3]
    packed_grad_refs = refs[3:-2]
    held, sems = refs[-2:]
    parts = part_order(place, split)
    copies = weight_copies(w_refs, plan, held, sems, parts, place)
    order = (2, 3, 0, 1) if split else (0, 1, 2, 3)
    for slot in order:
        copies[slot].start()
    normal = normal_ref[...]
    grad_first = grad_first_ref[...]
    grad_one = norm_backward(grad_first, normal, factor_ref[:, :1], norm_ref[1:2])
    sum_ref[0:1] = column_sum(grad_one)
    sum_ref[1:2] = column_sum(grad_first * normal)
    sum_ref[2:3] = column_sum(grad_first)
    sum_ref[7:8] = jnp.zeros((1, WIDTH), F32)
    low = grad_one.astype(BF)
    low_t_ref[...] = low.T
    grad_input = grad_one
    for slot in order:
        copies[slot].wait()
        grad_mix = nn(low, held[slot, :, :, :, SLAB - ROWS :].reshape(WIDTH, ROWS)).astype(BF)
        packed = packed_ref[slot]
        keys_t = packed[:, OWN : 2 * OWN].T
        grad_queries, grad_keys, grad_values = [], [], []
        for head in range(HEADS_EACH):
            queries = packed[:, head * HEAD : (head + 1) * HEAD]
            values = packed[:, 2 * OWN + head * HEAD : 2 * OWN + (head + 1) * HEAD]
            upstream = grad_mix[:, (head + 1) * HEAD : (head + 2) * HEAD]
            chances = chances_ref[slot * HEADS_EACH + head]
            grad_values.append(nn(chances, upstream).astype(BF))
            wide = chances.astype(F32)
            product = wide * nt(values, upstream)
            grad_scores = (product - wide * jnp.sum(product, 0, keepdims=True)).astype(BF)
            grad_keys.append((nn(grad_scores, queries) * 0.125).astype(BF))
            grad_queries.append(nn(keys_t[head * HEAD : (head + 1) * HEAD], grad_scores) * 0.125)
        grad_packed = jnp.concatenate(
            [jnp.concatenate(grad_queries, 0).astype(BF).T]
            + grad_keys
            + grad_values
            + [jnp.zeros((ROWS, SLAB - 3 * OWN), BF)],
            1,
        )
        sum_ref[pl.ds(3 + parts[slot], 1), :] = column_sum(grad_packed)
        stored(packed_grad_refs, slot, grad_packed)
        grad_input = grad_input + nt(grad_packed, held[slot].reshape(WIDTH, SLAB))
    dx_ref[...] = grad_input


def rows_of(refs):
    return jnp.concatenate([ref[...] for ref in refs], 1)


def rows_at(refs, slot):
    return jnp.concatenate([ref[slot] for ref in refs], 0)


def block_sends(stage, slot, targets, sems, place, y_first, base, start=0, width=None):
    width = stage.shape[-1] if width is None else width
    lanes, taken = pl.ds(base, width), pl.ds(start, width)
    if len(targets) == 1:
        copies = [
            pltpu.make_async_copy(
                stage.at[0, 0, :, taken], targets[0].at[slot, :, lanes], sems.at[0, 0]
            )
        ]
    else:
        copies = []
        for y_rel in range(2):
            first, second = (y_rel, slot) if y_first else (slot, y_rel)
            for z_rel in range(4):
                copies.append(
                    pltpu.make_async_copy(
                        stage.at[(place[3] + z_rel) & 3, place[2] ^ y_rel, :, taken],
                        targets[first].at[second, z_rel, :, lanes],
                        sems.at[y_rel, z_rel],
                    )
                )
    for copy in copies:
        copy.start()
    return copies


def mlp_grad_kernel(top, split, place, *refs):
    sides = 2 if split else 1
    groups = []
    for _ in range(4):
        groups.append(refs[:sides])
        refs = refs[sides:]
    first_t_refs, pre_refs, low_t_refs, act_refs = groups
    if top:
        proj_refs, refs = refs[:sides], refs[sides:]
    up_targets, refs = refs[:sides], refs[sides:]
    down_targets, refs = refs[:sides], refs[sides:]
    stage, sems = refs[:2]
    fold = stage.shape[2:]
    slots = PARTS // sides
    sends = []
    if top:
        proj_stage, proj_sems = refs[2:]
        total = proj_refs[0][...]
        for ref in proj_refs[1:]:
            total = total + ref[...]
        proj_stage[...] = total.astype(BF).reshape(proj_stage.shape)
        for slot in range(slots):
            sends += block_sends(
                proj_stage, slot, down_targets, proj_sems.at[slot], place, True, SLAB
            )
    first_t = rows_of(first_t_refs)
    low_t = rows_of(low_t_refs)
    for slot in reversed(range(slots)):
        stage[0, slot] = nn(first_t, rows_at(pre_refs, slot)).astype(BF).reshape(*fold)
        sends += block_sends(stage.at[0, slot], slot, up_targets, sems.at[0, slot], place, False, 0)
        stage[1, slot] = nn(low_t, rows_at(act_refs, slot)).astype(BF).reshape(*fold)
        sends += block_sends(stage.at[1, slot], slot, down_targets, sems.at[1, slot], place, True, 0)
    for copy in sends:
        copy.wait()


def attention_grad_kernel(cuts, split, place, *refs):
    sides = 2 if split else 1
    groups = []
    for _ in range(4):
        groups.append(refs[:sides])
        refs = refs[sides:]
    x_t_refs, packed_refs, low_t_refs, mixture_refs = groups
    targets = []
    for _ in cuts:
        targets.append(refs[:sides])
        refs = refs[sides:]
    stage, sems = refs
    fold = stage.shape[1:]
    sends = []
    x_t = rows_of(x_t_refs)
    low_t = rows_of(low_t_refs)
    for slot in reversed(range(PARTS // sides)):
        grad_weight = nn(x_t, rows_at(packed_refs, slot))
        grad_out = nn(low_t, rows_at(mixture_refs, slot))
        stage[slot] = (
            jnp.concatenate(
                [grad_weight[:, : SLAB - ROWS], grad_weight[:, SLAB - ROWS :] + grad_out], 1
            )
            .astype(BF)
            .reshape(*fold)
        )
        for at, (start, width, y_first) in enumerate(cuts):
            sends += block_sends(
                stage.at[slot], slot, targets[at], sems.at[at, slot], place, y_first, 0, start, width
            )
    for copy in sends:
        copy.wait()


def any_spec():
    return pl.BlockSpec(memory_space=pl.ANY)


def vmem_spec():
    return pl.BlockSpec(memory_space=pltpu.VMEM)


def shaped(shape, kind):
    return jax.ShapeDtypeStruct(shape, kind)


def price(micros):
    return pl.CostEstimate(
        flops=int(micros * 1e6), bytes_accessed=int(micros * 3e3), transcendentals=0
    )


def params():
    return pltpu.CompilerParams(vmem_limit_bytes=VMEM_BYTES)


def smem_spec():
    return pl.BlockSpec(memory_space=pltpu.SMEM)


def sided(split, shape, kind):
    if split:
        return [shaped((2, *shape), kind)] * 2
    return [shaped((PARTS, *shape), kind)]


def held_scratch(fold, count):
    return [pltpu.VMEM((PARTS, *fold, SLAB), BF)] * count + [
        pltpu.SemaphoreType.DMA((PARTS, 8))
    ] * count


def projection_scratch(fold):
    return [pltpu.VMEM((*fold, DIM), BF), pltpu.SemaphoreType.DMA]


def call(kernel, name, micros, place, args, outs, scratch, in_hbm=(), out_hbm=()):
    return pl.pallas_call(
        kernel,
        out_shape=outs,
        in_specs=[smem_spec()]
        + [any_spec() if at in in_hbm else vmem_spec() for at in range(len(args))],
        out_specs=[any_spec() if at in out_hbm else vmem_spec() for at in range(len(outs))],
        scratch_shapes=scratch,
        compiler_params=params(),
        cost_estimate=price(micros),
        name=name,
    )(place, *args)


def run_attention(layer_at, place, hidden, mask, pair_rows, norms, weights, split):
    arrays, plan = weights["att"]
    outs = [
        shaped((ROWS, WIDTH), F32),
        shaped((WIDTH, ROWS), BF),
        shaped((PARTS, ROWS, HELD), BF),
        shaped((PARTS * HEADS_EACH, ROWS, ROWS), BF),
        shaped((ROWS, WIDTH), F32),
        shaped((ROWS, DIM), F32),
        shaped((WIDTH, ROWS), BF),
    ] + sided(split, (ROWS, ROWS), BF)
    args = [hidden, mask, pair_rows, norms, *arrays]
    return call(
        functools.partial(attention_kernel, plan, len(arrays), split),
        f"attention_{layer_at}",
        9,
        place,
        args,
        outs,
        held_scratch(weights["fold"], 1),
        in_hbm=range(4, len(args)),
    )


def run_mlp(layer_at, place, first, up_rows, norms, weights, split):
    top = layer_at == LAYERS - 1
    ups, up_plan = weights["up"]
    downs, down_plan = weights["down"]
    outs = [
        shaped((ROWS, WIDTH), F32),
        shaped((PARTS, ROWS, SLAB), BF),
        shaped((ROWS, WIDTH), F32),
        shaped((ROWS, DIM), F32),
    ] + sided(split, (ROWS, SLAB), BF)
    scratch = held_scratch(weights["fold"], 2)
    if top:
        outs += [
            shaped((ROWS, DIM), BF),
            shaped((ROWS, DIM), F32),
            shaped((ROWS, DIM), F32),
            shaped((WIDTH, ROWS), BF),
        ]
        scratch += projection_scratch(weights["fold"])
    args = [first, up_rows, norms, *ups, *downs]
    return call(
        functools.partial(
            mlp_kernel, up_plan, down_plan, weights.get("proj"), len(ups), top, split
        ),
        f"mlp_{layer_at}",
        9,
        place,
        args,
        outs,
        scratch,
        in_hbm=range(3, len(args)),
    )


def run_mlp_pull(layer_at, place, upstream, saved, norms, weights, split):
    top = layer_at == LAYERS - 1
    ups, up_plan = weights["up"]
    downs, down_plan = weights["down"]
    outs = [
        shaped((ROWS, WIDTH), F32),
        shaped((8, WIDTH), F32),
        shaped((WIDTH, ROWS), BF),
    ] + sided(split, (ROWS, SLAB), BF)
    scratch = held_scratch(weights["fold"], 2)
    if top:
        outs += [shaped((WIDTH, DIM), F32)]
        scratch += projection_scratch(weights["fold"])
    inputs = [*upstream, *saved, norms]
    args = [*inputs, *ups, *downs]
    return call(
        functools.partial(
            mlp_pull_kernel, up_plan, down_plan, weights.get("proj"), len(ups), top, split
        ),
        f"pull_mlp_{layer_at}",
        8,
        place,
        args,
        outs,
        scratch,
        in_hbm=range(len(inputs), len(args)),
    )


def run_attention_pull(layer_at, place, grad_first, saved, norms, weights, split):
    arrays, plan = weights["att"]
    outs = [
        shaped((ROWS, WIDTH), F32),
        shaped((8, WIDTH), F32),
        shaped((WIDTH, ROWS), BF),
    ] + sided(split, (ROWS, SLAB), BF)
    inputs = [grad_first, *saved, norms]
    args = [*inputs, *arrays]
    return call(
        functools.partial(attention_pull_kernel, plan, len(arrays), split),
        f"pull_attention_{layer_at}",
        10,
        place,
        args,
        outs,
        held_scratch(weights["fold"], 1),
        in_hbm=range(len(inputs), len(args)),
    )


def grad_shapes(split, rows_each, width):
    if split:
        return [shaped((2, 4, rows_each, width), BF)] * 2
    return [shaped((PARTS, WIDTH, width), BF)]


def run_mlp_grad(layer_at, place, groups, split, rows_each):
    top = layer_at == LAYERS - 1
    args = [value for group in groups for value in group]
    sides = 2 if split else 1
    outs = grad_shapes(split, rows_each, SLAB)
    outs += grad_shapes(split, rows_each, SLAB + (DIM if top else 0))
    fold = (4, 2, rows_each) if split else (1, 1, WIDTH)
    slots = PARTS // sides
    scratch = [
        pltpu.VMEM((2, slots, *fold, SLAB), BF),
        pltpu.SemaphoreType.DMA((2, slots, 2, 4)),
    ]
    if top:
        scratch += [pltpu.VMEM((*fold, DIM), BF), pltpu.SemaphoreType.DMA((slots, 2, 4))]
    results = call(
        functools.partial(mlp_grad_kernel, top, split),
        f"grad_mlp_{layer_at}",
        8,
        place,
        args,
        outs,
        scratch,
        out_hbm=range(len(outs)),
    )
    return results[:sides], results[sides:]


def run_attention_grad(layer_at, cuts, place, groups, split, rows_each):
    args = [value for group in groups for value in group]
    sides = 2 if split else 1
    outs = []
    for _, width, _ in cuts:
        outs += grad_shapes(split, rows_each, width)
    fold = (4, 2, rows_each) if split else (1, 1, WIDTH)
    slots = PARTS // sides
    results = call(
        functools.partial(attention_grad_kernel, cuts, split),
        f"grad_attention_{layer_at}",
        5,
        place,
        args,
        outs,
        [
            pltpu.VMEM((slots, *fold, SLAB), BF),
            pltpu.SemaphoreType.DMA((len(cuts), slots, 2, 4)),
        ],
        out_hbm=range(len(outs)),
    )
    return [results[sides * at : sides * (at + 1)] for at in range(len(cuts))]


CORE_SWAP = [(at, at ^ 1) for at in range(PARTS)]
X_SWAP = [(at, at ^ 2) for at in range(PARTS)]
Y_SWAP = [(at, at ^ 1) for at in range(8)]
Z_GROUPS = [[0, 2, 4, 6], [1, 3, 5, 7]]


def added(*terms):
    total = terms[0].astype(F32)
    for term in terms[1:]:
        total = total + term.astype(F32)
    return total


def over_x(value, name):
    with jax.named_scope(f"x_{name}"):
        return lax.ppermute(value, "tensor", X_SWAP)


def over_y(value, name):
    with jax.named_scope(f"y_{name}"):
        return lax.ppermute(value, "dp", Y_SWAP)


def over_core(value, name="pair"):
    with jax.named_scope(f"core_{name}"):
        return lax.ppermute(value, "tensor", CORE_SWAP)


def along_z(value, step, name):
    pairs = [(at, ((at // 2 + step) % 4) * 2 + at % 2) for at in range(8)]
    with jax.named_scope(f"z_{name}_{step}"):
        return lax.ppermute(value, "dp", pairs)


def tied(*values):
    return lax.optimization_barrier(values)


class Reduction:
    def __init__(self, name, pieces, y_first):
        self.name = name
        self.keep, self.send = pieces
        self.first, self.second = (over_y, over_x) if y_first else (over_x, over_y)

    def start(self):
        self.one = self.first(self.send, self.name + "_first")

    def add_second(self):
        with jax.named_scope(f"add_{self.name}_second"):
            self.terms = added(self.keep[1], self.one[1]).astype(BF)

    def start_second(self):
        self.two = self.second(self.terms, self.name + "_second")

    def block(self, step):
        return added(self.keep[0, step], self.one[0, step], self.two[step])


class Column:
    def __init__(self, *items):
        self.items = items
        self.name = "_".join(item.name for item in items)

    def add_third(self):
        with jax.named_scope(f"add_{self.name}_third"):
            self.blocks = [
                jnp.concatenate([item.block(step).astype(BF) for item in self.items], 1)
                for step in range(1, 4)
            ]

    def start_third(self):
        self.arrived = [
            along_z(block, step + 1, self.name) for step, block in enumerate(self.blocks)
        ]

    def totals(self):
        with jax.named_scope(f"add_{self.name}_last"):
            results, at = [], 0
            for item in self.items:
                own = item.block(0)
                end = at + own.shape[1]
                results.append(own + added(*[value[:, at:end] for value in self.arrived]))
                at = end
        return results


def reduce_whole(grads, devices):
    grads = grads.reshape(PARTS, devices, WIDTH // devices, -1)
    grads = jnp.transpose(grads, (1, 0, 2, 3)).reshape(devices * PARTS, WIDTH // devices, -1)
    return lax.psum_scatter(grads, BOTH, scatter_dimension=0, tiled=True)[0].astype(F32)


def total_over_plane(value):
    with jax.named_scope("cross_sums"):
        far = lax.ppermute(value, "tensor", [(at, at ^ 3) for at in range(PARTS)])
    value = (value + over_core(value, "sums")) + (over_x(value, "sums") + far)
    return value + over_y(value, "sums")


def total_over_column(value):
    column = jnp.stack([value, *[along_z(value, step, "sums") for step in range(1, 4)]])
    z_at = lax.axis_index("dp") // 2
    ordered = [
        lax.dynamic_index_in_dim(column, (z_at - at) & 3, 0, keepdims=False) for at in range(4)
    ]
    return (ordered[0] + ordered[1]) + (ordered[2] + ordered[3])


def score_kernel(count, lengths_ref, log_ref, queries_ref, passages_ref, powers_ref, sums_ref, logit_ref):
    queries = queries_ref[...]

    def single(at, carry):
        similar = nt(passages_ref[at], queries)
        spot = lax.broadcasted_iota(jnp.int32, (PLEN, ROWS), 0)
        powers = jnp.where(spot < lengths_ref[at], jnp.exp(SHARPNESS * similar), 0.0)
        powers_ref[at] = powers.astype(BF)
        sums_ref[pl.ds(at, 1), :] = jnp.sum(powers, 0, keepdims=True)
        return carry

    lax.fori_loop(0, count, single, 0)
    smooth = (jnp.log(sums_ref[...]) - log_ref[...]) / SHARPNESS
    token = lax.broadcasted_iota(jnp.int32, (ROWS, DIM), 0) // QLEN
    query = lax.broadcasted_iota(jnp.int32, (ROWS, DIM), 1)
    pick = (token == query).astype(F32)
    logit_ref[...] = SCORE_SCALE * jnp.dot(
        smooth, pick, precision=lax.Precision.HIGHEST, preferred_element_type=F32
    )


def pull_kernel(count, powers_ref, steer_ref, queries_ref, passages_ref, passage_out, query_out, total):
    queries = queries_ref[...]
    total[...] = jnp.zeros_like(total)

    def single(at, carry):
        shares = (powers_ref[at].astype(F32) * steer_ref[pl.ds(at, 1), :]).astype(BF)
        passage_out[at] = nn(shares, queries).astype(BF)
        total[...] += nn(passages_ref[at].T, shares)
        return carry

    lax.fori_loop(0, count, single, 0)
    query_out[...] = total[...].T


def scores_of(queries, passages, lengths):
    count = passages.shape[0]
    return pl.pallas_call(
        functools.partial(score_kernel, count),
        out_shape=[
            shaped((count, PLEN, ROWS), BF),
            shaped((count, ROWS), F32),
            shaped((count, DIM), F32),
        ],
        in_specs=[pl.BlockSpec(memory_space=pltpu.SMEM)] + [vmem_spec()] * 3,
        out_specs=[vmem_spec()] * 3,
        compiler_params=params(),
        cost_estimate=price(4),
        name="scores",
    )(lengths, jnp.log(lengths.astype(F32))[:, None], queries, passages)


def pulls_of(powers, steer, queries, passages):
    count = passages.shape[0]
    return pl.pallas_call(
        functools.partial(pull_kernel, count),
        out_shape=[shaped((count, PLEN, DIM), BF), shaped((ROWS, DIM), F32)],
        in_specs=[vmem_spec()] * 4,
        out_specs=[vmem_spec()] * 2,
        scratch_shapes=[pltpu.VMEM((DIM, ROWS), F32)],
        compiler_params=params(),
        cost_estimate=price(4),
        name="score_pulls",
    )(powers, steer, queries, passages)


def adam_step(master, moment, second, gradient, decay):
    moment_new = BETA_ONE * moment + (1.0 - BETA_ONE) * gradient
    second_new = BETA_TWO * second + (1.0 - BETA_TWO) * gradient * gradient
    rising = moment_new / (1.0 - BETA_ONE**STEP)
    spread = jnp.sqrt(second_new / (1.0 - BETA_TWO**STEP))
    return (moment_new, second_new, -LEARN_RATE * (rising / (spread + ADAM_EPS) + decay * master))


def joined(*pieces):
    return jnp.concatenate([piece.astype(BF) for piece in pieces], 1)


def attention_shard(qkv, out):
    return joined(qkv[0], qkv[1], qkv[2], out.T)


class Gathering:
    def __init__(self, name, shard, x_last):
        self.name = name
        self.shard = shard
        self.plan = ("x_last" if x_last else "y_last", 0)
        self.first, self.second = (over_y, over_x) if x_last else (over_x, over_y)

    def column(self):
        arrived = [along_z(self.shard, step, self.name) for step in range(1, 4)]
        self.held = jnp.stack([self.shard, *arrived])

    def plane(self):
        self.held = jnp.stack([self.held, self.first(self.held, self.name + "_first")])

    def cross(self):
        self.other = self.second(self.held, self.name + "_second")

    def all(self):
        pairs = [over_core(self.held, self.name), over_core(self.other, self.name)]
        return [self.held, self.other, *pairs], self.plan


def gather_whole(shard, devices):
    rows_each = shard.shape[0]
    value = lax.all_gather(shard, BOTH, axis=0, tiled=False)
    if devices == 8:
        return value.reshape(4, 2, PARTS, rows_each, -1)
    value = value.reshape(devices, PARTS, rows_each, -1)
    return jnp.transpose(value, (1, 0, 2, 3)).reshape(1, 1, PARTS, WIDTH, -1)


def whole_weights(value):
    return {
        "att": ([value], ("whole", 0)),
        "up": ([value], ("whole", SLAB)),
        "down": ([value], ("whole", 2 * SLAB)),
        "proj": PACK,
    }


def unpack_grads(att_list, up_list, down_list):
    qkv = jnp.stack(
        [
            jnp.stack([att[:, kind * OWN : (kind + 1) * OWN] for kind in range(3)])
            for att in att_list
        ]
    )
    out = jnp.stack([att[:, 3 * OWN :].T for att in att_list])
    return qkv, out, jnp.stack(up_list), jnp.stack([down[:, :SLAB].T for down in down_list])


def to_output_rows(grad, tensor_at):
    rows = PDEV * PLEN // PARTS
    query_rows = QDEV * QLEN // PARTS
    start = jnp.where(tensor_at == PARTS - 1, 0, ROWS - rows)
    step = lax.ppermute(
        lax.dynamic_slice_in_dim(grad, start, rows, 0).astype(BF),
        "tensor",
        [(at, (at + 1) % PARTS) for at in range(PARTS)],
    ).astype(F32)
    last = PARTS - 1
    sent = grad.astype(BF)
    one = lax.ppermute(sent[query_rows : 2 * query_rows], "tensor", [(last, 1)]).astype(F32)
    two = lax.ppermute(sent[2 * query_rows : 3 * query_rows], "tensor", [(last, 2)]).astype(F32)
    own = grad[last * query_rows :]
    query = jnp.where(
        tensor_at == 0,
        step[:query_rows],
        jnp.where(tensor_at == 1, one, jnp.where(tensor_at == 2, two, own)),
    )
    unit = query_rows
    passage = jnp.where(
        tensor_at == 0,
        grad[:rows],
        jnp.where(
            tensor_at == 1,
            jnp.concatenate([step[2 * unit :], grad[: 2 * unit]]),
            jnp.where(tensor_at == 2, jnp.concatenate([step[unit:], grad[:unit]]), step),
        ),
    )
    return query, passage


def body(
    query_tokens,
    passage_tokens,
    query_mask,
    passage_lengths,
    positives,
    qkv_weight,
    qkv_moment,
    qkv_second,
    out_weight,
    out_moment,
    out_second,
    up_weight,
    up_moment,
    up_second,
    down_weight,
    down_moment,
    down_second,
    projection,
    projection_moment,
    projection_second,
    bias_pair,
    bias_pair_moment,
    bias_pair_second,
    bias_up,
    bias_up_moment,
    bias_up_second,
    norm_terms,
    norm_terms_moment,
    norm_terms_second,
):
    devices = lax.axis_size("dp")
    dev_index = lax.axis_index("dp")
    tensor_at = lax.axis_index("tensor")
    last = PARTS - 1
    is_query = tensor_at == last
    rows_each = WIDTH // devices
    split = devices == 8
    pair_own = jnp.concatenate(
        [
            bias_pair[:, 0],
            jnp.zeros((LAYERS, OWN), F32),
            bias_pair[:, 1],
            jnp.zeros((LAYERS, HELD - 3 * OWN), F32),
        ],
        -1,
    )
    small = jnp.concatenate([pair_own, bias_up], -1)
    if split:
        crossed = over_x(small, "biases")
        small_all = [small, crossed, over_core(small, "biases"), over_core(crossed, "biases")]
        small_all = jnp.stack(small_all)
    else:
        small_all = lax.all_gather(small, "tensor", axis=0, tiled=False)

    shards = [
        (
            attention_shard(qkv_weight[at], out_weight[at]),
            up_weight[at].astype(BF),
            down_weight[at].T.astype(BF),
        )
        for at in range(LAYERS)
    ]
    if split:
        last_layer = whole_weights(gather_whole(joined(*shards[1], projection), devices))
        att = Gathering("att_0", shards[0][0], True)
        up = Gathering("up_0", shards[0][1], False)
        down = Gathering("down_0", shards[0][2], True)
        att.column()
        att.held, up.shard, down.shard, small_all = tied(
            att.held, up.shard, down.shard, small_all
        )
        att.plane()
        up.column()
        down.column()
        up.plane()
        down.plane()
        att.cross()
        up.cross()
        down.cross()
        first_layer = {"att": att.all()}
    else:
        first_layer = whole_weights(gather_whole(joined(*shards[0]), devices))
        last_layer = whole_weights(gather_whole(joined(*shards[1], projection), devices))
    weights = [first_layer, last_layer]
    for layer in weights:
        layer["fold"] = (4, 2, rows_each) if split else (1, 1, WIDTH)
    pair_rows = small_all[:, :, None, :HELD]
    up_all = small_all[:, :, None, HELD:]
    passage_at = jnp.minimum(tensor_at, last - 1)
    own_passage = lax.dynamic_slice_in_dim(passage_tokens, passage_at * PLEN, PLEN, 0)
    hidden = jnp.where(is_query, query_tokens, own_passage)
    own_length = lax.dynamic_slice_in_dim(passage_lengths, dev_index * PDEV + passage_at, 1, 0)
    spot = jnp.arange(ROWS, dtype=jnp.int32)
    key_valid = jnp.where(is_query, query_mask.reshape(ROWS) == 1, spot < own_length)
    together = jnp.logical_or(
        jnp.logical_not(is_query), spot[:, None] // QLEN == spot[None, :] // QLEN
    )
    mask = jnp.where(jnp.logical_and(key_valid[:, None], together), 0.0, MASKED).astype(F32)

    place = jnp.stack([tensor_at // 2, tensor_at % 2, dev_index % 2, dev_index // 2]).astype(jnp.int32)

    def sides_of(keep, send):
        return [keep, over_core(send)] if split else [keep]

    def shared(value):
        return [value, over_core(value)] if split else [value]

    saved_list = []
    for layer_at in range(LAYERS):
        outs = run_attention(
            layer_at,
            place,
            hidden,
            mask,
            pair_rows[:, layer_at],
            norm_terms[layer_at],
            weights[layer_at],
            split,
        )
        first, x_t, packed, chances, normal_one, factor_one, first_t = outs[:7]
        if split and layer_at == 0:
            first, up.held, up.other, down.held, down.other = tied(
                first, up.held, up.other, down.held, down.other
            )
            weights[0].update(up=up.all(), down=down.all())
        mixtures = sides_of(outs[7], outs[-1])
        outs = run_mlp(
            layer_at, place, first, up_all[:, layer_at], norm_terms[layer_at], weights[layer_at], split
        )
        hidden, slope, normal_two, factor_two = outs[:4]
        acts = sides_of(outs[4], outs[5 if split else 4])
        saved_list.append(
            dict(
                mlp=(slope, normal_two, factor_two),
                attention=(packed, chances, normal_one, factor_one),
                x_t=shared(x_t),
                first_t=shared(first_t),
                mixtures=mixtures,
                acts=acts,
            )
        )
    embedding, unit, scale, top_t = outs[-4:]

    passages = lax.all_to_all(
        jnp.broadcast_to(embedding[None], (devices, ROWS, DIM)), "dp", 0, 0, tiled=True
    )
    queries = embedding
    arrived = [lax.ppermute(embedding, "tensor", [(last, at)]) for at in range(last)]
    for at in range(last):
        queries = jnp.where(tensor_at == at, arrived[at], queries)
    length_table = passage_lengths.reshape(devices, PDEV)
    own_lengths = lax.dynamic_slice_in_dim(length_table, passage_at, 1, 1)[:, 0]
    powers, sums, logit_part = scores_of(queries, passages, own_lengths)
    logits = lax.all_gather(logit_part[:, :QDEV], "tensor", axis=0, tiled=False)[:last]
    own_positives = lax.dynamic_slice_in_dim(positives, dev_index * QDEV, QDEV, 0)
    ids = (
        lax.broadcasted_iota(jnp.int32, logits.shape, 1) * PDEV
        + lax.broadcasted_iota(jnp.int32, logits.shape, 0)
    )
    chosen = ids == own_positives[None, None, :]
    highest = jnp.max(logits, (0, 1), keepdims=True)
    raised = jnp.exp(logits - highest)
    summed = jnp.sum(raised, (0, 1), keepdims=True)
    losses = highest + jnp.log(summed) - jnp.sum(jnp.where(chosen, logits, 0.0), (0, 1), keepdims=True)
    deltas = raised / summed - chosen.astype(F32)
    own_deltas = lax.dynamic_slice_in_dim(deltas, passage_at, 1, 0)[0]
    steer = jnp.where(is_query, 0.0, SCORE_SCALE) * jnp.repeat(own_deltas, QLEN, axis=1) / sums
    passage_terms, query_terms = pulls_of(powers, steer, queries, passages)
    passage_back = lax.all_to_all(passage_terms, "dp", 0, 0, tiled=True)
    grad_passage = jnp.sum(passage_back.astype(F32), 0)
    returned = [lax.ppermute(query_terms, "tensor", [(at, last)]) for at in range(last)]
    grad_query = returned[0] + returned[1] + returned[2]
    grad_emb = jnp.where(is_query, grad_query, grad_passage)

    upstream = (grad_emb, unit, scale, top_t)
    mlp_sums, attention_sums = [None] * LAYERS, [None] * LAYERS

    def stacked_sums():
        loss_part = jnp.where(tensor_at == 0, jnp.sum(losses), 0.0)
        sums = jnp.stack([attention_sums[0], mlp_sums[0], attention_sums[1], mlp_sums[1]])
        row_ids = lax.broadcasted_iota(jnp.int32, sums.shape, 1)
        sums = sums + jnp.where(row_ids == 7, loss_part, 0.0)
        return sums

    def mlp_pull(layer_at, upstream):
        saved = saved_list[layer_at]
        outs = run_mlp_pull(
            layer_at, place, upstream, saved["mlp"], norm_terms[layer_at], weights[layer_at], split
        )
        grad_first, mlp_sums[layer_at], low_t = outs[:3]
        groups = [
            saved["first_t"],
            sides_of(outs[3], outs[4 if split else 3]),
            shared(low_t),
            saved["acts"],
        ]
        if layer_at == LAYERS - 1:
            groups.append(shared(outs[-1]))
        return grad_first, groups

    def attention_pull(layer_at, grad_first):
        saved = saved_list[layer_at]
        outs = run_attention_pull(
            layer_at,
            place,
            grad_first,
            saved["attention"],
            norm_terms[layer_at],
            weights[layer_at],
            split,
        )
        dx, attention_sums[layer_at], low_t = outs[:3]
        return dx, [
            saved["x_t"],
            sides_of(outs[3], outs[-1]),
            shared(low_t),
            saved["mixtures"],
        ]

    def mlp_grad(layer_at, groups):
        return run_mlp_grad(layer_at, place, groups, split, rows_each)

    def attention_grad(layer_at, cuts, groups):
        return run_attention_grad(layer_at, cuts, place, groups, split, rows_each)

    if split:
        grad_first, mlp_groups = mlp_pull(1, upstream)
        up_grads, down_grads = mlp_grad(1, mlp_groups)
        up_one, down_one = Reduction("up_1", up_grads, False), Reduction("down_1", down_grads, True)
        grad_first, up_one.send, down_one.send = tied(grad_first, up_one.send, down_one.send)
        up_one.start()
        down_one.start()
        dx, att_groups = attention_pull(1, grad_first)
        att_one = Reduction("att_1", attention_grad(1, ((0, SLAB, False),), att_groups)[0], False)
        dx, att_one.send = tied(dx, att_one.send)
        att_one.start()
        grad_first, mlp_groups = mlp_pull(0, (dx,))
        up_one.add_second()
        down_one.add_second()
        mlp_groups[0][0], up_one.terms, down_one.terms = tied(
            mlp_groups[0][0], up_one.terms, down_one.terms
        )
        up_one.start_second()
        down_one.start_second()
        up_grads, down_grads = mlp_grad(0, mlp_groups)
        up_zero = Reduction("up_0", up_grads, False)
        down_zero = Reduction("down_0", down_grads, True)
        grad_first, up_zero.send, down_zero.send = tied(grad_first, up_zero.send, down_zero.send)
        up_zero.start()
        down_zero.start()
        dx, att_groups = attention_pull(0, grad_first)
        dx, att_one.one = tied(dx, att_one.one)
        att_one.add_second()
        att_groups[0][0], att_one.terms = tied(att_groups[0][0], att_one.terms)
        att_one.start_second()
        mlp_one = Column(up_one, down_one)
        mlp_one.add_third()
        up_zero.add_second()
        down_zero.add_second()
        att_groups[0][0], up_zero.terms, down_zero.terms = tied(
            att_groups[0][0], up_zero.terms, down_zero.terms
        )
        half = SLAB // 2
        left, right = attention_grad(0, ((0, half, False), (half, half, True)), att_groups)
        halves = (Reduction("qk_0", left, False), Reduction("vo_0", right, True))
        column_one = Column(att_one)
        mlp_one.start_third()
        column_one.add_third()
        column_one.start_third()
        for item in (up_zero, down_zero):
            item.start_second()
        qk_zero, vo_zero = halves
        up_zero.two, down_zero.two, qk_zero.send, vo_zero.send = tied(
            up_zero.two, down_zero.two, qk_zero.send, vo_zero.send
        )
        for item in halves:
            item.start()
        mlp_zero = Column(up_zero, down_zero)
        mlp_zero.add_third()
        mlp_zero.start_third()
        for item in halves:
            item.add_second()
        attention_sums[0], dx, qk_zero.terms, vo_zero.terms = tied(
            attention_sums[0], dx, qk_zero.terms, vo_zero.terms
        )
        for item in halves:
            item.start_second()
        sums = total_over_plane(stacked_sums())
        sums, qk_zero.two, vo_zero.two = tied(sums, qk_zero.two, vo_zero.two)
        column_zero = Column(qk_zero, vo_zero)
        column_zero.add_third()
        column_zero.start_third()
        sums = total_over_column(sums)
        att_list = [jnp.concatenate(column_zero.totals(), 1), *column_one.totals()]
        (up_grad_zero, down_grad_zero), (up_grad_one, down_grad_one) = (
            mlp_zero.totals(),
            mlp_one.totals(),
        )
        up_list, down_list = [up_grad_zero, up_grad_one], [down_grad_zero, down_grad_one]
    else:
        att_list, up_list, down_list = [], [], []
        dx = None
        for layer_at in range(LAYERS - 1, -1, -1):
            grad_first, groups = mlp_pull(layer_at, (dx,) if upstream is None else upstream)
            upstream = None
            up_grads, down_grads = mlp_grad(layer_at, groups)
            dx, groups = attention_pull(layer_at, grad_first)
            att_grads = attention_grad(layer_at, ((0, SLAB, False),), groups)[0]
            up_list.insert(0, reduce_whole(up_grads[0], devices))
            down_list.insert(0, reduce_whole(down_grads[0], devices))
            att_list.insert(0, reduce_whole(att_grads[0], devices))
        sums = lax.psum(stacked_sums(), BOTH)
    sums = sums.reshape(LAYERS, 2, 8, WIDTH)
    norms_grad = sums[:, :, :3].reshape(LAYERS, 6, WIDTH)
    own_sums = lax.dynamic_slice_in_dim(sums, 3 + tensor_at, 1, 2)[:, :, 0]
    pair_grad = jnp.stack([own_sums[:, 0, :OWN], own_sums[:, 0, 2 * OWN : 3 * OWN]], 1)
    bias_grad = own_sums[:, 1]
    loss_mean = sums[0, 0, 7, 0] / (QDEV * devices)
    projection_grad = down_list[LAYERS - 1][:, SLAB:]
    qkv_grad, out_grad, up_grad, down_grad = unpack_grads(att_list, up_list, down_list)
    qkv_m, qkv_v, qkv_u = adam_step(qkv_weight, qkv_moment, qkv_second, qkv_grad, WEIGHT_DECAY)
    out_m, out_v, out_u = adam_step(out_weight, out_moment, out_second, out_grad, WEIGHT_DECAY)
    up_m, up_v, up_u = adam_step(up_weight, up_moment, up_second, up_grad, WEIGHT_DECAY)
    down_m, down_v, down_u = adam_step(
        down_weight, down_moment, down_second, down_grad, WEIGHT_DECAY
    )
    proj_m, proj_v, proj_u = adam_step(
        projection, projection_moment, projection_second, projection_grad, WEIGHT_DECAY
    )
    pair_m, pair_v, pair_u = adam_step(
        bias_pair, bias_pair_moment, bias_pair_second, pair_grad, 0.0
    )
    bias_m, bias_v, bias_u = adam_step(bias_up, bias_up_moment, bias_up_second, bias_grad, 0.0)
    norm_m, norm_v, norm_u = adam_step(
        norm_terms, norm_terms_moment, norm_terms_second, norms_grad, 0.0
    )
    query_grad, passage_grad = to_output_rows(dx, tensor_at)
    return (
        loss_mean,
        query_grad,
        passage_grad,
        qkv_grad,
        qkv_m,
        qkv_v,
        qkv_u,
        out_grad,
        out_m,
        out_v,
        out_u,
        up_grad,
        up_m,
        up_v,
        up_u,
        down_grad,
        down_m,
        down_v,
        down_u,
        projection_grad,
        proj_m,
        proj_v,
        proj_u,
        pair_grad,
        pair_m,
        pair_v,
        pair_u,
        bias_grad,
        bias_m,
        bias_v,
        bias_u,
        norms_grad,
        norm_m,
        norm_v,
        norm_u,
    )


def solution(mesh):
    placed = (
        P("dp", None),
        P("dp", None),
        P("dp", None),
        P(),
        P(),
        P(None, None, "dp", "tensor"),
        P(None, None, "dp", "tensor"),
        P(None, None, "dp", "tensor"),
        P(None, "tensor", "dp"),
        P(None, "tensor", "dp"),
        P(None, "tensor", "dp"),
        P(None, "dp", "tensor"),
        P(None, "dp", "tensor"),
        P(None, "dp", "tensor"),
        P(None, "tensor", "dp"),
        P(None, "tensor", "dp"),
        P(None, "tensor", "dp"),
        P("dp", None),
        P("dp", None),
        P("dp", None),
        P(None, None, "tensor"),
        P(None, None, "tensor"),
        P(None, None, "tensor"),
        P(None, "tensor"),
        P(None, "tensor"),
        P(None, "tensor"),
        P(),
        P(),
        P(),
    )
    return jax.shard_map(
        body,
        mesh=mesh,
        in_specs=placed,
        out_specs=(
            P(),
            P(("dp", "tensor"), None),
            P(("dp", "tensor"), None),
            P(None, None, "dp", "tensor"),
            P(None, None, "dp", "tensor"),
            P(None, None, "dp", "tensor"),
            P(None, None, "dp", "tensor"),
            P(None, "tensor", "dp"),
            P(None, "tensor", "dp"),
            P(None, "tensor", "dp"),
            P(None, "tensor", "dp"),
            P(None, "dp", "tensor"),
            P(None, "dp", "tensor"),
            P(None, "dp", "tensor"),
            P(None, "dp", "tensor"),
            P(None, "tensor", "dp"),
            P(None, "tensor", "dp"),
            P(None, "tensor", "dp"),
            P(None, "tensor", "dp"),
            P("dp", None),
            P("dp", None),
            P("dp", None),
            P("dp", None),
            P(None, None, "tensor"),
            P(None, None, "tensor"),
            P(None, None, "tensor"),
            P(None, None, "tensor"),
            P(None, "tensor"),
            P(None, "tensor"),
            P(None, "tensor"),
            P(None, "tensor"),
            P(),
            P(),
            P(),
            P(),
        ),
        check_vma=False,
    )
```

```python
import functools

import jax
import jax.numpy as jnp
from jax import lax
from jax.experimental import pallas as pl
from jax.experimental.pallas import tpu as pltpu
from jax.sharding import PartitionSpec as P

WIDTH = 768
HEAD = 64
DIM = 128
QLEN = 32
PLEN = 256
LAYERS = 2
STEP = 10
QDEV = 8
PDEV = 3
ROWS = 256
PARTS = 4
HEADS_EACH = 3
OWN = HEADS_EACH * HEAD
SLAB = 768
HELD = 640
PACK = 3 * SLAB

MASKED = -1e30
SHARPNESS = 24.0
SCORE_SCALE = 4.0
LN_EPS = 1e-12
NORM_EPS = 1e-12
BETA_ONE = 0.9
BETA_TWO = 0.999
ADAM_EPS = 1e-08
LEARN_RATE = 0.02
WEIGHT_DECAY = 0.01
VMEM_BYTES = 60 * 1024 * 1024

BF = jnp.bfloat16
F32 = jnp.float32
BOTH = ("dp", "tensor")


def nn(left, right):
    return jnp.dot(left, right, preferred_element_type=F32)


def nt(left, right):
    return lax.dot_general(left, right, (((1,), (1,)), ((), ())), preferred_element_type=F32)


def norm_forward(values):
    average = jnp.mean(values, -1, keepdims=True)
    centred = values - average
    factor = lax.rsqrt(jnp.mean(centred * centred, -1, keepdims=True) + LN_EPS)
    return centred * factor, factor


def norm_backward(upstream, normal, factor, gains):
    scaled = upstream * gains
    average = jnp.mean(scaled, -1, keepdims=True)
    cross = jnp.mean(scaled * normal, -1, keepdims=True)
    return factor * (scaled - average - normal * cross)


def column_sum(values):
    return jnp.sum(values.astype(F32), 0, keepdims=True)


def part_order(place, split):
    if not split:
        return list(range(PARTS))
    x_at, c_at = place[0], place[1]
    return [
        (x_at ^ x_rel) * 2 + (c_at ^ c_rel) for c_rel in range(2) for x_rel in range(2)
    ]


class Copies:
    def __init__(self, copies):
        self.copies = copies

    def start(self):
        for copy in self.copies:
            copy.start()

    def wait(self):
        for copy in self.copies:
            copy.wait()


def weight_copies(refs, plan, held, sems, parts, place):
    kind, base = plan
    groups = []
    for slot, part in enumerate(parts):
        copies = []
        if kind == "whole":
            source = refs[0].at[:, :, part, :, pl.ds(base, SLAB)]
            copies.append(pltpu.make_async_copy(source, held.at[slot], sems.at[slot, 0]))
        else:
            c_rel, x_rel = divmod(slot, 2)
            for y_rel in range(2):
                outer, inner = (x_rel, y_rel) if kind == "x_last" else (y_rel, x_rel)
                for back in range(4):
                    copies.append(
                        pltpu.make_async_copy(
                            refs[2 * c_rel + outer].at[inner, back],
                            held.at[slot, (place[3] - back) & 3, place[2] ^ y_rel],
                            sems.at[slot, 4 * y_rel + back],
                        )
                    )
        groups.append(Copies(copies))
    return groups


def projection_copy(w_ref, proj, sem, base):
    return pltpu.make_async_copy(w_ref.at[:, :, 0, :, pl.ds(base, DIM)], proj, sem)


def stored(refs, slot, value):
    refs[slot // 2 if len(refs) > 1 else 0][slot % 2 if len(refs) > 1 else slot] = value


def attention_kernel(plan, count, split, place, *refs):
    x_ref, mask_ref, pair_ref, norm_ref = refs[:4]
    w_refs, refs = refs[4 : 4 + count], refs[4 + count :]
    first_ref, low_t_ref, packed_ref, chances_ref, normal_ref, factor_ref, first_t_ref = refs[:7]
    mixture_refs = refs[7:-2]
    held, sems = refs[-2:]
    parts = part_order(place, split)
    copies = weight_copies(w_refs, plan, held, sems, parts, place)
    for copy in copies:
        copy.start()
    hidden = x_ref[...]
    low = hidden.astype(BF)
    low_t_ref[...] = low.T
    mask = mask_ref[...]
    attended = jnp.zeros((ROWS, WIDTH), F32)
    for slot in range(PARTS):
        copies[slot].wait()
        weight = held[slot, :, :, :, :HELD].reshape(WIDTH, HELD)
        packed = (nn(low, weight) + pair_ref[slot]).astype(BF)
        packed_ref[slot] = packed
        values_t = packed[:, 2 * OWN : 3 * OWN].T
        mixed = [jnp.zeros((HEAD, ROWS), F32)]
        for head in range(HEADS_EACH):
            queries = packed[:, head * HEAD : (head + 1) * HEAD]
            keys = packed[:, OWN + head * HEAD : OWN + (head + 1) * HEAD]
            scores = nt(keys, queries) * 0.125 + mask
            powers = jnp.exp(scores - jnp.max(scores, 0, keepdims=True))
            chances = (powers * (1.0 / jnp.sum(powers, 0, keepdims=True))).astype(BF)
            chances_ref[slot * HEADS_EACH + head] = chances
            mixed.append(nn(values_t[head * HEAD : (head + 1) * HEAD], chances))
        mixture = jnp.concatenate(mixed, 0).astype(BF).T
        stored(mixture_refs, slot, mixture)
        attended = attended + nt(
            mixture, held[slot, :, :, :, SLAB - ROWS :].reshape(WIDTH, ROWS)
        )
    normal, factor = norm_forward(hidden + attended + norm_ref[0:1])
    normal_ref[...] = normal
    factor_ref[...] = jnp.broadcast_to(factor, factor_ref.shape)
    first = normal * norm_ref[1:2] + norm_ref[2:3]
    first_ref[...] = first
    first_t_ref[...] = first.astype(BF).T


def mlp_kernel(up_plan, down_plan, proj_base, count, top, split, place, *refs):
    first_ref, up_bias_ref, norm_ref = refs[:3]
    up_refs, down_refs = refs[3 : 3 + count], refs[3 + count : 3 + 2 * count]
    refs = refs[3 + 2 * count :]
    out_ref, slope_ref, normal_ref, factor_ref = refs[:4]
    act_refs = refs[4 : 6 if split else 5]
    refs = refs[4 + len(act_refs) :]
    if top:
        emb_ref, unit_ref, scale_ref, top_t_ref = refs[:4]
        refs = refs[4:]
    up_held, down_held, up_sems, down_sems = refs[:4]
    parts = part_order(place, split)
    ups = weight_copies(up_refs, up_plan, up_held, up_sems, parts, place)
    downs = weight_copies(down_refs, down_plan, down_held, down_sems, parts, place)
    for slot in range(PARTS):
        ups[slot].start()
        downs[slot].start()
    if top:
        proj, proj_sem = refs[4:]
        proj_load = projection_copy(up_refs[0], proj, proj_sem, proj_base)
        proj_load.start()
    first = first_ref[...]
    first_low = first.astype(BF)
    spread = jnp.zeros((ROWS, WIDTH), F32)
    for slot in range(PARTS):
        ups[slot].wait()
        pre_act = nn(first_low, up_held[slot].reshape(WIDTH, SLAB)) + up_bias_ref[slot]
        chance = 0.5 * (1.0 + lax.erf(pre_act * 0.7071067811865476))
        act = (pre_act * chance).astype(BF)
        stored(act_refs, slot, act)
        slope_ref[slot] = (
            chance + pre_act * jnp.exp(-0.5 * pre_act * pre_act) * 0.3989422804014327
        ).astype(BF)
        downs[slot].wait()
        spread = spread + nt(act, down_held[slot].reshape(WIDTH, SLAB))
    normal, factor = norm_forward(first + spread + norm_ref[3:4])
    normal_ref[...] = normal
    factor_ref[...] = jnp.broadcast_to(factor, factor_ref.shape)
    second = normal * norm_ref[4:5] + norm_ref[5:6]
    out_ref[...] = second
    if top:
        second_low = second.astype(BF)
        top_t_ref[...] = second_low.T
        proj_load.wait()
        embedded = nn(second_low, proj[...].reshape(WIDTH, DIM))
        scale = lax.rsqrt(jnp.sum(embedded * embedded, -1, keepdims=True) + NORM_EPS)
        unit = embedded * scale
        unit_ref[...] = unit
        emb_ref[...] = jnp.broadcast_to(unit.astype(BF)[None], emb_ref.shape)
        scale_ref[...] = jnp.broadcast_to(scale, scale_ref.shape)


def mlp_pull_kernel(up_plan, down_plan, proj_base, count, top, split, place, *refs):
    if top:
        grad_emb_ref, unit_ref, scale_ref, top_t_ref = refs[:4]
        refs = refs[4:]
    else:
        dy_ref = refs[0]
        refs = refs[1:]
    slope_ref, normal_ref, factor_ref, norm_ref = refs[:4]
    up_refs, down_refs = refs[4 : 4 + count], refs[4 + count : 4 + 2 * count]
    refs = refs[4 + 2 * count :]
    grad_ref, sum_ref, low_t_ref = refs[:3]
    pre_refs = refs[3 : 5 if split else 4]
    refs = refs[3 + len(pre_refs) :]
    if top:
        proj_grad_ref = refs[0]
        refs = refs[1:]
    up_held, down_held, up_sems, down_sems = refs[:4]
    parts = part_order(place, split)
    ups = weight_copies(up_refs, up_plan, up_held, up_sems, parts, place)
    downs = weight_copies(down_refs, down_plan, down_held, down_sems, parts, place)
    if top:
        proj, proj_sem = refs[4:]
        proj_load = projection_copy(up_refs[0], proj, proj_sem, proj_base)
        proj_load.start()
    order = (2, 3, 0, 1) if split else (0, 1, 2, 3)
    for slot in order:
        downs[slot].start()
        ups[slot].start()
    if top:
        grad_emb = grad_emb_ref[...]
        unit = unit_ref[...]
        low_emb = (
            scale_ref[:, :1] * (grad_emb - unit * jnp.sum(grad_emb * unit, -1, keepdims=True))
        ).astype(BF)
        proj_grad_ref[...] = nn(top_t_ref[...], low_emb)
        proj_load.wait()
        dy = nt(low_emb, proj[...].reshape(WIDTH, DIM))
    else:
        dy = dy_ref[...]
    normal = normal_ref[...]
    grad_two = norm_backward(dy, normal, factor_ref[:, :1], norm_ref[4:5])
    sum_ref[0:1] = column_sum(grad_two)
    sum_ref[1:2] = column_sum(dy * normal)
    sum_ref[2:3] = column_sum(dy)
    sum_ref[7:8] = jnp.zeros((1, WIDTH), F32)
    low = grad_two.astype(BF)
    low_t_ref[...] = low.T
    grad_first = grad_two
    for slot in order:
        downs[slot].wait()
        grad_act = nn(low, down_held[slot].reshape(WIDTH, SLAB))
        pre_low = (grad_act * slope_ref[slot].astype(F32)).astype(BF)
        sum_ref[pl.ds(3 + parts[slot], 1), :] = column_sum(pre_low)
        stored(pre_refs, slot, pre_low)
        ups[slot].wait()
        grad_first = grad_first + nt(pre_low, up_held[slot].reshape(WIDTH, SLAB))
    grad_ref[...] = grad_first


def attention_pull_kernel(plan, count, split, place, *refs):
    grad_first_ref, packed_ref, chances_ref, normal_ref, factor_ref, norm_ref = refs[:6]
    w_refs, refs = refs[6 : 6 + count], refs[6 + count :]
    dx_ref, sum_ref, low_t_ref = refs[:3]
    packed_grad_refs = refs[3:-2]
    held, sems = refs[-2:]
    parts = part_order(place, split)
    copies = weight_copies(w_refs, plan, held, sems, parts, place)
    order = (2, 3, 0, 1) if split else (0, 1, 2, 3)
    for slot in order:
        copies[slot].start()
    normal = normal_ref[...]
    grad_first = grad_first_ref[...]
    grad_one = norm_backward(grad_first, normal, factor_ref[:, :1], norm_ref[1:2])
    sum_ref[0:1] = column_sum(grad_one)
    sum_ref[1:2] = column_sum(grad_first * normal)
    sum_ref[2:3] = column_sum(grad_first)
    sum_ref[7:8] = jnp.zeros((1, WIDTH), F32)
    low = grad_one.astype(BF)
    low_t_ref[...] = low.T
    grad_input = grad_one
    for slot in order:
        copies[slot].wait()
        grad_mix = nn(low, held[slot, :, :, :, SLAB - ROWS :].reshape(WIDTH, ROWS)).astype(BF)
        packed = packed_ref[slot]
        keys_t = packed[:, OWN : 2 * OWN].T
        grad_queries, grad_keys, grad_values = [], [], []
        for head in range(HEADS_EACH):
            queries = packed[:, head * HEAD : (head + 1) * HEAD]
            values = packed[:, 2 * OWN + head * HEAD : 2 * OWN + (head + 1) * HEAD]
            upstream = grad_mix[:, (head + 1) * HEAD : (head + 2) * HEAD]
            chances = chances_ref[slot * HEADS_EACH + head]
            grad_values.append(nn(chances, upstream).astype(BF))
            wide = chances.astype(F32)
            product = wide * nt(values, upstream)
            grad_scores = (product - wide * jnp.sum(product, 0, keepdims=True)).astype(BF)
            grad_keys.append((nn(grad_scores, queries) * 0.125).astype(BF))
            grad_queries.append(nn(keys_t[head * HEAD : (head + 1) * HEAD], grad_scores) * 0.125)
        grad_packed = jnp.concatenate(
            [jnp.concatenate(grad_queries, 0).astype(BF).T]
            + grad_keys
            + grad_values
            + [jnp.zeros((ROWS, SLAB - 3 * OWN), BF)],
            1,
        )
        sum_ref[pl.ds(3 + parts[slot], 1), :] = column_sum(grad_packed)
        stored(packed_grad_refs, slot, grad_packed)
        grad_input = grad_input + nt(grad_packed, held[slot].reshape(WIDTH, SLAB))
    dx_ref[...] = grad_input


def rows_of(refs):
    return jnp.concatenate([ref[...] for ref in refs], 1)


def rows_at(refs, slot):
    return jnp.concatenate([ref[slot] for ref in refs], 0)


def block_sends(stage, slot, targets, sems, place, y_first, base, start=0, width=None):
    width = stage.shape[-1] if width is None else width
    lanes, taken = pl.ds(base, width), pl.ds(start, width)
    if len(targets) == 1:
        copies = [
            pltpu.make_async_copy(
                stage.at[0, 0, :, taken], targets[0].at[slot, :, lanes], sems.at[0, 0]
            )
        ]
    else:
        copies = []
        for y_rel in range(2):
            first, second = (y_rel, slot) if y_first else (slot, y_rel)
            for z_rel in range(4):
                copies.append(
                    pltpu.make_async_copy(
                        stage.at[(place[3] + z_rel) & 3, place[2] ^ y_rel, :, taken],
                        targets[first].at[second, z_rel, :, lanes],
                        sems.at[y_rel, z_rel],
                    )
                )
    for copy in copies:
        copy.start()
    return copies


def mlp_grad_kernel(top, split, place, *refs):
    sides = 2 if split else 1
    groups = []
    for _ in range(4):
        groups.append(refs[:sides])
        refs = refs[sides:]
    first_t_refs, pre_refs, low_t_refs, act_refs = groups
    if top:
        proj_refs, refs = refs[:sides], refs[sides:]
    up_targets, refs = refs[:sides], refs[sides:]
    down_targets, refs = refs[:sides], refs[sides:]
    stage, sems = refs[:2]
    fold = stage.shape[2:]
    slots = PARTS // sides
    sends = []
    if top:
        proj_stage, proj_sems = refs[2:]
        total = proj_refs[0][...]
        for ref in proj_refs[1:]:
            total = total + ref[...]
        proj_stage[...] = total.astype(BF).reshape(proj_stage.shape)
        for slot in range(slots):
            sends += block_sends(
                proj_stage, slot, down_targets, proj_sems.at[slot], place, True, SLAB
            )
    first_t = rows_of(first_t_refs)
    low_t = rows_of(low_t_refs)
    for slot in reversed(range(slots)):
        stage[0, slot] = nn(first_t, rows_at(pre_refs, slot)).astype(BF).reshape(*fold)
        sends += block_sends(stage.at[0, slot], slot, up_targets, sems.at[0, slot], place, False, 0)
        stage[1, slot] = nn(low_t, rows_at(act_refs, slot)).astype(BF).reshape(*fold)
        sends += block_sends(stage.at[1, slot], slot, down_targets, sems.at[1, slot], place, True, 0)
    for copy in sends:
        copy.wait()


def attention_grad_kernel(cuts, split, place, *refs):
    sides = 2 if split else 1
    groups = []
    for _ in range(4):
        groups.append(refs[:sides])
        refs = refs[sides:]
    x_t_refs, packed_refs, low_t_refs, mixture_refs = groups
    targets = []
    for _ in cuts:
        targets.append(refs[:sides])
        refs = refs[sides:]
    stage, sems = refs
    fold = stage.shape[1:]
    sends = []
    x_t = rows_of(x_t_refs)
    low_t = rows_of(low_t_refs)
    for slot in reversed(range(PARTS // sides)):
        grad_weight = nn(x_t, rows_at(packed_refs, slot))
        grad_out = nn(low_t, rows_at(mixture_refs, slot))
        stage[slot] = (
            jnp.concatenate(
                [grad_weight[:, : SLAB - ROWS], grad_weight[:, SLAB - ROWS :] + grad_out], 1
            )
            .astype(BF)
            .reshape(*fold)
        )
        for at, (start, width, y_first) in enumerate(cuts):
            sends += block_sends(
                stage.at[slot], slot, targets[at], sems.at[at, slot], place, y_first, 0, start, width
            )
    for copy in sends:
        copy.wait()


def any_spec():
    return pl.BlockSpec(memory_space=pl.ANY)


def vmem_spec():
    return pl.BlockSpec(memory_space=pltpu.VMEM)


def shaped(shape, kind):
    return jax.ShapeDtypeStruct(shape, kind)


def price(micros):
    return pl.CostEstimate(
        flops=int(micros * 1e6), bytes_accessed=int(micros * 3e3), transcendentals=0
    )


def params():
    return pltpu.CompilerParams(vmem_limit_bytes=VMEM_BYTES)


def smem_spec():
    return pl.BlockSpec(memory_space=pltpu.SMEM)


def sided(split, shape, kind):
    if split:
        return [shaped((2, *shape), kind)] * 2
    return [shaped((PARTS, *shape), kind)]


def held_scratch(fold, count):
    return [pltpu.VMEM((PARTS, *fold, SLAB), BF)] * count + [
        pltpu.SemaphoreType.DMA((PARTS, 8))
    ] * count


def projection_scratch(fold):
    return [pltpu.VMEM((*fold, DIM), BF), pltpu.SemaphoreType.DMA]


def call(kernel, name, micros, place, args, outs, scratch, in_hbm=(), out_hbm=()):
    return pl.pallas_call(
        kernel,
        out_shape=outs,
        in_specs=[smem_spec()]
        + [any_spec() if at in in_hbm else vmem_spec() for at in range(len(args))],
        out_specs=[any_spec() if at in out_hbm else vmem_spec() for at in range(len(outs))],
        scratch_shapes=scratch,
        compiler_params=params(),
        cost_estimate=price(micros),
        name=name,
    )(place, *args)


def run_attention(layer_at, place, hidden, mask, pair_rows, norms, weights, split):
    arrays, plan = weights["att"]
    outs = [
        shaped((ROWS, WIDTH), F32),
        shaped((WIDTH, ROWS), BF),
        shaped((PARTS, ROWS, HELD), BF),
        shaped((PARTS * HEADS_EACH, ROWS, ROWS), BF),
        shaped((ROWS, WIDTH), F32),
        shaped((ROWS, DIM), F32),
        shaped((WIDTH, ROWS), BF),
    ] + sided(split, (ROWS, ROWS), BF)
    args = [hidden, mask, pair_rows, norms, *arrays]
    return call(
        functools.partial(attention_kernel, plan, len(arrays), split),
        f"attention_{layer_at}",
        9,
        place,
        args,
        outs,
        held_scratch(weights["fold"], 1),
        in_hbm=range(4, len(args)),
    )


def run_mlp(layer_at, place, first, up_rows, norms, weights, split, copies):
    top = layer_at == LAYERS - 1
    ups, up_plan = weights["up"]
    downs, down_plan = weights["down"]
    outs = [
        shaped((ROWS, WIDTH), F32),
        shaped((PARTS, ROWS, SLAB), BF),
        shaped((ROWS, WIDTH), F32),
        shaped((ROWS, DIM), F32),
    ] + sided(split, (ROWS, SLAB), BF)
    scratch = held_scratch(weights["fold"], 2)
    if top:
        outs += [
            shaped((copies, ROWS, DIM), BF),
            shaped((ROWS, DIM), F32),
            shaped((ROWS, DIM), F32),
            shaped((WIDTH, ROWS), BF),
        ]
        scratch += projection_scratch(weights["fold"])
    args = [first, up_rows, norms, *ups, *downs]
    return call(
        functools.partial(
            mlp_kernel, up_plan, down_plan, weights.get("proj"), len(ups), top, split
        ),
        f"mlp_{layer_at}",
        9,
        place,
        args,
        outs,
        scratch,
        in_hbm=range(3, len(args)),
    )


def run_mlp_pull(layer_at, place, upstream, saved, norms, weights, split):
    top = layer_at == LAYERS - 1
    ups, up_plan = weights["up"]
    downs, down_plan = weights["down"]
    outs = [
        shaped((ROWS, WIDTH), F32),
        shaped((8, WIDTH), F32),
        shaped((WIDTH, ROWS), BF),
    ] + sided(split, (ROWS, SLAB), BF)
    scratch = held_scratch(weights["fold"], 2)
    if top:
        outs += [shaped((WIDTH, DIM), F32)]
        scratch += projection_scratch(weights["fold"])
    inputs = [*upstream, *saved, norms]
    args = [*inputs, *ups, *downs]
    return call(
        functools.partial(
            mlp_pull_kernel, up_plan, down_plan, weights.get("proj"), len(ups), top, split
        ),
        f"pull_mlp_{layer_at}",
        8,
        place,
        args,
        outs,
        scratch,
        in_hbm=range(len(inputs), len(args)),
    )


def run_attention_pull(layer_at, place, grad_first, saved, norms, weights, split):
    arrays, plan = weights["att"]
    outs = [
        shaped((ROWS, WIDTH), F32),
        shaped((8, WIDTH), F32),
        shaped((WIDTH, ROWS), BF),
    ] + sided(split, (ROWS, SLAB), BF)
    inputs = [grad_first, *saved, norms]
    args = [*inputs, *arrays]
    return call(
        functools.partial(attention_pull_kernel, plan, len(arrays), split),
        f"pull_attention_{layer_at}",
        10,
        place,
        args,
        outs,
        held_scratch(weights["fold"], 1),
        in_hbm=range(len(inputs), len(args)),
    )


def grad_shapes(split, rows_each, width):
    if split:
        return [shaped((2, 4, rows_each, width), BF)] * 2
    return [shaped((PARTS, WIDTH, width), BF)]


def run_mlp_grad(layer_at, place, groups, split, rows_each):
    top = layer_at == LAYERS - 1
    args = [value for group in groups for value in group]
    sides = 2 if split else 1
    outs = grad_shapes(split, rows_each, SLAB)
    outs += grad_shapes(split, rows_each, SLAB + (DIM if top else 0))
    fold = (4, 2, rows_each) if split else (1, 1, WIDTH)
    slots = PARTS // sides
    scratch = [
        pltpu.VMEM((2, slots, *fold, SLAB), BF),
        pltpu.SemaphoreType.DMA((2, slots, 2, 4)),
    ]
    if top:
        scratch += [pltpu.VMEM((*fold, DIM), BF), pltpu.SemaphoreType.DMA((slots, 2, 4))]
    results = call(
        functools.partial(mlp_grad_kernel, top, split),
        f"grad_mlp_{layer_at}",
        8,
        place,
        args,
        outs,
        scratch,
        out_hbm=range(len(outs)),
    )
    return results[:sides], results[sides:]


def run_attention_grad(layer_at, cuts, place, groups, split, rows_each):
    args = [value for group in groups for value in group]
    sides = 2 if split else 1
    outs = []
    for _, width, _ in cuts:
        outs += grad_shapes(split, rows_each, width)
    fold = (4, 2, rows_each) if split else (1, 1, WIDTH)
    slots = PARTS // sides
    results = call(
        functools.partial(attention_grad_kernel, cuts, split),
        f"grad_attention_{layer_at}",
        5,
        place,
        args,
        outs,
        [
            pltpu.VMEM((slots, *fold, SLAB), BF),
            pltpu.SemaphoreType.DMA((len(cuts), slots, 2, 4)),
        ],
        out_hbm=range(len(outs)),
    )
    return [results[sides * at : sides * (at + 1)] for at in range(len(cuts))]


CORE_SWAP = [(at, at ^ 1) for at in range(PARTS)]
X_SWAP = [(at, at ^ 2) for at in range(PARTS)]
Y_SWAP = [(at, at ^ 1) for at in range(8)]
Z_GROUPS = [[0, 2, 4, 6], [1, 3, 5, 7]]


def added(*terms):
    total = terms[0].astype(F32)
    for term in terms[1:]:
        total = total + term.astype(F32)
    return total


def over_x(value, name):
    with jax.named_scope(f"x_{name}"):
        return lax.ppermute(value, "tensor", X_SWAP)


def over_y(value, name):
    with jax.named_scope(f"y_{name}"):
        return lax.ppermute(value, "dp", Y_SWAP)


def over_core(value, name="pair"):
    with jax.named_scope(f"core_{name}"):
        return lax.ppermute(value, "tensor", CORE_SWAP)


def along_z(value, step, name):
    pairs = [(at, ((at // 2 + step) % 4) * 2 + at % 2) for at in range(8)]
    with jax.named_scope(f"z_{name}_{step}"):
        return lax.ppermute(value, "dp", pairs)


def tied(*values):
    return lax.optimization_barrier(values)


class Reduction:
    def __init__(self, name, pieces, y_first):
        self.name = name
        self.keep, self.send = pieces
        self.first, self.second = (over_y, over_x) if y_first else (over_x, over_y)

    def start(self):
        self.one = self.first(self.send, self.name + "_first")

    def add_second(self):
        with jax.named_scope(f"add_{self.name}_second"):
            self.terms = added(self.keep[1], self.one[1]).astype(BF)

    def start_second(self):
        self.two = self.second(self.terms, self.name + "_second")

    def block(self, step):
        return added(self.keep[0, step], self.one[0, step], self.two[step])


class Column:
    def __init__(self, *items):
        self.items = items
        self.name = "_".join(item.name for item in items)

    def add_third(self):
        with jax.named_scope(f"add_{self.name}_third"):
            self.blocks = [
                jnp.concatenate([item.block(step).astype(BF) for item in self.items], 1)
                for step in range(1, 4)
            ]

    def start_third(self):
        self.arrived = [
            along_z(block, step + 1, self.name) for step, block in enumerate(self.blocks)
        ]

    def totals(self):
        with jax.named_scope(f"add_{self.name}_last"):
            results, at = [], 0
            for item in self.items:
                own = item.block(0)
                end = at + own.shape[1]
                results.append(own + added(*[value[:, at:end] for value in self.arrived]))
                at = end
        return results


def reduce_whole(grads, devices):
    grads = grads.reshape(PARTS, devices, WIDTH // devices, -1)
    grads = jnp.transpose(grads, (1, 0, 2, 3)).reshape(devices * PARTS, WIDTH // devices, -1)
    return lax.psum_scatter(grads, BOTH, scatter_dimension=0, tiled=True)[0].astype(F32)


def total_over_plane(value):
    with jax.named_scope("cross_sums"):
        far = lax.ppermute(value, "tensor", [(at, at ^ 3) for at in range(PARTS)])
    value = (value + over_core(value, "sums")) + (over_x(value, "sums") + far)
    return value + over_y(value, "sums")


def total_over_column(value):
    column = jnp.stack([value, *[along_z(value, step, "sums") for step in range(1, 4)]])
    z_at = lax.axis_index("dp") // 2
    ordered = [
        lax.dynamic_index_in_dim(column, (z_at - at) & 3, 0, keepdims=False) for at in range(4)
    ]
    return (ordered[0] + ordered[1]) + (ordered[2] + ordered[3])


def score_kernel(count, lengths_ref, log_ref, queries_ref, passages_ref, powers_ref, sums_ref, logit_ref):
    queries = queries_ref[...]

    def single(at, carry):
        similar = nt(passages_ref[at], queries)
        spot = lax.broadcasted_iota(jnp.int32, (PLEN, ROWS), 0)
        powers = jnp.where(spot < lengths_ref[at], jnp.exp(SHARPNESS * similar), 0.0)
        powers_ref[at] = powers.astype(BF)
        sums_ref[pl.ds(at, 1), :] = jnp.sum(powers, 0, keepdims=True)
        return carry

    lax.fori_loop(0, count, single, 0)
    smooth = (jnp.log(sums_ref[...]) - log_ref[...]) / SHARPNESS
    token = lax.broadcasted_iota(jnp.int32, (ROWS, DIM), 0) // QLEN
    query = lax.broadcasted_iota(jnp.int32, (ROWS, DIM), 1)
    pick = (token == query).astype(F32)
    logit_ref[...] = SCORE_SCALE * jnp.dot(
        smooth, pick, precision=lax.Precision.HIGHEST, preferred_element_type=F32
    )


def pull_kernel(count, powers_ref, steer_ref, queries_ref, passages_ref, passage_out, query_out, total):
    queries = queries_ref[...]
    total[...] = jnp.zeros_like(total)

    def single(at, carry):
        shares = (powers_ref[at].astype(F32) * steer_ref[pl.ds(at, 1), :]).astype(BF)
        passage_out[at] = nn(shares, queries).astype(BF)
        total[...] += nn(passages_ref[at].T, shares)
        return carry

    lax.fori_loop(0, count, single, 0)
    query_out[...] = total[...].T


def scores_of(queries, passages, lengths):
    count = passages.shape[0]
    return pl.pallas_call(
        functools.partial(score_kernel, count),
        out_shape=[
            shaped((count, PLEN, ROWS), BF),
            shaped((count, ROWS), F32),
            shaped((count, DIM), F32),
        ],
        in_specs=[pl.BlockSpec(memory_space=pltpu.SMEM)] + [vmem_spec()] * 3,
        out_specs=[vmem_spec()] * 3,
        compiler_params=params(),
        cost_estimate=price(4),
        name="scores",
    )(lengths, jnp.log(lengths.astype(F32))[:, None], queries, passages)


def pulls_of(powers, steer, queries, passages):
    count = passages.shape[0]
    return pl.pallas_call(
        functools.partial(pull_kernel, count),
        out_shape=[shaped((count, PLEN, DIM), BF), shaped((ROWS, DIM), F32)],
        in_specs=[vmem_spec()] * 4,
        out_specs=[vmem_spec()] * 2,
        scratch_shapes=[pltpu.VMEM((DIM, ROWS), F32)],
        compiler_params=params(),
        cost_estimate=price(4),
        name="score_pulls",
    )(powers, steer, queries, passages)


def adam_step(master, moment, second, gradient, decay):
    moment_new = BETA_ONE * moment + (1.0 - BETA_ONE) * gradient
    second_new = BETA_TWO * second + (1.0 - BETA_TWO) * gradient * gradient
    rising = moment_new / (1.0 - BETA_ONE**STEP)
    spread = jnp.sqrt(second_new / (1.0 - BETA_TWO**STEP))
    return (moment_new, second_new, -LEARN_RATE * (rising / (spread + ADAM_EPS) + decay * master))


def joined(*pieces):
    return jnp.concatenate([piece.astype(BF) for piece in pieces], 1)


def attention_shard(qkv, out):
    return joined(qkv[0], qkv[1], qkv[2], out.T)


class Gathering:
    def __init__(self, name, shard, x_last):
        self.name = name
        self.shard = shard
        self.plan = ("x_last" if x_last else "y_last", 0)
        self.first, self.second = (over_y, over_x) if x_last else (over_x, over_y)

    def column(self):
        arrived = [along_z(self.shard, step, self.name) for step in range(1, 4)]
        self.held = jnp.stack([self.shard, *arrived])

    def plane(self):
        self.held = jnp.stack([self.held, self.first(self.held, self.name + "_first")])

    def cross(self):
        self.other = self.second(self.held, self.name + "_second")

    def all(self):
        pairs = [over_core(self.held, self.name), over_core(self.other, self.name)]
        return [self.held, self.other, *pairs], self.plan


def gather_whole(shard, devices):
    rows_each = shard.shape[0]
    value = lax.all_gather(shard, BOTH, axis=0, tiled=False)
    if devices == 8:
        return value.reshape(4, 2, PARTS, rows_each, -1)
    value = value.reshape(devices, PARTS, rows_each, -1)
    return jnp.transpose(value, (1, 0, 2, 3)).reshape(1, 1, PARTS, WIDTH, -1)


def whole_weights(value):
    return {
        "att": ([value], ("whole", 0)),
        "up": ([value], ("whole", SLAB)),
        "down": ([value], ("whole", 2 * SLAB)),
        "proj": PACK,
    }


def unpack_grads(att_list, up_list, down_list):
    qkv = jnp.stack(
        [
            jnp.stack([att[:, kind * OWN : (kind + 1) * OWN] for kind in range(3)])
            for att in att_list
        ]
    )
    out = jnp.stack([att[:, 3 * OWN :].T for att in att_list])
    return qkv, out, jnp.stack(up_list), jnp.stack([down[:, :SLAB].T for down in down_list])


def to_output_rows(grad, tensor_at):
    rows = PDEV * PLEN // PARTS
    query_rows = QDEV * QLEN // PARTS
    start = jnp.where(tensor_at == PARTS - 1, 0, ROWS - rows)
    step = lax.ppermute(
        lax.dynamic_slice_in_dim(grad, start, rows, 0).astype(BF),
        "tensor",
        [(at, (at + 1) % PARTS) for at in range(PARTS)],
    ).astype(F32)
    last = PARTS - 1
    sent = grad.astype(BF)
    one = lax.ppermute(sent[query_rows : 2 * query_rows], "tensor", [(last, 1)]).astype(F32)
    two = lax.ppermute(sent[2 * query_rows : 3 * query_rows], "tensor", [(last, 2)]).astype(F32)
    own = grad[last * query_rows :]
    query = jnp.where(
        tensor_at == 0,
        step[:query_rows],
        jnp.where(tensor_at == 1, one, jnp.where(tensor_at == 2, two, own)),
    )
    unit = query_rows
    passage = jnp.where(
        tensor_at == 0,
        grad[:rows],
        jnp.where(
            tensor_at == 1,
            jnp.concatenate([step[2 * unit :], grad[: 2 * unit]]),
            jnp.where(tensor_at == 2, jnp.concatenate([step[unit:], grad[:unit]]), step),
        ),
    )
    return query, passage


def body(
    query_tokens,
    passage_tokens,
    query_mask,
    passage_lengths,
    positives,
    qkv_weight,
    qkv_moment,
    qkv_second,
    out_weight,
    out_moment,
    out_second,
    up_weight,
    up_moment,
    up_second,
    down_weight,
    down_moment,
    down_second,
    projection,
    projection_moment,
    projection_second,
    bias_pair,
    bias_pair_moment,
    bias_pair_second,
    bias_up,
    bias_up_moment,
    bias_up_second,
    norm_terms,
    norm_terms_moment,
    norm_terms_second,
):
    devices = lax.axis_size("dp")
    dev_index = lax.axis_index("dp")
    tensor_at = lax.axis_index("tensor")
    last = PARTS - 1
    is_query = tensor_at == last
    rows_each = WIDTH // devices
    split = devices == 8
    pair_own = jnp.concatenate(
        [
            bias_pair[:, 0],
            jnp.zeros((LAYERS, OWN), F32),
            bias_pair[:, 1],
            jnp.zeros((LAYERS, HELD - 3 * OWN), F32),
        ],
        -1,
    )
    small = jnp.concatenate([pair_own, bias_up], -1)
    if split:
        crossed = over_x(small, "biases")
        small_all = [small, crossed, over_core(small, "biases"), over_core(crossed, "biases")]
        small_all = jnp.stack(small_all)
    else:
        small_all = lax.all_gather(small, "tensor", axis=0, tiled=False)

    shards = [
        (
            attention_shard(qkv_weight[at], out_weight[at]),
            up_weight[at].astype(BF),
            down_weight[at].T.astype(BF),
        )
        for at in range(LAYERS)
    ]
    if split:
        last_layer = whole_weights(gather_whole(joined(*shards[1], projection), devices))
        att = Gathering("att_0", shards[0][0], False)
        up = Gathering("up_0", shards[0][1], True)
        down = Gathering("down_0", shards[0][2], False)
        att.column()
        att.held, up.shard, down.shard, small_all = tied(
            att.held, up.shard, down.shard, small_all
        )
        att.plane()
        up.column()
        down.column()
        up.plane()
        down.plane()
        att.cross()
        up.cross()
        down.cross()
        first_layer = {"att": att.all()}
    else:
        first_layer = whole_weights(gather_whole(joined(*shards[0]), devices))
        last_layer = whole_weights(gather_whole(joined(*shards[1], projection), devices))
    weights = [first_layer, last_layer]
    for layer in weights:
        layer["fold"] = (4, 2, rows_each) if split else (1, 1, WIDTH)
    pair_rows = small_all[:, :, None, :HELD]
    up_all = small_all[:, :, None, HELD:]
    passage_at = jnp.minimum(tensor_at, last - 1)
    own_passage = lax.dynamic_slice_in_dim(passage_tokens, passage_at * PLEN, PLEN, 0)
    hidden = jnp.where(is_query, query_tokens, own_passage)
    own_length = lax.dynamic_slice_in_dim(passage_lengths, dev_index * PDEV + passage_at, 1, 0)
    spot = jnp.arange(ROWS, dtype=jnp.int32)
    key_valid = jnp.where(is_query, query_mask.reshape(ROWS) == 1, spot < own_length)
    together = jnp.logical_or(
        jnp.logical_not(is_query), spot[:, None] // QLEN == spot[None, :] // QLEN
    )
    mask = jnp.where(jnp.logical_and(key_valid[:, None], together), 0.0, MASKED).astype(F32)

    place = jnp.stack([tensor_at // 2, tensor_at % 2, dev_index % 2, dev_index // 2]).astype(jnp.int32)

    def sides_of(keep, send):
        return [keep, over_core(send)] if split else [keep]

    def shared(value):
        return [value, over_core(value)] if split else [value]

    saved_list = []
    for layer_at in range(LAYERS):
        outs = run_attention(
            layer_at,
            place,
            hidden,
            mask,
            pair_rows[:, layer_at],
            norm_terms[layer_at],
            weights[layer_at],
            split,
        )
        first, x_t, packed, chances, normal_one, factor_one, first_t = outs[:7]
        if split and layer_at == 0:
            first, up.held, up.other, down.held, down.other = tied(
                first, up.held, up.other, down.held, down.other
            )
            weights[0].update(up=up.all(), down=down.all())
        mixtures = sides_of(outs[7], outs[-1])
        outs = run_mlp(
            layer_at,
            place,
            first,
            up_all[:, layer_at],
            norm_terms[layer_at],
            weights[layer_at],
            split,
            devices,
        )
        hidden, slope, normal_two, factor_two = outs[:4]
        acts = sides_of(outs[4], outs[5 if split else 4])
        saved_list.append(
            dict(
                mlp=(slope, normal_two, factor_two),
                attention=(packed, chances, normal_one, factor_one),
                x_t=shared(x_t),
                first_t=shared(first_t),
                mixtures=mixtures,
                acts=acts,
            )
        )
    embedding, unit, scale, top_t = outs[-4:]

    passages = lax.all_to_all(embedding, "dp", 0, 0, tiled=True)
    embedding = embedding[0]
    queries = embedding
    arrived = [lax.ppermute(embedding, "tensor", [(last, at)]) for at in range(last)]
    for at in range(last):
        queries = jnp.where(tensor_at == at, arrived[at], queries)
    length_table = passage_lengths.reshape(devices, PDEV)
    own_lengths = lax.dynamic_slice_in_dim(length_table, passage_at, 1, 1)[:, 0]
    powers, sums, logit_part = scores_of(queries, passages, own_lengths)
    logits = lax.all_gather(logit_part[:, :QDEV], "tensor", axis=0, tiled=False)[:last]
    own_positives = lax.dynamic_slice_in_dim(positives, dev_index * QDEV, QDEV, 0)
    ids = (
        lax.broadcasted_iota(jnp.int32, logits.shape, 1) * PDEV
        + lax.broadcasted_iota(jnp.int32, logits.shape, 0)
    )
    chosen = ids == own_positives[None, None, :]
    highest = jnp.max(logits, (0, 1), keepdims=True)
    raised = jnp.exp(logits - highest)
    summed = jnp.sum(raised, (0, 1), keepdims=True)
    losses = highest + jnp.log(summed) - jnp.sum(jnp.where(chosen, logits, 0.0), (0, 1), keepdims=True)
    deltas = raised / summed - chosen.astype(F32)
    own_deltas = lax.dynamic_slice_in_dim(deltas, passage_at, 1, 0)[0]
    steer = jnp.where(is_query, 0.0, SCORE_SCALE) * jnp.repeat(own_deltas, QLEN, axis=1) / sums
    passage_terms, query_terms = pulls_of(powers, steer, queries, passages)
    passage_back = lax.all_to_all(passage_terms, "dp", 0, 0, tiled=True)
    grad_passage = jnp.sum(passage_back.astype(F32), 0)
    returned = [lax.ppermute(query_terms, "tensor", [(at, last)]) for at in range(last)]
    grad_query = returned[0] + returned[1] + returned[2]
    grad_emb = jnp.where(is_query, grad_query, grad_passage)

    upstream = (grad_emb, unit, scale, top_t)
    mlp_sums, attention_sums = [None] * LAYERS, [None] * LAYERS

    def stacked_sums():
        loss_part = jnp.where(tensor_at == 0, jnp.sum(losses), 0.0)
        sums = jnp.stack([attention_sums[0], mlp_sums[0], attention_sums[1], mlp_sums[1]])
        row_ids = lax.broadcasted_iota(jnp.int32, sums.shape, 1)
        sums = sums + jnp.where(row_ids == 7, loss_part, 0.0)
        return sums

    def mlp_pull(layer_at, upstream):
        saved = saved_list[layer_at]
        outs = run_mlp_pull(
            layer_at, place, upstream, saved["mlp"], norm_terms[layer_at], weights[layer_at], split
        )
        grad_first, mlp_sums[layer_at], low_t = outs[:3]
        groups = [
            saved["first_t"],
            sides_of(outs[3], outs[4 if split else 3]),
            shared(low_t),
            saved["acts"],
        ]
        if layer_at == LAYERS - 1:
            groups.append(shared(outs[-1]))
        return grad_first, groups

    def attention_pull(layer_at, grad_first):
        saved = saved_list[layer_at]
        outs = run_attention_pull(
            layer_at,
            place,
            grad_first,
            saved["attention"],
            norm_terms[layer_at],
            weights[layer_at],
            split,
        )
        dx, attention_sums[layer_at], low_t = outs[:3]
        return dx, [
            saved["x_t"],
            sides_of(outs[3], outs[-1]),
            shared(low_t),
            saved["mixtures"],
        ]

    def mlp_grad(layer_at, groups):
        return run_mlp_grad(layer_at, place, groups, split, rows_each)

    def attention_grad(layer_at, cuts, groups):
        return run_attention_grad(layer_at, cuts, place, groups, split, rows_each)

    if split:
        grad_first, mlp_groups = mlp_pull(1, upstream)
        up_grads, down_grads = mlp_grad(1, mlp_groups)
        up_one, down_one = Reduction("up_1", up_grads, False), Reduction("down_1", down_grads, True)
        grad_first, up_one.send, down_one.send = tied(grad_first, up_one.send, down_one.send)
        up_one.start()
        down_one.start()
        dx, att_groups = attention_pull(1, grad_first)
        att_one = Reduction("att_1", attention_grad(1, ((0, SLAB, False),), att_groups)[0], False)
        dx, att_one.send = tied(dx, att_one.send)
        att_one.start()
        grad_first, mlp_groups = mlp_pull(0, (dx,))
        up_one.add_second()
        down_one.add_second()
        mlp_groups[0][0], up_one.terms, down_one.terms = tied(
            mlp_groups[0][0], up_one.terms, down_one.terms
        )
        up_one.start_second()
        down_one.start_second()
        up_grads, down_grads = mlp_grad(0, mlp_groups)
        up_zero = Reduction("up_0", up_grads, False)
        down_zero = Reduction("down_0", down_grads, True)
        grad_first, up_zero.send, down_zero.send = tied(grad_first, up_zero.send, down_zero.send)
        up_zero.start()
        down_zero.start()
        dx, att_groups = attention_pull(0, grad_first)
        dx, att_one.one = tied(dx, att_one.one)
        att_one.add_second()
        att_groups[0][0], att_one.terms = tied(att_groups[0][0], att_one.terms)
        att_one.start_second()
        mlp_one = Column(up_one, down_one)
        mlp_one.add_third()
        up_zero.add_second()
        down_zero.add_second()
        att_groups[0][0], up_zero.terms, down_zero.terms = tied(
            att_groups[0][0], up_zero.terms, down_zero.terms
        )
        half = SLAB // 2
        left, right = attention_grad(0, ((0, half, False), (half, half, True)), att_groups)
        halves = (Reduction("qk_0", left, False), Reduction("vo_0", right, True))
        column_one = Column(att_one)
        mlp_one.start_third()
        column_one.add_third()
        column_one.start_third()
        for item in (up_zero, down_zero):
            item.start_second()
        qk_zero, vo_zero = halves
        up_zero.two, down_zero.two, qk_zero.send, vo_zero.send = tied(
            up_zero.two, down_zero.two, qk_zero.send, vo_zero.send
        )
        for item in halves:
            item.start()
        mlp_zero = Column(up_zero, down_zero)
        mlp_zero.add_third()
        mlp_zero.start_third()
        for item in halves:
            item.add_second()
        attention_sums[0], dx, qk_zero.terms, vo_zero.terms = tied(
            attention_sums[0], dx, qk_zero.terms, vo_zero.terms
        )
        for item in halves:
            item.start_second()
        sums = total_over_plane(stacked_sums())
        sums, qk_zero.two, vo_zero.two = tied(sums, qk_zero.two, vo_zero.two)
        column_zero = Column(qk_zero, vo_zero)
        column_zero.add_third()
        column_zero.start_third()
        sums = total_over_column(sums)
        att_list = [jnp.concatenate(column_zero.totals(), 1), *column_one.totals()]
        (up_grad_zero, down_grad_zero), (up_grad_one, down_grad_one) = (
            mlp_zero.totals(),
            mlp_one.totals(),
        )
        up_list, down_list = [up_grad_zero, up_grad_one], [down_grad_zero, down_grad_one]
    else:
        att_list, up_list, down_list = [], [], []
        dx = None
        for layer_at in range(LAYERS - 1, -1, -1):
            grad_first, groups = mlp_pull(layer_at, (dx,) if upstream is None else upstream)
            upstream = None
            up_grads, down_grads = mlp_grad(layer_at, groups)
            dx, groups = attention_pull(layer_at, grad_first)
            att_grads = attention_grad(layer_at, ((0, SLAB, False),), groups)[0]
            up_list.insert(0, reduce_whole(up_grads[0], devices))
            down_list.insert(0, reduce_whole(down_grads[0], devices))
            att_list.insert(0, reduce_whole(att_grads[0], devices))
        sums = lax.psum(stacked_sums(), BOTH)
    sums = sums.reshape(LAYERS, 2, 8, WIDTH)
    norms_grad = sums[:, :, :3].reshape(LAYERS, 6, WIDTH)
    own_sums = lax.dynamic_slice_in_dim(sums, 3 + tensor_at, 1, 2)[:, :, 0]
    pair_grad = jnp.stack([own_sums[:, 0, :OWN], own_sums[:, 0, 2 * OWN : 3 * OWN]], 1)
    bias_grad = own_sums[:, 1]
    loss_mean = sums[0, 0, 7, 0] / (QDEV * devices)
    projection_grad = down_list[LAYERS - 1][:, SLAB:]
    qkv_grad, out_grad, up_grad, down_grad = unpack_grads(att_list, up_list, down_list)
    qkv_m, qkv_v, qkv_u = adam_step(qkv_weight, qkv_moment, qkv_second, qkv_grad, WEIGHT_DECAY)
    out_m, out_v, out_u = adam_step(out_weight, out_moment, out_second, out_grad, WEIGHT_DECAY)
    up_m, up_v, up_u = adam_step(up_weight, up_moment, up_second, up_grad, WEIGHT_DECAY)
    down_m, down_v, down_u = adam_step(
        down_weight, down_moment, down_second, down_grad, WEIGHT_DECAY
    )
    proj_m, proj_v, proj_u = adam_step(
        projection, projection_moment, projection_second, projection_grad, WEIGHT_DECAY
    )
    pair_m, pair_v, pair_u = adam_step(
        bias_pair, bias_pair_moment, bias_pair_second, pair_grad, 0.0
    )
    bias_m, bias_v, bias_u = adam_step(bias_up, bias_up_moment, bias_up_second, bias_grad, 0.0)
    norm_m, norm_v, norm_u = adam_step(
        norm_terms, norm_terms_moment, norm_terms_second, norms_grad, 0.0
    )
    query_grad, passage_grad = to_output_rows(dx, tensor_at)
    return (
        loss_mean,
        query_grad,
        passage_grad,
        qkv_grad,
        qkv_m,
        qkv_v,
        qkv_u,
        out_grad,
        out_m,
        out_v,
        out_u,
        up_grad,
        up_m,
        up_v,
        up_u,
        down_grad,
        down_m,
        down_v,
        down_u,
        projection_grad,
        proj_m,
        proj_v,
        proj_u,
        pair_grad,
        pair_m,
        pair_v,
        pair_u,
        bias_grad,
        bias_m,
        bias_v,
        bias_u,
        norms_grad,
        norm_m,
        norm_v,
        norm_u,
    )


def solution(mesh):
    placed = (
        P("dp", None),
        P("dp", None),
        P("dp", None),
        P(),
        P(),
        P(None, None, "dp", "tensor"),
        P(None, None, "dp", "tensor"),
        P(None, None, "dp", "tensor"),
        P(None, "tensor", "dp"),
        P(None, "tensor", "dp"),
        P(None, "tensor", "dp"),
        P(None, "dp", "tensor"),
        P(None, "dp", "tensor"),
        P(None, "dp", "tensor"),
        P(None, "tensor", "dp"),
        P(None, "tensor", "dp"),
        P(None, "tensor", "dp"),
        P("dp", None),
        P("dp", None),
        P("dp", None),
        P(None, None, "tensor"),
        P(None, None, "tensor"),
        P(None, None, "tensor"),
        P(None, "tensor"),
        P(None, "tensor"),
        P(None, "tensor"),
        P(),
        P(),
        P(),
    )
    return jax.shard_map(
        body,
        mesh=mesh,
        in_specs=placed,
        out_specs=(
            P(),
            P(("dp", "tensor"), None),
            P(("dp", "tensor"), None),
            P(None, None, "dp", "tensor"),
            P(None, None, "dp", "tensor"),
            P(None, None, "dp", "tensor"),
            P(None, None, "dp", "tensor"),
            P(None, "tensor", "dp"),
            P(None, "tensor", "dp"),
            P(None, "tensor", "dp"),
            P(None, "tensor", "dp"),
            P(None, "dp", "tensor"),
            P(None, "dp", "tensor"),
            P(None, "dp", "tensor"),
            P(None, "dp", "tensor"),
            P(None, "tensor", "dp"),
            P(None, "tensor", "dp"),
            P(None, "tensor", "dp"),
            P(None, "tensor", "dp"),
            P("dp", None),
            P("dp", None),
            P("dp", None),
            P("dp", None),
            P(None, None, "tensor"),
            P(None, None, "tensor"),
            P(None, None, "tensor"),
            P(None, None, "tensor"),
            P(None, "tensor"),
            P(None, "tensor"),
            P(None, "tensor"),
            P(None, "tensor"),
            P(),
            P(),
            P(),
            P(),
        ),
        check_vma=False,
    )
```

```python
import functools

import jax
import jax.numpy as jnp
from jax import lax
from jax.experimental import pallas as pl
from jax.experimental.pallas import tpu as pltpu
from jax.sharding import PartitionSpec as P

WIDTH = 768
HEAD = 64
DIM = 128
QLEN = 32
PLEN = 256
LAYERS = 2
STEP = 10
QDEV = 8
PDEV = 3
ROWS = 256
PARTS = 4
HEADS_EACH = 3
OWN = HEADS_EACH * HEAD
SLAB = 768
HELD = 640
PACK = 3 * SLAB

MASKED = -1e30
SHARPNESS = 24.0
SCORE_SCALE = 4.0
LN_EPS = 1e-12
NORM_EPS = 1e-12
BETA_ONE = 0.9
BETA_TWO = 0.999
ADAM_EPS = 1e-08
LEARN_RATE = 0.02
WEIGHT_DECAY = 0.01
VMEM_BYTES = 60 * 1024 * 1024

BF = jnp.bfloat16
F32 = jnp.float32
BOTH = ("dp", "tensor")


def nn(left, right):
    return jnp.dot(left, right, preferred_element_type=F32)


def nt(left, right):
    return lax.dot_general(left, right, (((1,), (1,)), ((), ())), preferred_element_type=F32)


def norm_forward(values):
    average = jnp.mean(values, -1, keepdims=True)
    centred = values - average
    factor = lax.rsqrt(jnp.mean(centred * centred, -1, keepdims=True) + LN_EPS)
    return centred * factor, factor


def norm_backward(upstream, normal, factor, gains):
    scaled = upstream * gains
    average = jnp.mean(scaled, -1, keepdims=True)
    cross = jnp.mean(scaled * normal, -1, keepdims=True)
    return factor * (scaled - average - normal * cross)


def column_sum(values):
    return jnp.sum(values.astype(F32), 0, keepdims=True)


def part_order(place, split):
    if not split:
        return list(range(PARTS))
    x_at, c_at = place[0], place[1]
    return [
        (x_at ^ x_rel) * 2 + (c_at ^ c_rel) for c_rel in range(2) for x_rel in range(2)
    ]


class Copies:
    def __init__(self, copies):
        self.copies = copies

    def start(self):
        for copy in self.copies:
            copy.start()

    def wait(self):
        for copy in self.copies:
            copy.wait()


def weight_copies(refs, plan, held, sems, parts, place):
    kind, base = plan
    groups = []
    for slot, part in enumerate(parts):
        copies = []
        if kind == "whole":
            source = refs[0].at[:, :, part, :, pl.ds(base, SLAB)]
            copies.append(pltpu.make_async_copy(source, held.at[slot], sems.at[slot, 0]))
        else:
            c_rel, x_rel = divmod(slot, 2)
            for y_rel in range(2):
                outer, inner = (x_rel, y_rel) if kind == "x_last" else (y_rel, x_rel)
                for back in range(4):
                    copies.append(
                        pltpu.make_async_copy(
                            refs[2 * c_rel + outer].at[inner, back],
                            held.at[slot, (place[3] - back) & 3, place[2] ^ y_rel],
                            sems.at[slot, 4 * y_rel + back],
                        )
                    )
        groups.append(Copies(copies))
    return groups


def projection_copy(w_ref, proj, sem, base):
    return pltpu.make_async_copy(w_ref.at[:, :, 0, :, pl.ds(base, DIM)], proj, sem)


def stored(refs, slot, value):
    refs[slot // 2 if len(refs) > 1 else 0][slot % 2 if len(refs) > 1 else slot] = value


def attention_kernel(plan, count, split, place, *refs):
    x_ref, mask_ref, pair_ref, norm_ref = refs[:4]
    w_refs, refs = refs[4 : 4 + count], refs[4 + count :]
    first_ref, low_t_ref, packed_ref, chances_ref, normal_ref, factor_ref, first_t_ref = refs[:7]
    mixture_refs = refs[7:-2]
    held, sems = refs[-2:]
    parts = part_order(place, split)
    copies = weight_copies(w_refs, plan, held, sems, parts, place)
    for copy in copies:
        copy.start()
    hidden = x_ref[...]
    low = hidden.astype(BF)
    low_t_ref[...] = low.T
    mask = mask_ref[...]
    attended = jnp.zeros((ROWS, WIDTH), F32)
    for slot in range(PARTS):
        copies[slot].wait()
        weight = held[slot, :, :, :, :HELD].reshape(WIDTH, HELD)
        packed = (nn(low, weight) + pair_ref[slot]).astype(BF)
        packed_ref[slot] = packed
        values_t = packed[:, 2 * OWN : 3 * OWN].T
        mixed = [jnp.zeros((HEAD, ROWS), F32)]
        for head in range(HEADS_EACH):
            queries = packed[:, head * HEAD : (head + 1) * HEAD]
            keys = packed[:, OWN + head * HEAD : OWN + (head + 1) * HEAD]
            scores = nt(keys, queries) * 0.125 + mask
            powers = jnp.exp(scores - jnp.max(scores, 0, keepdims=True))
            chances = (powers * (1.0 / jnp.sum(powers, 0, keepdims=True))).astype(BF)
            chances_ref[slot * HEADS_EACH + head] = chances
            mixed.append(nn(values_t[head * HEAD : (head + 1) * HEAD], chances))
        mixture = jnp.concatenate(mixed, 0).astype(BF).T
        stored(mixture_refs, slot, mixture)
        attended = attended + nt(
            mixture, held[slot, :, :, :, SLAB - ROWS :].reshape(WIDTH, ROWS)
        )
    normal, factor = norm_forward(hidden + attended + norm_ref[0:1])
    normal_ref[...] = normal
    factor_ref[...] = jnp.broadcast_to(factor, factor_ref.shape)
    first = normal * norm_ref[1:2] + norm_ref[2:3]
    first_ref[...] = first
    first_t_ref[...] = first.astype(BF).T


def mlp_kernel(up_plan, down_plan, proj_base, count, top, split, place, *refs):
    first_ref, up_bias_ref, norm_ref = refs[:3]
    up_refs, down_refs = refs[3 : 3 + count], refs[3 + count : 3 + 2 * count]
    refs = refs[3 + 2 * count :]
    out_ref, slope_ref, normal_ref, factor_ref = refs[:4]
    act_refs = refs[4 : 6 if split else 5]
    refs = refs[4 + len(act_refs) :]
    if top:
        emb_ref, unit_ref, scale_ref, top_t_ref = refs[:4]
        refs = refs[4:]
    up_held, down_held, up_sems, down_sems = refs[:4]
    parts = part_order(place, split)
    ups = weight_copies(up_refs, up_plan, up_held, up_sems, parts, place)
    downs = weight_copies(down_refs, down_plan, down_held, down_sems, parts, place)
    for slot in range(PARTS):
        ups[slot].start()
        downs[slot].start()
    if top:
        proj, proj_sem = refs[4:]
        proj_load = projection_copy(up_refs[0], proj, proj_sem, proj_base)
        proj_load.start()
    first = first_ref[...]
    first_low = first.astype(BF)
    spread = jnp.zeros((ROWS, WIDTH), F32)
    for slot in range(PARTS):
        ups[slot].wait()
        pre_act = nn(first_low, up_held[slot].reshape(WIDTH, SLAB)) + up_bias_ref[slot]
        chance = 0.5 * (1.0 + lax.erf(pre_act * 0.7071067811865476))
        act = (pre_act * chance).astype(BF)
        stored(act_refs, slot, act)
        slope_ref[slot] = (
            chance + pre_act * jnp.exp(-0.5 * pre_act * pre_act) * 0.3989422804014327
        ).astype(BF)
        downs[slot].wait()
        spread = spread + nt(act, down_held[slot].reshape(WIDTH, SLAB))
    normal, factor = norm_forward(first + spread + norm_ref[3:4])
    normal_ref[...] = normal
    factor_ref[...] = jnp.broadcast_to(factor, factor_ref.shape)
    second = normal * norm_ref[4:5] + norm_ref[5:6]
    out_ref[...] = second
    if top:
        second_low = second.astype(BF)
        top_t_ref[...] = second_low.T
        proj_load.wait()
        embedded = nn(second_low, proj[...].reshape(WIDTH, DIM))
        scale = lax.rsqrt(jnp.sum(embedded * embedded, -1, keepdims=True) + NORM_EPS)
        unit = embedded * scale
        unit_ref[...] = unit
        emb_ref[...] = jnp.broadcast_to(unit.astype(BF)[None], emb_ref.shape)
        scale_ref[...] = jnp.broadcast_to(scale, scale_ref.shape)


def mlp_pull_kernel(up_plan, down_plan, proj_base, count, top, split, place, *refs):
    if top:
        grad_emb_ref, unit_ref, scale_ref, top_t_ref = refs[:4]
        refs = refs[4:]
    else:
        dy_ref = refs[0]
        refs = refs[1:]
    slope_ref, normal_ref, factor_ref, norm_ref = refs[:4]
    up_refs, down_refs = refs[4 : 4 + count], refs[4 + count : 4 + 2 * count]
    refs = refs[4 + 2 * count :]
    grad_ref, sum_ref, low_t_ref = refs[:3]
    pre_refs = refs[3 : 5 if split else 4]
    refs = refs[3 + len(pre_refs) :]
    if top:
        proj_grad_ref = refs[0]
        refs = refs[1:]
    up_held, down_held, up_sems, down_sems = refs[:4]
    parts = part_order(place, split)
    ups = weight_copies(up_refs, up_plan, up_held, up_sems, parts, place)
    downs = weight_copies(down_refs, down_plan, down_held, down_sems, parts, place)
    if top:
        proj, proj_sem = refs[4:]
        proj_load = projection_copy(up_refs[0], proj, proj_sem, proj_base)
        proj_load.start()
    order = (2, 3, 0, 1) if split else (0, 1, 2, 3)
    for slot in order:
        downs[slot].start()
        ups[slot].start()
    if top:
        grad_emb = grad_emb_ref[...]
        unit = unit_ref[...]
        low_emb = (
            scale_ref[:, :1] * (grad_emb - unit * jnp.sum(grad_emb * unit, -1, keepdims=True))
        ).astype(BF)
        proj_grad_ref[...] = nn(top_t_ref[...], low_emb)
        proj_load.wait()
        dy = nt(low_emb, proj[...].reshape(WIDTH, DIM))
    else:
        dy = dy_ref[...]
    normal = normal_ref[...]
    grad_two = norm_backward(dy, normal, factor_ref[:, :1], norm_ref[4:5])
    sum_ref[0:1] = column_sum(grad_two)
    sum_ref[1:2] = column_sum(dy * normal)
    sum_ref[2:3] = column_sum(dy)
    sum_ref[7:8] = jnp.zeros((1, WIDTH), F32)
    low = grad_two.astype(BF)
    low_t_ref[...] = low.T
    grad_first = grad_two
    for slot in order:
        downs[slot].wait()
        grad_act = nn(low, down_held[slot].reshape(WIDTH, SLAB))
        pre_low = (grad_act * slope_ref[slot].astype(F32)).astype(BF)
        sum_ref[pl.ds(3 + parts[slot], 1), :] = column_sum(pre_low)
        stored(pre_refs, slot, pre_low)
        ups[slot].wait()
        grad_first = grad_first + nt(pre_low, up_held[slot].reshape(WIDTH, SLAB))
    grad_ref[...] = grad_first


def attention_pull_kernel(plan, count, split, place, *refs):
    grad_first_ref, packed_ref, chances_ref, normal_ref, factor_ref, norm_ref = refs[:6]
    w_refs, refs = refs[6 : 6 + count], refs[6 + count :]
    dx_ref, sum_ref, low_t_ref = refs[:3]
    packed_grad_refs = refs[3:-2]
    held, sems = refs[-2:]
    parts = part_order(place, split)
    copies = weight_copies(w_refs, plan, held, sems, parts, place)
    order = (2, 3, 0, 1) if split else (0, 1, 2, 3)
    for slot in order:
        copies[slot].start()
    normal = normal_ref[...]
    grad_first = grad_first_ref[...]
    grad_one = norm_backward(grad_first, normal, factor_ref[:, :1], norm_ref[1:2])
    sum_ref[0:1] = column_sum(grad_one)
    sum_ref[1:2] = column_sum(grad_first * normal)
    sum_ref[2:3] = column_sum(grad_first)
    sum_ref[7:8] = jnp.zeros((1, WIDTH), F32)
    low = grad_one.astype(BF)
    low_t_ref[...] = low.T
    grad_input = grad_one
    for slot in order:
        copies[slot].wait()
        grad_mix = nn(low, held[slot, :, :, :, SLAB - ROWS :].reshape(WIDTH, ROWS)).astype(BF)
        packed = packed_ref[slot]
        keys_t = packed[:, OWN : 2 * OWN].T
        grad_queries, grad_keys, grad_values = [], [], []
        for head in range(HEADS_EACH):
            queries = packed[:, head * HEAD : (head + 1) * HEAD]
            values = packed[:, 2 * OWN + head * HEAD : 2 * OWN + (head + 1) * HEAD]
            upstream = grad_mix[:, (head + 1) * HEAD : (head + 2) * HEAD]
            chances = chances_ref[slot * HEADS_EACH + head]
            grad_values.append(nn(chances, upstream).astype(BF))
            wide = chances.astype(F32)
            product = wide * nt(values, upstream)
            grad_scores = (product - wide * jnp.sum(product, 0, keepdims=True)).astype(BF)
            grad_keys.append((nn(grad_scores, queries) * 0.125).astype(BF))
            grad_queries.append(nn(keys_t[head * HEAD : (head + 1) * HEAD], grad_scores) * 0.125)
        grad_packed = jnp.concatenate(
            [jnp.concatenate(grad_queries, 0).astype(BF).T]
            + grad_keys
            + grad_values
            + [jnp.zeros((ROWS, SLAB - 3 * OWN), BF)],
            1,
        )
        sum_ref[pl.ds(3 + parts[slot], 1), :] = column_sum(grad_packed)
        stored(packed_grad_refs, slot, grad_packed)
        grad_input = grad_input + nt(grad_packed, held[slot].reshape(WIDTH, SLAB))
    dx_ref[...] = grad_input


def rows_of(refs):
    return jnp.concatenate([ref[...] for ref in refs], 1)


def rows_at(refs, slot):
    return jnp.concatenate([ref[slot] for ref in refs], 0)


def block_sends(stage, slot, targets, sems, place, y_first, base, start=0, width=None):
    width = stage.shape[-1] if width is None else width
    lanes, taken = pl.ds(base, width), pl.ds(start, width)
    if len(targets) == 1:
        copies = [
            pltpu.make_async_copy(
                stage.at[0, 0, :, taken], targets[0].at[slot, :, lanes], sems.at[0, 0]
            )
        ]
    else:
        copies = []
        for y_rel in range(2):
            first, second = (y_rel, slot) if y_first else (slot, y_rel)
            for z_rel in range(4):
                copies.append(
                    pltpu.make_async_copy(
                        stage.at[(place[3] + z_rel) & 3, place[2] ^ y_rel, :, taken],
                        targets[first].at[second, z_rel, :, lanes],
                        sems.at[y_rel, z_rel],
                    )
                )
    for copy in copies:
        copy.start()
    return copies


def mlp_grad_kernel(top, split, place, *refs):
    sides = 2 if split else 1
    groups = []
    for _ in range(4):
        groups.append(refs[:sides])
        refs = refs[sides:]
    first_t_refs, pre_refs, low_t_refs, act_refs = groups
    if top:
        proj_refs, refs = refs[:sides], refs[sides:]
    up_targets, refs = refs[:sides], refs[sides:]
    down_targets, refs = refs[:sides], refs[sides:]
    stage, sems = refs[:2]
    fold = stage.shape[2:]
    slots = PARTS // sides
    sends = []
    if top:
        proj_stage, proj_sems = refs[2:]
        total = proj_refs[0][...]
        for ref in proj_refs[1:]:
            total = total + ref[...]
        proj_stage[...] = total.astype(BF).reshape(proj_stage.shape)
        for slot in range(slots):
            sends += block_sends(
                proj_stage, slot, down_targets, proj_sems.at[slot], place, True, SLAB
            )
    first_t = rows_of(first_t_refs)
    low_t = rows_of(low_t_refs)
    for slot in reversed(range(slots)):
        stage[0, slot] = nn(first_t, rows_at(pre_refs, slot)).astype(BF).reshape(*fold)
        sends += block_sends(stage.at[0, slot], slot, up_targets, sems.at[0, slot], place, False, 0)
        stage[1, slot] = nn(low_t, rows_at(act_refs, slot)).astype(BF).reshape(*fold)
        sends += block_sends(stage.at[1, slot], slot, down_targets, sems.at[1, slot], place, True, 0)
    for copy in sends:
        copy.wait()


def attention_grad_kernel(cuts, split, place, *refs):
    sides = 2 if split else 1
    groups = []
    for _ in range(4):
        groups.append(refs[:sides])
        refs = refs[sides:]
    x_t_refs, packed_refs, low_t_refs, mixture_refs = groups
    targets = []
    for _ in cuts:
        targets.append(refs[:sides])
        refs = refs[sides:]
    stage, sems = refs
    fold = stage.shape[1:]
    sends = []
    x_t = rows_of(x_t_refs)
    low_t = rows_of(low_t_refs)
    for slot in reversed(range(PARTS // sides)):
        grad_weight = nn(x_t, rows_at(packed_refs, slot))
        grad_out = nn(low_t, rows_at(mixture_refs, slot))
        stage[slot] = (
            jnp.concatenate(
                [grad_weight[:, : SLAB - ROWS], grad_weight[:, SLAB - ROWS :] + grad_out], 1
            )
            .astype(BF)
            .reshape(*fold)
        )
        for at, (start, width, y_first) in enumerate(cuts):
            sends += block_sends(
                stage.at[slot], slot, targets[at], sems.at[at, slot], place, y_first, 0, start, width
            )
    for copy in sends:
        copy.wait()


def any_spec():
    return pl.BlockSpec(memory_space=pl.ANY)


def vmem_spec():
    return pl.BlockSpec(memory_space=pltpu.VMEM)


def shaped(shape, kind):
    return jax.ShapeDtypeStruct(shape, kind)


def price(micros):
    return pl.CostEstimate(
        flops=int(micros * 1e6), bytes_accessed=int(micros * 3e3), transcendentals=0
    )


def params():
    return pltpu.CompilerParams(vmem_limit_bytes=VMEM_BYTES)


def smem_spec():
    return pl.BlockSpec(memory_space=pltpu.SMEM)


def sided(split, shape, kind):
    if split:
        return [shaped((2, *shape), kind)] * 2
    return [shaped((PARTS, *shape), kind)]


def held_scratch(fold, count):
    return [pltpu.VMEM((PARTS, *fold, SLAB), BF)] * count + [
        pltpu.SemaphoreType.DMA((PARTS, 8))
    ] * count


def projection_scratch(fold):
    return [pltpu.VMEM((*fold, DIM), BF), pltpu.SemaphoreType.DMA]


def call(kernel, name, micros, place, args, outs, scratch, in_hbm=(), out_hbm=()):
    return pl.pallas_call(
        kernel,
        out_shape=outs,
        in_specs=[smem_spec()]
        + [any_spec() if at in in_hbm else vmem_spec() for at in range(len(args))],
        out_specs=[any_spec() if at in out_hbm else vmem_spec() for at in range(len(outs))],
        scratch_shapes=scratch,
        compiler_params=params(),
        cost_estimate=price(micros),
        name=name,
    )(place, *args)


def run_attention(layer_at, place, hidden, mask, pair_rows, norms, weights, split):
    arrays, plan = weights["att"]
    outs = [
        shaped((ROWS, WIDTH), F32),
        shaped((WIDTH, ROWS), BF),
        shaped((PARTS, ROWS, HELD), BF),
        shaped((PARTS * HEADS_EACH, ROWS, ROWS), BF),
        shaped((ROWS, WIDTH), F32),
        shaped((ROWS, DIM), F32),
        shaped((WIDTH, ROWS), BF),
    ] + sided(split, (ROWS, ROWS), BF)
    args = [hidden, mask, pair_rows, norms, *arrays]
    return call(
        functools.partial(attention_kernel, plan, len(arrays), split),
        f"attention_{layer_at}",
        9,
        place,
        args,
        outs,
        held_scratch(weights["fold"], 1),
        in_hbm=range(4, len(args)),
    )


def run_mlp(layer_at, place, first, up_rows, norms, weights, split, copies):
    top = layer_at == LAYERS - 1
    ups, up_plan = weights["up"]
    downs, down_plan = weights["down"]
    outs = [
        shaped((ROWS, WIDTH), F32),
        shaped((PARTS, ROWS, SLAB), BF),
        shaped((ROWS, WIDTH), F32),
        shaped((ROWS, DIM), F32),
    ] + sided(split, (ROWS, SLAB), BF)
    scratch = held_scratch(weights["fold"], 2)
    if top:
        outs += [
            shaped((copies, ROWS, DIM), BF),
            shaped((ROWS, DIM), F32),
            shaped((ROWS, DIM), F32),
            shaped((WIDTH, ROWS), BF),
        ]
        scratch += projection_scratch(weights["fold"])
    args = [first, up_rows, norms, *ups, *downs]
    return call(
        functools.partial(
            mlp_kernel, up_plan, down_plan, weights.get("proj"), len(ups), top, split
        ),
        f"mlp_{layer_at}",
        9,
        place,
        args,
        outs,
        scratch,
        in_hbm=range(3, len(args)),
    )


def run_mlp_pull(layer_at, place, upstream, saved, norms, weights, split):
    top = layer_at == LAYERS - 1
    ups, up_plan = weights["up"]
    downs, down_plan = weights["down"]
    outs = [
        shaped((ROWS, WIDTH), F32),
        shaped((8, WIDTH), F32),
        shaped((WIDTH, ROWS), BF),
    ] + sided(split, (ROWS, SLAB), BF)
    scratch = held_scratch(weights["fold"], 2)
    if top:
        outs += [shaped((WIDTH, DIM), F32)]
        scratch += projection_scratch(weights["fold"])
    inputs = [*upstream, *saved, norms]
    args = [*inputs, *ups, *downs]
    return call(
        functools.partial(
            mlp_pull_kernel, up_plan, down_plan, weights.get("proj"), len(ups), top, split
        ),
        f"pull_mlp_{layer_at}",
        8,
        place,
        args,
        outs,
        scratch,
        in_hbm=range(len(inputs), len(args)),
    )


def run_attention_pull(layer_at, place, grad_first, saved, norms, weights, split):
    arrays, plan = weights["att"]
    outs = [
        shaped((ROWS, WIDTH), F32),
        shaped((8, WIDTH), F32),
        shaped((WIDTH, ROWS), BF),
    ] + sided(split, (ROWS, SLAB), BF)
    inputs = [grad_first, *saved, norms]
    args = [*inputs, *arrays]
    return call(
        functools.partial(attention_pull_kernel, plan, len(arrays), split),
        f"pull_attention_{layer_at}",
        10,
        place,
        args,
        outs,
        held_scratch(weights["fold"], 1),
        in_hbm=range(len(inputs), len(args)),
    )


def grad_shapes(split, rows_each, width):
    if split:
        return [shaped((2, 4, rows_each, width), BF)] * 2
    return [shaped((PARTS, WIDTH, width), BF)]


def run_mlp_grad(layer_at, place, groups, split, rows_each):
    top = layer_at == LAYERS - 1
    args = [value for group in groups for value in group]
    sides = 2 if split else 1
    outs = grad_shapes(split, rows_each, SLAB)
    outs += grad_shapes(split, rows_each, SLAB + (DIM if top else 0))
    fold = (4, 2, rows_each) if split else (1, 1, WIDTH)
    slots = PARTS // sides
    scratch = [
        pltpu.VMEM((2, slots, *fold, SLAB), BF),
        pltpu.SemaphoreType.DMA((2, slots, 2, 4)),
    ]
    if top:
        scratch += [pltpu.VMEM((*fold, DIM), BF), pltpu.SemaphoreType.DMA((slots, 2, 4))]
    results = call(
        functools.partial(mlp_grad_kernel, top, split),
        f"grad_mlp_{layer_at}",
        8,
        place,
        args,
        outs,
        scratch,
        out_hbm=range(len(outs)),
    )
    return results[:sides], results[sides:]


def run_attention_grad(layer_at, cuts, place, groups, split, rows_each):
    args = [value for group in groups for value in group]
    sides = 2 if split else 1
    outs = []
    for _, width, _ in cuts:
        outs += grad_shapes(split, rows_each, width)
    fold = (4, 2, rows_each) if split else (1, 1, WIDTH)
    slots = PARTS // sides
    results = call(
        functools.partial(attention_grad_kernel, cuts, split),
        f"grad_attention_{layer_at}",
        5,
        place,
        args,
        outs,
        [
            pltpu.VMEM((slots, *fold, SLAB), BF),
            pltpu.SemaphoreType.DMA((len(cuts), slots, 2, 4)),
        ],
        out_hbm=range(len(outs)),
    )
    return [results[sides * at : sides * (at + 1)] for at in range(len(cuts))]


CORE_SWAP = [(at, at ^ 1) for at in range(PARTS)]
X_SWAP = [(at, at ^ 2) for at in range(PARTS)]
Y_SWAP = [(at, at ^ 1) for at in range(8)]
Z_GROUPS = [[0, 2, 4, 6], [1, 3, 5, 7]]


def added(*terms):
    total = terms[0].astype(F32)
    for term in terms[1:]:
        total = total + term.astype(F32)
    return total


def over_x(value, name):
    with jax.named_scope(f"x_{name}"):
        return lax.ppermute(value, "tensor", X_SWAP)


def over_y(value, name):
    with jax.named_scope(f"y_{name}"):
        return lax.ppermute(value, "dp", Y_SWAP)


def over_core(value, name="pair"):
    with jax.named_scope(f"core_{name}"):
        return lax.ppermute(value, "tensor", CORE_SWAP)


def along_z(value, step, name):
    pairs = [(at, ((at // 2 + step) % 4) * 2 + at % 2) for at in range(8)]
    with jax.named_scope(f"z_{name}_{step}"):
        return lax.ppermute(value, "dp", pairs)


def tied(*values):
    return lax.optimization_barrier(values)


class Reduction:
    def __init__(self, name, pieces, y_first):
        self.name = name
        self.keep, self.send = pieces
        self.first, self.second = (over_y, over_x) if y_first else (over_x, over_y)

    def start(self):
        self.one = self.first(self.send, self.name + "_first")

    def add_second(self):
        with jax.named_scope(f"add_{self.name}_second"):
            self.terms = added(self.keep[1], self.one[1]).astype(BF)

    def start_second(self):
        self.two = self.second(self.terms, self.name + "_second")

    def block(self, step):
        return added(self.keep[0, step], self.one[0, step], self.two[step])


class Column:
    def __init__(self, *items):
        self.items = items
        self.name = "_".join(item.name for item in items)

    def add_third(self):
        with jax.named_scope(f"add_{self.name}_third"):
            self.blocks = [
                jnp.concatenate([item.block(step).astype(BF) for item in self.items], 1)
                for step in range(1, 4)
            ]

    def start_third(self):
        self.arrived = [
            along_z(block, step + 1, self.name) for step, block in enumerate(self.blocks)
        ]

    def totals(self):
        with jax.named_scope(f"add_{self.name}_last"):
            results, at = [], 0
            for item in self.items:
                own = item.block(0)
                end = at + own.shape[1]
                results.append(own + added(*[value[:, at:end] for value in self.arrived]))
                at = end
        return results


def reduce_whole(grads, devices):
    grads = grads.reshape(PARTS, devices, WIDTH // devices, -1)
    grads = jnp.transpose(grads, (1, 0, 2, 3)).reshape(devices * PARTS, WIDTH // devices, -1)
    return lax.psum_scatter(grads, BOTH, scatter_dimension=0, tiled=True)[0].astype(F32)


def total_over_plane(value):
    with jax.named_scope("cross_sums"):
        far = lax.ppermute(value, "tensor", [(at, at ^ 3) for at in range(PARTS)])
    value = (value + over_core(value, "sums")) + (over_x(value, "sums") + far)
    return value + over_y(value, "sums")


def total_over_column(value):
    column = jnp.stack([value, *[along_z(value, step, "sums") for step in range(1, 4)]])
    z_at = lax.axis_index("dp") // 2
    ordered = [
        lax.dynamic_index_in_dim(column, (z_at - at) & 3, 0, keepdims=False) for at in range(4)
    ]
    return (ordered[0] + ordered[1]) + (ordered[2] + ordered[3])


def score_kernel(count, lengths_ref, log_ref, queries_ref, passages_ref, powers_ref, sums_ref, logit_ref):
    queries = queries_ref[...]

    def single(at, carry):
        similar = nt(passages_ref[at], queries)
        spot = lax.broadcasted_iota(jnp.int32, (PLEN, ROWS), 0)
        powers = jnp.where(spot < lengths_ref[at], jnp.exp(SHARPNESS * similar), 0.0)
        powers_ref[at] = powers.astype(BF)
        sums_ref[pl.ds(at, 1), :] = jnp.sum(powers, 0, keepdims=True)
        return carry

    lax.fori_loop(0, count, single, 0)
    smooth = (jnp.log(sums_ref[...]) - log_ref[...]) / SHARPNESS
    token = lax.broadcasted_iota(jnp.int32, (ROWS, DIM), 0) // QLEN
    query = lax.broadcasted_iota(jnp.int32, (ROWS, DIM), 1)
    pick = (token == query).astype(F32)
    logit_ref[...] = SCORE_SCALE * jnp.dot(
        smooth, pick, precision=lax.Precision.HIGHEST, preferred_element_type=F32
    )


def pull_kernel(count, powers_ref, steer_ref, queries_ref, passages_ref, passage_out, query_out, total):
    queries = queries_ref[...]
    total[...] = jnp.zeros_like(total)

    def single(at, carry):
        shares = (powers_ref[at].astype(F32) * steer_ref[pl.ds(at, 1), :]).astype(BF)
        passage_out[at] = nn(shares, queries).astype(BF)
        total[...] += nn(passages_ref[at].T, shares)
        return carry

    lax.fori_loop(0, count, single, 0)
    query_out[...] = total[...].T


def scores_of(queries, passages, lengths):
    count = passages.shape[0]
    return pl.pallas_call(
        functools.partial(score_kernel, count),
        out_shape=[
            shaped((count, PLEN, ROWS), BF),
            shaped((count, ROWS), F32),
            shaped((count, DIM), F32),
        ],
        in_specs=[pl.BlockSpec(memory_space=pltpu.SMEM)] + [vmem_spec()] * 3,
        out_specs=[vmem_spec()] * 3,
        compiler_params=params(),
        cost_estimate=price(4),
        name="scores",
    )(lengths, jnp.log(lengths.astype(F32))[:, None], queries, passages)


def pulls_of(powers, steer, queries, passages):
    count = passages.shape[0]
    return pl.pallas_call(
        functools.partial(pull_kernel, count),
        out_shape=[shaped((count, PLEN, DIM), BF), shaped((ROWS, DIM), F32)],
        in_specs=[vmem_spec()] * 4,
        out_specs=[vmem_spec()] * 2,
        scratch_shapes=[pltpu.VMEM((DIM, ROWS), F32)],
        compiler_params=params(),
        cost_estimate=price(4),
        name="score_pulls",
    )(powers, steer, queries, passages)


def adam_step(master, moment, second, gradient, decay):
    moment_new = BETA_ONE * moment + (1.0 - BETA_ONE) * gradient
    second_new = BETA_TWO * second + (1.0 - BETA_TWO) * gradient * gradient
    rising = moment_new / (1.0 - BETA_ONE**STEP)
    spread = jnp.sqrt(second_new / (1.0 - BETA_TWO**STEP))
    return (moment_new, second_new, -LEARN_RATE * (rising / (spread + ADAM_EPS) + decay * master))


def joined(*pieces):
    return jnp.concatenate([piece.astype(BF) for piece in pieces], 1)


def attention_shard(qkv, out):
    return joined(qkv[0], qkv[1], qkv[2], out.T)


class Gathering:
    def __init__(self, name, shard, x_last):
        self.name = name
        self.shard = shard
        self.plan = ("x_last" if x_last else "y_last", 0)
        self.first, self.second = (over_y, over_x) if x_last else (over_x, over_y)

    def column(self):
        arrived = [along_z(self.shard, step, self.name) for step in range(1, 4)]
        self.held = jnp.stack([self.shard, *arrived])

    def plane(self):
        self.held = jnp.stack([self.held, self.first(self.held, self.name + "_first")])

    def cross(self):
        self.other = self.second(self.held, self.name + "_second")

    def all(self):
        pairs = [over_core(self.held, self.name), over_core(self.other, self.name)]
        return [self.held, self.other, *pairs], self.plan


def gather_whole(shard, devices):
    rows_each = shard.shape[0]
    value = lax.all_gather(shard, BOTH, axis=0, tiled=False)
    if devices == 8:
        return value.reshape(4, 2, PARTS, rows_each, -1)
    value = value.reshape(devices, PARTS, rows_each, -1)
    return jnp.transpose(value, (1, 0, 2, 3)).reshape(1, 1, PARTS, WIDTH, -1)


def whole_weights(value):
    return {
        "att": ([value], ("whole", 0)),
        "up": ([value], ("whole", SLAB)),
        "down": ([value], ("whole", 2 * SLAB)),
        "proj": PACK,
    }


def unpack_grads(att_list, up_list, down_list):
    qkv = jnp.stack(
        [
            jnp.stack([att[:, kind * OWN : (kind + 1) * OWN] for kind in range(3)])
            for att in att_list
        ]
    )
    out = jnp.stack([att[:, 3 * OWN :].T for att in att_list])
    return qkv, out, jnp.stack(up_list), jnp.stack([down[:, :SLAB].T for down in down_list])


def to_output_rows(grad, tensor_at):
    rows = PDEV * PLEN // PARTS
    query_rows = QDEV * QLEN // PARTS
    start = jnp.where(tensor_at == PARTS - 1, 0, ROWS - rows)
    step = lax.ppermute(
        lax.dynamic_slice_in_dim(grad, start, rows, 0).astype(BF),
        "tensor",
        [(at, (at + 1) % PARTS) for at in range(PARTS)],
    ).astype(F32)
    last = PARTS - 1
    sent = grad.astype(BF)
    one = lax.ppermute(sent[query_rows : 2 * query_rows], "tensor", [(last, 1)]).astype(F32)
    two = lax.ppermute(sent[2 * query_rows : 3 * query_rows], "tensor", [(last, 2)]).astype(F32)
    own = grad[last * query_rows :]
    query = jnp.where(
        tensor_at == 0,
        step[:query_rows],
        jnp.where(tensor_at == 1, one, jnp.where(tensor_at == 2, two, own)),
    )
    unit = query_rows
    passage = jnp.where(
        tensor_at == 0,
        grad[:rows],
        jnp.where(
            tensor_at == 1,
            jnp.concatenate([step[2 * unit :], grad[: 2 * unit]]),
            jnp.where(tensor_at == 2, jnp.concatenate([step[unit:], grad[:unit]]), step),
        ),
    )
    return query, passage


def body(
    query_tokens,
    passage_tokens,
    query_mask,
    passage_lengths,
    positives,
    qkv_weight,
    qkv_moment,
    qkv_second,
    out_weight,
    out_moment,
    out_second,
    up_weight,
    up_moment,
    up_second,
    down_weight,
    down_moment,
    down_second,
    projection,
    projection_moment,
    projection_second,
    bias_pair,
    bias_pair_moment,
    bias_pair_second,
    bias_up,
    bias_up_moment,
    bias_up_second,
    norm_terms,
    norm_terms_moment,
    norm_terms_second,
):
    devices = lax.axis_size("dp")
    dev_index = lax.axis_index("dp")
    tensor_at = lax.axis_index("tensor")
    last = PARTS - 1
    is_query = tensor_at == last
    rows_each = WIDTH // devices
    split = devices == 8
    pair_own = jnp.concatenate(
        [
            bias_pair[:, 0],
            jnp.zeros((LAYERS, OWN), F32),
            bias_pair[:, 1],
            jnp.zeros((LAYERS, HELD - 3 * OWN), F32),
        ],
        -1,
    )
    small = jnp.concatenate([pair_own, bias_up], -1)
    if split:
        crossed = over_x(small, "biases")
        small_all = [small, crossed, over_core(small, "biases"), over_core(crossed, "biases")]
        small_all = jnp.stack(small_all)
    else:
        small_all = lax.all_gather(small, "tensor", axis=0, tiled=False)

    shards = [
        (
            attention_shard(qkv_weight[at], out_weight[at]),
            up_weight[at].astype(BF),
            down_weight[at].T.astype(BF),
        )
        for at in range(LAYERS)
    ]
    if split:
        last_layer = whole_weights(gather_whole(joined(*shards[1], projection), devices))
        att = Gathering("att_0", shards[0][0], False)
        up = Gathering("up_0", shards[0][1], True)
        down = Gathering("down_0", shards[0][2], False)
        att.column()
        att.held, up.shard, down.shard, small_all = tied(
            att.held, up.shard, down.shard, small_all
        )
        att.plane()
        up.column()
        down.column()
        up.plane()
        down.plane()
        att.cross()
        up.cross()
        down.cross()
        first_layer = {"att": att.all()}
    else:
        first_layer = whole_weights(gather_whole(joined(*shards[0]), devices))
        last_layer = whole_weights(gather_whole(joined(*shards[1], projection), devices))
    weights = [first_layer, last_layer]
    for layer in weights:
        layer["fold"] = (4, 2, rows_each) if split else (1, 1, WIDTH)
    pair_rows = small_all[:, :, None, :HELD]
    up_all = small_all[:, :, None, HELD:]
    passage_at = jnp.minimum(tensor_at, last - 1)
    own_passage = lax.dynamic_slice_in_dim(passage_tokens, passage_at * PLEN, PLEN, 0)
    hidden = jnp.where(is_query, query_tokens, own_passage)
    own_length = lax.dynamic_slice_in_dim(passage_lengths, dev_index * PDEV + passage_at, 1, 0)
    spot = jnp.arange(ROWS, dtype=jnp.int32)
    key_valid = jnp.where(is_query, query_mask.reshape(ROWS) == 1, spot < own_length)
    together = jnp.logical_or(
        jnp.logical_not(is_query), spot[:, None] // QLEN == spot[None, :] // QLEN
    )
    mask = jnp.where(jnp.logical_and(key_valid[:, None], together), 0.0, MASKED).astype(F32)

    place = jnp.stack([tensor_at // 2, tensor_at % 2, dev_index % 2, dev_index // 2]).astype(jnp.int32)

    def sides_of(keep, send):
        return [keep, over_core(send)] if split else [keep]

    def shared(value):
        return [value, over_core(value)] if split else [value]

    saved_list = []
    for layer_at in range(LAYERS):
        outs = run_attention(
            layer_at,
            place,
            hidden,
            mask,
            pair_rows[:, layer_at],
            norm_terms[layer_at],
            weights[layer_at],
            split,
        )
        first, x_t, packed, chances, normal_one, factor_one, first_t = outs[:7]
        if split and layer_at == 0:
            first, up.held, up.other, down.held, down.other = tied(
                first, up.held, up.other, down.held, down.other
            )
            weights[0].update(up=up.all(), down=down.all())
        mixtures = sides_of(outs[7], outs[-1])
        outs = run_mlp(
            layer_at,
            place,
            first,
            up_all[:, layer_at],
            norm_terms[layer_at],
            weights[layer_at],
            split,
            devices,
        )
        hidden, slope, normal_two, factor_two = outs[:4]
        acts = sides_of(outs[4], outs[5 if split else 4])
        saved_list.append(
            dict(
                mlp=(slope, normal_two, factor_two),
                attention=(packed, chances, normal_one, factor_one),
                x_t=shared(x_t),
                first_t=shared(first_t),
                mixtures=mixtures,
                acts=acts,
            )
        )
    embedding, unit, scale, top_t = outs[-4:]

    passages = lax.all_to_all(embedding, "dp", 0, 0, tiled=True)
    embedding = embedding[0]
    queries = embedding
    arrived = [lax.ppermute(embedding, "tensor", [(last, at)]) for at in range(last)]
    for at in range(last):
        queries = jnp.where(tensor_at == at, arrived[at], queries)
    length_table = passage_lengths.reshape(devices, PDEV)
    own_lengths = lax.dynamic_slice_in_dim(length_table, passage_at, 1, 1)[:, 0]
    powers, sums, logit_part = scores_of(queries, passages, own_lengths)
    logits = lax.all_gather(logit_part[:, :QDEV], "tensor", axis=0, tiled=False)[:last]
    own_positives = lax.dynamic_slice_in_dim(positives, dev_index * QDEV, QDEV, 0)
    ids = (
        lax.broadcasted_iota(jnp.int32, logits.shape, 1) * PDEV
        + lax.broadcasted_iota(jnp.int32, logits.shape, 0)
    )
    chosen = ids == own_positives[None, None, :]
    highest = jnp.max(logits, (0, 1), keepdims=True)
    raised = jnp.exp(logits - highest)
    summed = jnp.sum(raised, (0, 1), keepdims=True)
    losses = highest + jnp.log(summed) - jnp.sum(jnp.where(chosen, logits, 0.0), (0, 1), keepdims=True)
    deltas = raised / summed - chosen.astype(F32)
    own_deltas = lax.dynamic_slice_in_dim(deltas, passage_at, 1, 0)[0]
    steer = jnp.where(is_query, 0.0, SCORE_SCALE) * jnp.repeat(own_deltas, QLEN, axis=1) / sums
    passage_terms, query_terms = pulls_of(powers, steer, queries, passages)
    passage_back = lax.all_to_all(passage_terms, "dp", 0, 0, tiled=True)
    grad_passage = jnp.sum(passage_back.astype(F32), 0)
    returned = [lax.ppermute(query_terms, "tensor", [(at, last)]) for at in range(last)]
    grad_query = returned[0] + returned[1] + returned[2]
    grad_emb = jnp.where(is_query, grad_query, grad_passage)

    upstream = (grad_emb, unit, scale, top_t)
    mlp_sums, attention_sums = [None] * LAYERS, [None] * LAYERS

    def stacked_sums():
        loss_part = jnp.where(tensor_at == 0, jnp.sum(losses), 0.0)
        sums = jnp.stack([attention_sums[0], mlp_sums[0], attention_sums[1], mlp_sums[1]])
        row_ids = lax.broadcasted_iota(jnp.int32, sums.shape, 1)
        sums = sums + jnp.where(row_ids == 7, loss_part, 0.0)
        return sums

    def mlp_pull(layer_at, upstream):
        saved = saved_list[layer_at]
        outs = run_mlp_pull(
            layer_at, place, upstream, saved["mlp"], norm_terms[layer_at], weights[layer_at], split
        )
        grad_first, mlp_sums[layer_at], low_t = outs[:3]
        groups = [
            saved["first_t"],
            sides_of(outs[3], outs[4 if split else 3]),
            shared(low_t),
            saved["acts"],
        ]
        if layer_at == LAYERS - 1:
            groups.append(shared(outs[-1]))
        return grad_first, groups

    def attention_pull(layer_at, grad_first):
        saved = saved_list[layer_at]
        outs = run_attention_pull(
            layer_at,
            place,
            grad_first,
            saved["attention"],
            norm_terms[layer_at],
            weights[layer_at],
            split,
        )
        dx, attention_sums[layer_at], low_t = outs[:3]
        return dx, [
            saved["x_t"],
            sides_of(outs[3], outs[-1]),
            shared(low_t),
            saved["mixtures"],
        ]

    def mlp_grad(layer_at, groups):
        return run_mlp_grad(layer_at, place, groups, split, rows_each)

    def attention_grad(layer_at, cuts, groups):
        return run_attention_grad(layer_at, cuts, place, groups, split, rows_each)

    if split:
        grad_first, mlp_groups = mlp_pull(1, upstream)
        up_grads, down_grads = mlp_grad(1, mlp_groups)
        up_one, down_one = Reduction("up_1", up_grads, False), Reduction("down_1", down_grads, True)
        grad_first, up_one.send, down_one.send = tied(grad_first, up_one.send, down_one.send)
        up_one.start()
        down_one.start()
        dx, att_groups = attention_pull(1, grad_first)
        att_one = Reduction("att_1", attention_grad(1, ((0, SLAB, False),), att_groups)[0], False)
        dx, att_one.send = tied(dx, att_one.send)
        att_one.start()
        grad_first, mlp_groups = mlp_pull(0, (dx,))
        up_one.add_second()
        down_one.add_second()
        mlp_groups[0][0], up_one.terms, down_one.terms = tied(
            mlp_groups[0][0], up_one.terms, down_one.terms
        )
        up_one.start_second()
        down_one.start_second()
        up_grads, down_grads = mlp_grad(0, mlp_groups)
        up_zero = Reduction("up_0", up_grads, False)
        down_zero = Reduction("down_0", down_grads, True)
        grad_first, up_zero.send, down_zero.send = tied(grad_first, up_zero.send, down_zero.send)
        up_zero.start()
        down_zero.start()
        dx, att_groups = attention_pull(0, grad_first)
        dx, att_one.one = tied(dx, att_one.one)
        att_one.add_second()
        att_one.start_second()
        mlp_one = Column(up_one, down_one)
        mlp_one.add_third()
        up_zero.add_second()
        down_zero.add_second()
        half = SLAB // 2
        left, right = attention_grad(0, ((0, half, False), (half, half, True)), att_groups)
        halves = (Reduction("qk_0", left, False), Reduction("vo_0", right, True))
        column_one = Column(att_one)
        mlp_one.start_third()
        column_one.add_third()
        column_one.start_third()
        for item in (up_zero, down_zero):
            item.start_second()
        qk_zero, vo_zero = halves
        up_zero.two, down_zero.two, qk_zero.send, vo_zero.send = tied(
            up_zero.two, down_zero.two, qk_zero.send, vo_zero.send
        )
        for item in halves:
            item.start()
        mlp_zero = Column(up_zero, down_zero)
        mlp_zero.add_third()
        mlp_zero.start_third()
        for item in halves:
            item.add_second()
        attention_sums[0], dx, qk_zero.terms, vo_zero.terms = tied(
            attention_sums[0], dx, qk_zero.terms, vo_zero.terms
        )
        for item in halves:
            item.start_second()
        sums = total_over_plane(stacked_sums())
        sums, qk_zero.two, vo_zero.two = tied(sums, qk_zero.two, vo_zero.two)
        column_zero = Column(qk_zero, vo_zero)
        column_zero.add_third()
        column_zero.start_third()
        sums = total_over_column(sums)
        att_list = [jnp.concatenate(column_zero.totals(), 1), *column_one.totals()]
        (up_grad_zero, down_grad_zero), (up_grad_one, down_grad_one) = (
            mlp_zero.totals(),
            mlp_one.totals(),
        )
        up_list, down_list = [up_grad_zero, up_grad_one], [down_grad_zero, down_grad_one]
    else:
        att_list, up_list, down_list = [], [], []
        dx = None
        for layer_at in range(LAYERS - 1, -1, -1):
            grad_first, groups = mlp_pull(layer_at, (dx,) if upstream is None else upstream)
            upstream = None
            up_grads, down_grads = mlp_grad(layer_at, groups)
            dx, groups = attention_pull(layer_at, grad_first)
            att_grads = attention_grad(layer_at, ((0, SLAB, False),), groups)[0]
            up_list.insert(0, reduce_whole(up_grads[0], devices))
            down_list.insert(0, reduce_whole(down_grads[0], devices))
            att_list.insert(0, reduce_whole(att_grads[0], devices))
        sums = lax.psum(stacked_sums(), BOTH)
    sums = sums.reshape(LAYERS, 2, 8, WIDTH)
    norms_grad = sums[:, :, :3].reshape(LAYERS, 6, WIDTH)
    own_sums = lax.dynamic_slice_in_dim(sums, 3 + tensor_at, 1, 2)[:, :, 0]
    pair_grad = jnp.stack([own_sums[:, 0, :OWN], own_sums[:, 0, 2 * OWN : 3 * OWN]], 1)
    bias_grad = own_sums[:, 1]
    loss_mean = sums[0, 0, 7, 0] / (QDEV * devices)
    projection_grad = down_list[LAYERS - 1][:, SLAB:]
    qkv_grad, out_grad, up_grad, down_grad = unpack_grads(att_list, up_list, down_list)
    qkv_m, qkv_v, qkv_u = adam_step(qkv_weight, qkv_moment, qkv_second, qkv_grad, WEIGHT_DECAY)
    out_m, out_v, out_u = adam_step(out_weight, out_moment, out_second, out_grad, WEIGHT_DECAY)
    up_m, up_v, up_u = adam_step(up_weight, up_moment, up_second, up_grad, WEIGHT_DECAY)
    down_m, down_v, down_u = adam_step(
        down_weight, down_moment, down_second, down_grad, WEIGHT_DECAY
    )
    proj_m, proj_v, proj_u = adam_step(
        projection, projection_moment, projection_second, projection_grad, WEIGHT_DECAY
    )
    pair_m, pair_v, pair_u = adam_step(
        bias_pair, bias_pair_moment, bias_pair_second, pair_grad, 0.0
    )
    bias_m, bias_v, bias_u = adam_step(bias_up, bias_up_moment, bias_up_second, bias_grad, 0.0)
    norm_m, norm_v, norm_u = adam_step(
        norm_terms, norm_terms_moment, norm_terms_second, norms_grad, 0.0
    )
    query_grad, passage_grad = to_output_rows(dx, tensor_at)
    return (
        loss_mean,
        query_grad,
        passage_grad,
        qkv_grad,
        qkv_m,
        qkv_v,
        qkv_u,
        out_grad,
        out_m,
        out_v,
        out_u,
        up_grad,
        up_m,
        up_v,
        up_u,
        down_grad,
        down_m,
        down_v,
        down_u,
        projection_grad,
        proj_m,
        proj_v,
        proj_u,
        pair_grad,
        pair_m,
        pair_v,
        pair_u,
        bias_grad,
        bias_m,
        bias_v,
        bias_u,
        norms_grad,
        norm_m,
        norm_v,
        norm_u,
    )


def solution(mesh):
    placed = (
        P("dp", None),
        P("dp", None),
        P("dp", None),
        P(),
        P(),
        P(None, None, "dp", "tensor"),
        P(None, None, "dp", "tensor"),
        P(None, None, "dp", "tensor"),
        P(None, "tensor", "dp"),
        P(None, "tensor", "dp"),
        P(None, "tensor", "dp"),
        P(None, "dp", "tensor"),
        P(None, "dp", "tensor"),
        P(None, "dp", "tensor"),
        P(None, "tensor", "dp"),
        P(None, "tensor", "dp"),
        P(None, "tensor", "dp"),
        P("dp", None),
        P("dp", None),
        P("dp", None),
        P(None, None, "tensor"),
        P(None, None, "tensor"),
        P(None, None, "tensor"),
        P(None, "tensor"),
        P(None, "tensor"),
        P(None, "tensor"),
        P(),
        P(),
        P(),
    )
    return jax.shard_map(
        body,
        mesh=mesh,
        in_specs=placed,
        out_specs=(
            P(),
            P(("dp", "tensor"), None),
            P(("dp", "tensor"), None),
            P(None, None, "dp", "tensor"),
            P(None, None, "dp", "tensor"),
            P(None, None, "dp", "tensor"),
            P(None, None, "dp", "tensor"),
            P(None, "tensor", "dp"),
            P(None, "tensor", "dp"),
            P(None, "tensor", "dp"),
            P(None, "tensor", "dp"),
            P(None, "dp", "tensor"),
            P(None, "dp", "tensor"),
            P(None, "dp", "tensor"),
            P(None, "dp", "tensor"),
            P(None, "tensor", "dp"),
            P(None, "tensor", "dp"),
            P(None, "tensor", "dp"),
            P(None, "tensor", "dp"),
            P("dp", None),
            P("dp", None),
            P("dp", None),
            P("dp", None),
            P(None, None, "tensor"),
            P(None, None, "tensor"),
            P(None, None, "tensor"),
            P(None, None, "tensor"),
            P(None, "tensor"),
            P(None, "tensor"),
            P(None, "tensor"),
            P(None, "tensor"),
            P(),
            P(),
            P(),
            P(),
        ),
        check_vma=False,
    )
```
